128 devices in a mesh: walk: 16 (over y_hi, z, core), band: 8 (over y_lo, x).
Axes of the slice: x: 4, y: 4 (y_hi: 2, y_lo: 2; y = y_hi * 2 + y_lo), z: 4, core: 2. Of those that a mesh axis runs over, the one named last changes fastest.
Arguments:
- positions: float32 [2, 49152], P(None, 'walk'), may hold values from 0 to 1
- coefficients: bfloat16 [2, 18432, 1024], P(None, 'walk', 'band')
- lattice: int32 [2, 18432], replicated, may hold values from -76 to 76
- spin_labels: int32 [49152], P('walk'), may hold values from 0 to 1
- occupied: int32 [2, 48], replicated, may hold values from 0 to 1023
- features: bfloat16 [49152, 256], P('walk'), may hold values from -6 to 6
- orbital_head: bfloat16 [256, 192], replicated, may hold values from -0.029907227 to 0.029907227
Outputs:
- gradient: float32 [256, 192], replicated
The draws below stay inside these ranges and needn't reach their ends.
All inputs are finite; a program needn't handle non-finite values.
Results may differ from the reference program's by a relative error of at most 0.0003.
Values may be sent and summed in bfloat16 or wider, within the bound.
No kernel may reach another device: no remote copies, remote signals or barrier semaphores. Data moves between devices by JAX's collectives and lax.ppermute only.
A program may use at most 128 MiB of HBM per device.

```python
import jax
import jax.numpy as jnp
from jax import lax

NG = 18432
NB = 1024
NORB = 48
DH = 256
WALKERS = 512
POSITIONS = 49152


def lattice_rows(key):
    drawn = jax.random.randint(jax.random.fold_in(key, 7), (2, NG), -76, 77, dtype=jnp.int32)
    corner = jnp.array([76, -76], dtype=jnp.int32)
    return drawn.at[:, 0].set(corner)


def draw_lattice(key, part):
    return lattice_rows(key)


def draw_coefficients(key, part):
    indices = lattice_rows(key)
    reach_share = (jnp.abs(indices[0]) + jnp.abs(indices[1])).astype(jnp.float32) / 152.0
    weight_row = 1.0 + 9.0 * reach_share * reach_share
    noise_key = jax.random.fold_in(key, 13)
    base_draw = jnp.clip(jax.random.normal(noise_key, (2, NG, NB), jnp.float32), -6.0, 6.0)
    values = base_draw * weight_row[None, :, None] / jnp.sqrt(16.7 * NG)
    return values.astype(jnp.bfloat16)


def plant(values, rng, least, high):
    extent = values.shape
    index_at = [jax.random.randint(jax.random.fold_in(rng, axis), (), 0, extent[axis]) for axis in range(len(extent))]
    values = values.at[tuple(index_at)].set(least)
    longest = extent.index(max(extent))
    index_at[longest] = (index_at[longest] + 1) % extent[longest]
    return values.at[tuple(index_at)].set(high)


def block_levels(rng, shape, split, smallest, top_value):
    gain = 1.0
    for position, parts in split:
        steps = jax.random.uniform(jax.random.fold_in(jax.random.fold_in(rng, 6), position), (parts,), jnp.float32, smallest / len(split), top_value / len(split))
        gain = gain * jnp.repeat(jnp.exp(steps), shape[position] // parts).reshape((-1,) + (1,) * (len(shape) - 1 - position))
    return gain


def gaussian(rng, extent, deviation, most, split=(), kind=jnp.bfloat16):
    entries = deviation * jax.random.normal(rng, extent, jnp.float32)
    if split:
        entries = entries * block_levels(rng, extent, split, -0.22, 0.18)
    return jnp.clip(entries, -most, most).astype(kind)


def setup_inputs(seed: int = 0) -> dict:
    keys = jax.random.split(jax.random.key(seed), 8)
    return {
        "positions": jnp.clip(1.0 * jax.random.uniform(keys[0], (2, POSITIONS), jnp.float32) ** block_levels(keys[0], (2, POSITIONS), ((1, 16),), -0.2, 0.2), 0.0, 1.0),
        "coefficients": draw_coefficients(jax.random.fold_in(keys[7], 71), 0),
        "lattice": draw_lattice(jax.random.fold_in(keys[7], 71), 0),
        "spin_labels": plant(jax.random.randint(keys[3], (POSITIONS,), 0, 2), jax.random.fold_in(keys[3], 1), 0, 1).astype(jnp.int32),
        "occupied": plant(jax.random.randint(keys[4], (2, NORB), 0, NB), jax.random.fold_in(keys[4], 1), 0, NB - 1).astype(jnp.int32),
        "features": gaussian(keys[5], (POSITIONS, DH), 1.0, 6.0, ((0, 16),)),
        "orbital_head": gaussian(keys[6], (DH, 4 * NORB), 0.005, 0.029907227),
    }


TWO_PI = 6.283185307179586


def orbital_block(pos_x, pos_y, lat_x, lat_y, right_cos, right_sin):
    phase_angle = TWO_PI * (pos_x[:, None] * lat_x[None, :] + pos_y[:, None] * lat_y[None, :])
    cosine = jnp.cos(phase_angle)
    sine_part = jnp.sin(phase_angle)
    first = jnp.dot(cosine, right_cos, precision=lax.Precision.HIGHEST, preferred_element_type=jnp.float32)
    second = jnp.dot(sine_part, right_sin, precision=lax.Precision.HIGHEST, preferred_element_type=jnp.float32)
    return first + second


def fit_gradient(orbitals, spin_labels, features, orbital_head, walkers):
    orbital_count = orbitals.shape[1] // 4
    spin_up = (spin_labels == 0)[:, None]
    real_pick = jnp.where(spin_up, orbitals[:, :orbital_count], orbitals[:, orbital_count:2 * orbital_count])
    imag_pick = jnp.where(spin_up, orbitals[:, 2 * orbital_count:3 * orbital_count], orbitals[:, 3 * orbital_count:])
    target = jnp.concatenate([real_pick, imag_pick], axis=1)
    net_all = jnp.dot(features, orbital_head, preferred_element_type=jnp.float32)
    net_value = jnp.where(spin_up, net_all[:, :2 * orbital_count], net_all[:, 2 * orbital_count:])
    scaled = (net_value - target) / walkers
    blank_rows = jnp.zeros_like(scaled)
    spread_rows = jnp.concatenate([jnp.where(spin_up, scaled, blank_rows), jnp.where(spin_up, blank_rows, scaled)], axis=1)
    return lax.dot_general(features.astype(jnp.float32), spread_rows, (((0,), (0,)), ((), ())), precision=lax.Precision.HIGHEST, preferred_element_type=jnp.float32)


def right_tables(picked):
    right_cos = jnp.concatenate([picked[0], picked[1]], axis=1).astype(jnp.float32)
    right_sin = jnp.concatenate([-picked[1], picked[0]], axis=1).astype(jnp.float32)
    return right_cos, right_sin


def reference(positions, coefficients, lattice, spin_labels, occupied, features, orbital_head):
    occ_flat = occupied.reshape(-1).astype(jnp.int32)
    picked = jnp.take(coefficients, occ_flat, axis=2)
    right_cos, right_sin = right_tables(picked)
    lat_x = lattice[0].astype(jnp.float32)
    lat_y = lattice[1].astype(jnp.float32)
    block_rows = min(384, POSITIONS)
    block_count = POSITIONS // block_rows
    pos_x = positions[0].reshape(block_count, block_rows)
    pos_y = positions[1].reshape(block_count, block_rows)
    orbitals = lax.map(lambda coords: orbital_block(coords[0], coords[1], lat_x, lat_y, right_cos, right_sin), (pos_x, pos_y))
    orbitals = orbitals.reshape(POSITIONS, right_cos.shape[1])
    return fit_gradient(orbitals, spin_labels, features, orbital_head, float(WALKERS))
```

```python
import functools

import jax
import jax.numpy as jnp
from jax import lax
from jax.experimental import pallas as pl
from jax.experimental.pallas import tpu as pltpu
from jax.sharding import PartitionSpec as P

INTERPRET = False
F32 = jnp.float32
BF16 = jnp.bfloat16
PI = 3.141592653589793
HALF = 80
LANES = 128


def split3(value):
    high = value.astype(BF16)
    rest = value - high.astype(F32)
    middle = rest.astype(BF16)
    low = (rest - middle.astype(F32)).astype(BF16)
    return high, middle, low


def send_kernel(coef_ref, pick_ref, pos_ref, out_ref):
    rows = coef_ref.shape[1]
    pick = pick_ref[...].astype(BF16)
    for part in range(2):
        taken = lax.dot_general(
            pick, coef_ref[part], (((1,), (1,)), ((), ())), preferred_element_type=F32
        )
        out_ref[:, part * rows : (part + 1) * rows] = taken.astype(BF16)
    pos = pos_ref[...]
    width = pos.shape[1]
    base = 2 * rows
    for index, piece in enumerate(split3(pos)):
        start = base + index * width
        out_ref[:, start : start + width] = jnp.broadcast_to(piece.astype(F32), (out_ref.shape[0], width)).astype(BF16)


def base_wave(turns):
    quarter = (turns - 0.5) * (0.5 * PI)
    square = quarter * quarter
    sine = quarter * (
        1.0 + square * (-1 / 6 + square * (1 / 120 + square * (-1 / 5040 + square * (1 / 362880))))
    )
    cosine = 1.0 + square * (
        -1 / 2 + square * (1 / 24 + square * (-1 / 720 + square * (1 / 40320 - square * (1 / 3628800))))
    )
    sine, cosine = 2.0 * sine * cosine, 1.0 - 2.0 * sine * sine
    sine, cosine = 2.0 * sine * cosine, 1.0 - 2.0 * sine * sine
    return -cosine, -sine


def times(left, right):
    return left[0] * right[0] - left[1] * right[1], left[1] * right[0] + left[0] * right[1]


def orbital_kernel(recv_ref, lat_ref, out_ref, sum_ref, table_ref, wave_ref, eight_ref, *, unroll):
    groups, senders, _ = recv_ref.shape
    rows = lat_ref.shape[2]
    base = 2 * rows
    piece = (recv_ref.shape[2] - base) // 6
    chunks = piece // LANES
    pairs = senders * chunks // 2

    sum_ref[...] = jnp.zeros_like(sum_ref)
    frequency = lax.broadcasted_iota(jnp.int32, (HALF, rows), 0)

    def fold(group, carry):
        both = jnp.sum(recv_ref[group, :, :base].astype(F32), axis=0, keepdims=True)
        c_real = both[:, :rows]
        c_imag = both[:, rows:]
        lat_a = lat_ref[0, pl.ds(group, 1), :]
        lat_b = lat_ref[1, pl.ds(group, 1), :]
        sign_a = jnp.where(lat_a < 0, -1.0, 1.0)
        sign_b = jnp.where(lat_b < 0, -1.0, 1.0)
        at_a = frequency == jnp.abs(lat_a)
        at_b = frequency == jnp.abs(lat_b)
        zero = jnp.zeros((), F32)
        left = jnp.concatenate(
            [
                jnp.where(at_a, value, zero).astype(BF16)
                for value in (c_real, c_real * sign_a, c_imag, c_imag * sign_a)
            ],
            axis=0,
        )
        right = jnp.concatenate(
            [jnp.where(at_b, value, zero).astype(BF16) for value in (jnp.ones_like(sign_b), sign_b)], axis=0
        )
        sum_ref[...] += lax.dot_general(left, right, (((1,), (1,)), ((), ())), preferred_element_type=F32)
        return carry

    lax.fori_loop(0, groups, fold, 0)
    real_even = sum_ref[0:HALF, :]
    real_odd = sum_ref[HALF : 2 * HALF, :]
    imag_even = sum_ref[2 * HALF : 3 * HALF, :]
    imag_odd = sum_ref[3 * HALF : 4 * HALF, :]
    even = lax.broadcasted_iota(jnp.int32, real_even.shape, 1) < HALF
    table = jnp.concatenate(
        [
            jnp.where(even, real_even, -imag_even),
            jnp.where(even, -imag_odd, -real_odd),
            jnp.where(even, imag_even, real_even),
            jnp.where(even, real_odd, -imag_odd),
        ],
        axis=0,
    )
    high = table.astype(BF16).astype(F32)
    low = table - high
    pad = jnp.zeros((4 * HALF, table_ref.shape[1] - 6 * HALF), F32)
    table_ref[...] = jnp.concatenate([high, high, low, pad], axis=1).astype(BF16)

    def waves(group, carry):
        for chunk in range(chunks):
            for axis in range(2):
                turns = jnp.zeros((senders, LANES), F32)
                for part in range(3):
                    start = base + (part * 2 + axis) * piece + chunk * LANES
                    turns = turns + recv_ref[group, :, start : start + LANES].astype(F32)
                first = base_wave(turns)
                power = (jnp.ones_like(turns), jnp.zeros_like(turns))
                for k in range(8):
                    for half in range(2):
                        wave_ref[2 * axis + half, group, pl.ds(chunk * 8 + k, senders, stride=chunks * 8), :] = power[half]
                    power = first if k == 0 else times(power, first)
                for half in range(2):
                    eight_ref[2 * axis + half, group, pl.ds(chunk, senders, stride=chunks), :] = power[half]
        return carry

    lax.fori_loop(0, groups, waves, 0)

    def basis(group, chunk, axis):
        cosines, sines = [], []
        now = tuple(wave_ref[2 * axis + half, group, pl.ds(chunk * 8, 8), :] for half in range(2))
        step = tuple(
            jnp.broadcast_to(eight_ref[2 * axis + half, group, pl.ds(chunk, 1), :], (8, LANES)) for half in range(2)
        )
        for block in range(HALF // 8):
            cosines.append(now[0])
            sines.append(now[1])
            if block < HALF // 8 - 1:
                now = times(now, step)
        return jnp.concatenate(cosines + sines, axis=0)

    zeros = jnp.zeros((table_ref.shape[1] - 6 * HALF, 2 * LANES), BF16)

    def evaluate(index, carry):
        for inner in range(unroll):
            flat = index * unroll + inner
            group = flat // pairs
            pair = flat % pairs
            wave_y = jnp.concatenate([basis(group, pair * 2 + side, 1) for side in range(2)], axis=1)
            high_y = wave_y.astype(BF16)
            low_y = (wave_y - high_y.astype(F32)).astype(BF16)
            weights = jnp.concatenate([high_y, low_y, high_y, zeros], axis=0)
            inside = jnp.dot(table_ref[...], weights, preferred_element_type=F32)
            wave_x = jnp.concatenate([basis(group, pair * 2 + side, 0) for side in range(2)], axis=1)
            for half in range(2):
                value = jnp.sum(inside[half * 2 * HALF : (half + 1) * 2 * HALF, :] * wave_x, axis=0, keepdims=True)
                start = pl.multiple_of(half * senders * piece + pair * 2 * LANES, 2 * LANES)
                out_ref[pl.ds(group, 1), pl.ds(start, 2 * LANES)] = value
        return carry

    lax.fori_loop(0, groups * pairs // unroll, evaluate, 0)


def gradient_kernel(target_ref, feature_ref, head_ref, mask_ref, out_ref, *, scale):
    count = feature_ref.shape[0]
    slots = target_ref.shape[0]
    features = feature_ref[...]
    net = lax.dot_general(head_ref[...], features, (((1,), (1,)), ((), ())), preferred_element_type=F32)
    mine = mask_ref[...] != 0
    parts = []
    for half in range(2):
        scaled = (net[half * slots : (half + 1) * slots, :] - target_ref[:, half * count : (half + 1) * count]) * scale
        parts.append(jnp.where(mine, scaled, 0.0))
    spread = jnp.concatenate(parts, axis=0)
    total = jnp.zeros(out_ref.shape, F32)
    for piece in split3(spread):
        total = total + jnp.dot(piece, features, preferred_element_type=F32)
    out_ref[...] = total


def call(kernel, out, scratch=(), name=None):
    return pl.pallas_call(
        kernel,
        out_shape=out,
        scratch_shapes=list(scratch),
        name=name,
        interpret=INTERPRET,
        compiler_params=pltpu.CompilerParams(vmem_limit_bytes=48 * 1024 * 1024),
    )


def local(positions, coefficients, lattice, spin_labels, occupied, features, orbital_head):
    walk_count = lax.axis_size("walk")
    band_count = lax.axis_size("band")
    everyone = ("walk", "band")
    devices = walk_count * band_count
    band_index = lax.axis_index("band")
    rows = coefficients.shape[1]
    bands = coefficients.shape[2]
    count = positions.shape[1]
    piece = count // band_count
    orbitals = occupied.shape[0] * occupied.shape[1]
    each = orbitals // band_count

    by_device = jnp.transpose(occupied.reshape(band_count, each).astype(jnp.int32))
    by_device = jnp.concatenate([by_device, jnp.full((walk_count - each, band_count), -1, jnp.int32)], axis=0)
    wanted = by_device.reshape(devices, 1) - band_index * bands
    pick = (wanted == lax.broadcasted_iota(jnp.int32, (devices, bands), 1)).astype(F32)
    share = lax.dynamic_slice_in_dim(positions, band_index * piece, piece, 1).reshape(1, 2 * piece)
    sent = call(
        send_kernel, jax.ShapeDtypeStruct((devices, 2 * rows + 6 * piece), BF16), name="send"
    )(coefficients, pick, share)
    received = lax.all_to_all(sent, everyone, 0, 0, tiled=True)
    received = received.reshape(walk_count, band_count, sent.shape[1])

    chunks = count // LANES
    values = call(
        functools.partial(orbital_kernel, unroll=4),
        jax.ShapeDtypeStruct((walk_count, 2 * count), F32),
        [
            pltpu.VMEM((4 * HALF, 2 * HALF), F32),
            pltpu.VMEM((4 * HALF, 512), BF16),
            pltpu.VMEM((4, walk_count, 8 * chunks, LANES), F32),
            pltpu.VMEM((4, walk_count, chunks, LANES), F32),
        ],
        name="orbital",
    )(received, lattice.reshape(2, walk_count, rows))
    target = lax.all_to_all(values, "walk", 0, 0, tiled=True)

    spins = occupied.shape[0]
    per_spin = band_count // spins
    spin = band_index // per_spin
    columns = orbital_head.reshape(orbital_head.shape[0], spins, 2, per_spin, each)
    columns = lax.dynamic_index_in_dim(columns, spin, 1, keepdims=False)
    columns = lax.dynamic_index_in_dim(columns, band_index % per_spin, 2, keepdims=False)
    columns = jnp.transpose(columns, (1, 2, 0))
    columns = jnp.pad(columns, ((0, 0), (0, walk_count - each), (0, 0))).reshape(2 * walk_count, -1)
    mine = (spin_labels == spin).astype(jnp.int32).reshape(1, count)
    walkers = walk_count * count // orbitals
    hidden = features.shape[1]
    own = call(
        functools.partial(gradient_kernel, scale=1.0 / walkers),
        jax.ShapeDtypeStruct((2 * walk_count, hidden), F32),
        name="gradient",
    )(target, features, columns, mine)
    own = own.reshape(2, walk_count, hidden)[:, :each].reshape(-1, LANES)
    shares = lax.all_to_all(jnp.broadcast_to(own, (walk_count, *own.shape)), "walk", 0, 0, tiled=True)
    summed = jnp.sum(shares, axis=0)
    whole = lax.all_to_all(jnp.broadcast_to(summed, (band_count, *own.shape)), "band", 0, 0, tiled=True)
    whole = whole.reshape(spins, per_spin, 2, each, hidden)
    return jnp.transpose(whole, (4, 0, 2, 1, 3)).reshape(hidden, 2 * orbitals)


def solution(mesh):
    return jax.shard_map(
        local,
        mesh=mesh,
        in_specs=(
            P(None, "walk"),
            P(None, "walk", "band"),
            P(),
            P("walk"),
            P(),
            P("walk", None),
            P(),
        ),
        out_specs=P(),
        check_vma=False,
    )
```

```python
import functools

import jax
import jax.numpy as jnp
from jax import lax
from jax.experimental import pallas as pl
from jax.experimental.pallas import tpu as pltpu
from jax.sharding import PartitionSpec as P

INTERPRET = False
F32 = jnp.float32
BF16 = jnp.bfloat16
PI = 3.141592653589793
BLOCK = 40
HALF = 80
LANES = 128


def split3(value):
    high = value.astype(BF16)
    rest = value - high.astype(F32)
    middle = rest.astype(BF16)
    low = (rest - middle.astype(F32)).astype(BF16)
    return high, middle, low


def coefficient_row(index):
    return 8 * (index // 2) + 6 + index % 2 if index < 6 else 18 + index


def send_kernel(coef_ref, occ_ref, pos_ref, label_ref, out_ref, slot_ref, stage_ref):
    rows = coef_ref.shape[1]
    bands = coef_ref.shape[2]
    devices = out_ref.shape[0] // BLOCK
    spins, per_spin = occ_ref.shape
    senders = lax.axis_size("band")
    each = spins * per_spin // senders
    count = pos_ref.shape[1]
    piece = count // senders
    tiles = rows // LANES
    mine = lax.axis_index("band")

    line = lax.broadcasted_iota(jnp.int32, (8, bands), 0)
    picks = []
    for group in range(devices // senders):
        if group >= each:
            picks.append(jnp.zeros((8, bands), F32))
            continue
        wanted = jnp.full((8, bands), -1, jnp.int32)
        for sender in range(senders):
            orbital = sender * each + group
            wanted = jnp.where(line == sender, occ_ref[orbital // per_spin, orbital % per_spin], wanted)
        lane = lax.broadcasted_iota(jnp.int32, (8, bands), 1) + mine * bands
        picks.append(jnp.where(lane == wanted, 1.0, 0.0))
    pick = jnp.concatenate(picks, axis=0).astype(BF16)
    for part in range(2):
        taken = lax.dot_general(
            pick, coef_ref[part], (((1,), (1,)), ((), ())), preferred_element_type=F32
        )
        for tile in range(tiles):
            at = coefficient_row(part * tiles + tile)
            stage_ref[pl.ds(at, devices, stride=BLOCK), :] = taken[:, tile * LANES : (tile + 1) * LANES]

    chunks = count // LANES
    up = label_ref[...] == 0
    ones = jnp.where(up, 1.0, 0.0)
    row = lax.broadcasted_iota(jnp.int32, (LANES, LANES), 0)
    column = lax.broadcasted_iota(jnp.int32, (LANES, LANES), 1)
    until = jnp.where(row <= column, 1.0, 0.0).astype(BF16)
    inside = jnp.dot(ones.astype(BF16), until, preferred_element_type=F32)
    whole = jnp.broadcast_to(inside[:, LANES - 1 : LANES], inside.shape)
    row = lax.broadcasted_iota(jnp.int32, (chunks, chunks), 0)
    column = lax.broadcasted_iota(jnp.int32, (chunks, chunks), 1)
    before = jnp.where(column < row, 1.0, 0.0).astype(BF16)
    rank = inside + jnp.dot(before, whole.astype(BF16), preferred_element_type=F32)
    total = jnp.sum(whole, axis=0, keepdims=True)
    place = (
        lax.broadcasted_iota(jnp.int32, rank.shape, 0) * LANES + lax.broadcasted_iota(jnp.int32, rank.shape, 1)
    ).astype(F32)
    slot = jnp.where(up, rank - 1.0, total + place - rank)
    slot = jnp.concatenate([slot[chunk : chunk + 1, :] for chunk in range(chunks)], axis=1)
    slot_ref[...] = slot
    here = lax.broadcasted_iota(jnp.int32, (piece, count), 0) + mine * piece
    move = jnp.where(here.astype(F32) == slot, 1.0, 0.0).astype(BF16)
    parts = jnp.concatenate([part.astype(F32) for part in split3(pos_ref[...])], axis=0).astype(BF16)
    moved = lax.dot_general(parts, move, (((1,), (1,)), ((), ())), preferred_element_type=F32)

    def everywhere(at, value):
        stage_ref[pl.ds(at, devices, stride=BLOCK), :] = jnp.broadcast_to(value, (devices, LANES))

    for part in range(3):
        for axis in range(2):
            for chunk in range(piece // LANES):
                at = 8 * part + axis * (piece // LANES) + chunk
                everywhere(at, moved[part * 2 + axis : part * 2 + axis + 1, chunk * LANES : (chunk + 1) * LANES])
    tens = jnp.floor(total * (1 / 64))
    everywhere(36, tens)
    everywhere(37, total - tens * 64.0)
    everywhere(38, jnp.zeros_like(total))
    everywhere(39, jnp.zeros_like(total))
    out_ref[...] = stage_ref[...].astype(BF16)


def sort_kernel(slot_ref, feature_ref, out_ref):
    count = feature_ref.shape[0]
    step = 384

    def block(index, carry):
        start = pl.multiple_of(index * step, step)
        here = lax.broadcasted_iota(jnp.int32, (step, count), 0) + start
        move = jnp.where(here.astype(F32) == slot_ref[...], 1.0, 0.0).astype(BF16)
        moved = jnp.dot(move, feature_ref[...], preferred_element_type=F32)
        out_ref[pl.ds(start, step), :] = moved.astype(BF16)
        return carry

    lax.fori_loop(0, count // step, block, 0)


def base_wave(turns):
    quarter = (turns - 0.5) * (0.5 * PI)
    square = quarter * quarter
    sine = quarter * (
        1.0 + square * (-1 / 6 + square * (1 / 120 + square * (-1 / 5040 + square * (1 / 362880))))
    )
    cosine = 1.0 + square * (
        -1 / 2 + square * (1 / 24 + square * (-1 / 720 + square * (1 / 40320 - square * (1 / 3628800))))
    )
    sine, cosine = 2.0 * sine * cosine, 1.0 - 2.0 * sine * sine
    sine, cosine = 2.0 * sine * cosine, 1.0 - 2.0 * sine * sine
    return -cosine, -sine


def times(left, right):
    return left[0] * right[0] - left[1] * right[1], left[1] * right[0] + left[0] * right[1]


def orbital_kernel(recv_ref, lat_ref, out_ref, sum_ref, table_ref, wave_ref, eight_ref, list_ref, *, unroll, each):
    groups = out_ref.shape[0]
    senders = recv_ref.shape[0] // groups
    rows = lat_ref.shape[2]
    tiles = rows // LANES
    chunks = out_ref.shape[1] // 2
    pairs = chunks // 2
    own = chunks // senders
    upper = lax.axis_index("band") < senders // 2
    active = lax.axis_index("walk") < each

    out_ref[...] = jnp.zeros_like(out_ref)
    sum_ref[...] = jnp.zeros_like(sum_ref)
    frequency = lax.broadcasted_iota(jnp.int32, (HALF, rows), 0)

    def fold(group, carry):
        both = jnp.zeros((BLOCK, LANES), F32)
        for sender in range(senders):
            both = both + recv_ref[group * senders + sender].astype(F32)
        c_real, c_imag = (
            jnp.concatenate([both[coefficient_row(k + t) :, :][:1] for t in range(tiles)], axis=1) for k in (0, tiles)
        )
        lat_a = lat_ref[0, pl.ds(group, 1), :]
        lat_b = lat_ref[1, pl.ds(group, 1), :]
        sign_a = jnp.where(lat_a < 0, -1.0, 1.0)
        sign_b = jnp.where(lat_b < 0, -1.0, 1.0)
        at_a = frequency == jnp.abs(lat_a)
        at_b = frequency == jnp.abs(lat_b)
        zero = jnp.zeros((), F32)
        left = jnp.concatenate(
            [
                jnp.where(at_a, value, zero).astype(BF16)
                for value in (c_real, c_real * sign_a, c_imag, c_imag * sign_a)
            ],
            axis=0,
        )
        right = jnp.concatenate(
            [jnp.where(at_b, value, zero).astype(BF16) for value in (jnp.ones_like(sign_b), sign_b)], axis=0
        )
        sum_ref[...] += lax.dot_general(left, right, (((1,), (1,)), ((), ())), preferred_element_type=F32)
        return carry

    lax.fori_loop(0, groups, fold, 0)
    real_even = sum_ref[0:HALF, :]
    real_odd = sum_ref[HALF : 2 * HALF, :]
    imag_even = sum_ref[2 * HALF : 3 * HALF, :]
    imag_odd = sum_ref[3 * HALF : 4 * HALF, :]
    even = lax.broadcasted_iota(jnp.int32, real_even.shape, 1) < HALF
    table = jnp.concatenate(
        [
            jnp.where(even, real_even, -imag_even),
            jnp.where(even, -imag_odd, -real_odd),
            jnp.where(even, imag_even, real_even),
            jnp.where(even, real_odd, -imag_odd),
        ],
        axis=0,
    )
    high = table.astype(BF16).astype(F32)
    low = table - high
    pad = jnp.zeros((4 * HALF, table_ref.shape[1] - 6 * HALF), F32)
    table_ref[...] = jnp.concatenate([high, high, low, pad], axis=1).astype(BF16)

    def waves(group, length):
        for sender in range(senders):
            block = recv_ref[group * senders + sender].astype(F32)
            first = base_wave(block[0:8] + block[8:16] + block[16:24])
            power = (jnp.ones((8, LANES), F32), jnp.zeros((8, LANES), F32))
            for k in range(8):
                for half in range(2):
                    wave_ref[half, group * senders + sender, pl.ds(k, 8, stride=8), :] = power[half]
                power = first if k == 0 else times(power, first)
            for half in range(2):
                eight_ref[half, group * senders + sender, :, :] = power[half]
            if sender == 0:
                number = (block[36:37, :] * 64.0 + block[37:38, :]).astype(jnp.int32)
        number = number[0, 0]
        low = jnp.where(upper, 0, number // (2 * LANES))
        high = jnp.where(upper, (number + 2 * LANES - 1) // (2 * LANES), pairs)
        high = jnp.where(active, high, low)

        def note(pair, at):
            list_ref[at] = group * pairs + pair
            return at + 1

        return lax.fori_loop(low, high, note, length)

    length = lax.fori_loop(0, groups, waves, 0)

    def basis(flat, axis):
        sender = flat // own
        line = axis * own + flat % own
        cosines, sines = [], []
        start = pl.multiple_of(line * 8, 8)
        now = tuple(wave_ref[half, sender, pl.ds(start, 8), :] for half in range(2))
        step = tuple(jnp.broadcast_to(eight_ref[half, sender, pl.ds(line, 1), :], (8, LANES)) for half in range(2))
        for block in range(HALF // 8):
            cosines.append(now[0])
            sines.append(now[1])
            if block < HALF // 8 - 1:
                now = times(now, step)
        return jnp.concatenate(cosines + sines, axis=0)

    zeros = jnp.zeros((table_ref.shape[1] - 6 * HALF, 2 * LANES), BF16)

    def evaluate(index, carry):
        for inner in range(unroll):
            entry = list_ref[jnp.minimum(index * unroll + inner, length - 1)]
            group = entry // pairs
            wave_y = jnp.concatenate([basis(entry * 2 + side, 1) for side in range(2)], axis=1)
            high_y = wave_y.astype(BF16)
            low_y = (wave_y - high_y.astype(F32)).astype(BF16)
            weights = jnp.concatenate([high_y, low_y, high_y, zeros], axis=0)
            inside = jnp.dot(table_ref[...], weights, preferred_element_type=F32)
            wave_x = jnp.concatenate([basis(entry * 2 + side, 0) for side in range(2)], axis=1)
            for half in range(2):
                value = jnp.sum(inside[half * 2 * HALF : (half + 1) * 2 * HALF, :] * wave_x, axis=0, keepdims=True)
                for side in range(2):
                    at = half * chunks + (entry - group * pairs) * 2 + side
                    out_ref[group, pl.ds(at, 1), :] = value[:, side * LANES : (side + 1) * LANES]
        return carry

    lax.fori_loop(0, (length + unroll - 1) // unroll, evaluate, 0)


def gradient_kernel(target_ref, feature_ref, head_ref, mask_ref, out_ref, *, scale):
    count = feature_ref.shape[0]
    chunks = count // LANES
    slots = head_ref.shape[0] // 2
    features = feature_ref[...]
    net = lax.dot_general(head_ref[...], features, (((1,), (1,)), ((), ())), preferred_element_type=F32)
    mine = mask_ref[...] != 0
    parts = []
    for half in range(2):
        target = jnp.concatenate(
            [target_ref[pl.ds(half * chunks + chunk, slots, stride=2 * chunks), :] for chunk in range(chunks)], axis=1
        )
        scaled = (net[half * slots : (half + 1) * slots, :] - target) * scale
        parts.append(jnp.where(mine, scaled, 0.0))
    spread = jnp.concatenate(parts, axis=0)
    total = jnp.zeros(out_ref.shape, F32)
    for piece in split3(spread):
        total = total + jnp.dot(piece, features, preferred_element_type=F32)
    out_ref[...] = total


def call(kernel, out, scratch=(), name=None, **more):
    return pl.pallas_call(
        kernel,
        out_shape=out,
        **more,
        scratch_shapes=list(scratch),
        name=name,
        interpret=INTERPRET,
        compiler_params=pltpu.CompilerParams(vmem_limit_bytes=48 * 1024 * 1024),
    )


def local(positions, coefficients, lattice, spin_labels, occupied, features, orbital_head):
    walk_count = lax.axis_size("walk")
    band_count = lax.axis_size("band")
    everyone = ("walk", "band")
    devices = walk_count * band_count
    band_index = lax.axis_index("band")
    rows = coefficients.shape[1]
    count = positions.shape[1]
    orbitals = occupied.shape[0] * occupied.shape[1]
    each = orbitals // band_count

    whole = pl.BlockSpec(memory_space=pltpu.VMEM)
    sent, slot = call(
        send_kernel,
        (
            jax.ShapeDtypeStruct((devices * BLOCK, LANES), BF16),
            jax.ShapeDtypeStruct((1, count), F32),
        ),
        [pltpu.VMEM((devices * BLOCK, LANES), F32)],
        name="send",
        in_specs=[whole, pl.BlockSpec(memory_space=pltpu.SMEM), whole, whole],
    )(coefficients, occupied, positions, spin_labels.reshape(count // LANES, LANES))
    received = lax.all_to_all(sent.reshape(devices, BLOCK, LANES), everyone, 0, 0, tiled=True)
    sorted_features = call(sort_kernel, jax.ShapeDtypeStruct(features.shape, BF16), name="sort")(slot, features)

    chunks = count // LANES
    values = call(
        functools.partial(orbital_kernel, unroll=4, each=each),
        jax.ShapeDtypeStruct((walk_count, 2 * chunks, LANES), F32),
        [
            pltpu.VMEM((4 * HALF, 2 * HALF), F32),
            pltpu.VMEM((4 * HALF, 512), BF16),
            pltpu.VMEM((2, devices, 64, LANES), F32),
            pltpu.VMEM((2, devices, 8, LANES), F32),
            pltpu.SMEM((walk_count * chunks // 2,), jnp.int32),
        ],
        name="orbital",
    )(received, lattice.reshape(2, walk_count, rows))
    target = lax.all_to_all(values, "walk", 0, 0, tiled=True).reshape(-1, LANES)

    spins = occupied.shape[0]
    per_spin = band_count // spins
    spin = band_index // per_spin
    columns = orbital_head.reshape(orbital_head.shape[0], spins, 2, per_spin, each)
    columns = lax.dynamic_index_in_dim(columns, spin, 1, keepdims=False)
    columns = lax.dynamic_index_in_dim(columns, band_index % per_spin, 2, keepdims=False)
    columns = jnp.transpose(columns, (1, 2, 0))
    columns = jnp.pad(columns, ((0, 0), (0, walk_count - each), (0, 0))).reshape(2 * walk_count, -1)
    ups = jnp.sum((spin_labels == 0).astype(jnp.int32))
    place = lax.broadcasted_iota(jnp.int32, (1, count), 1)
    mine = ((place < ups) == (spin == 0)).astype(jnp.int32)
    walkers = walk_count * count // orbitals
    hidden = features.shape[1]
    own = call(
        functools.partial(gradient_kernel, scale=1.0 / walkers),
        jax.ShapeDtypeStruct((2 * walk_count, hidden), F32),
        name="gradient",
    )(target, sorted_features, columns, mine)
    own = own.reshape(2, walk_count, hidden)[:, :each].reshape(-1, LANES)
    shares = lax.all_to_all(jnp.broadcast_to(own, (walk_count, *own.shape)), "walk", 0, 0, tiled=True)
    summed = jnp.sum(shares, axis=0)
    whole = lax.all_to_all(jnp.broadcast_to(summed, (band_count, *own.shape)), "band", 0, 0, tiled=True)
    whole = whole.reshape(spins, per_spin, 2, each, hidden)
    return jnp.transpose(whole, (4, 0, 2, 1, 3)).reshape(hidden, 2 * orbitals)


def solution(mesh):
    return jax.shard_map(
        local,
        mesh=mesh,
        in_specs=(
            P(None, "walk"),
            P(None, "walk", "band"),
            P(),
            P("walk"),
            P(),
            P("walk", None),
            P(),
        ),
        out_specs=P(),
        check_vma=False,
    )
```

```python
import functools

import jax
import jax.numpy as jnp
from jax import lax
from jax.experimental import pallas as pl
from jax.experimental.pallas import tpu as pltpu
from jax.sharding import PartitionSpec as P


INTERPRET = False
F32 = jnp.float32
BF16 = jnp.bfloat16
PI = 3.141592653589793
BLOCK = 24
RUN = 1024
HALF = 80
LANES = 128


def split3(value):
    high = value.astype(BF16)
    rest = value - high.astype(F32)
    middle = rest.astype(BF16)
    low = (rest - middle.astype(F32)).astype(BF16)
    return high, middle, low


def pick_kernel(coef_hbm, occ_hbm, out_ref, coef_ref, occ_ref, stage_ref, sems):
    copies = [pltpu.make_async_copy(occ_hbm, occ_ref, sems.at[2])]
    copies += [pltpu.make_async_copy(coef_hbm.at[part], coef_ref.at[part], sems.at[part]) for part in range(2)]
    for copy in copies:
        copy.start()
    _, rows, bands = coef_ref.shape
    spins, per_spin = occ_ref.shape
    devices = stage_ref.shape[0] // BLOCK
    senders = lax.axis_size("band")
    each = spins * per_spin // senders
    tiles = rows // LANES
    base = lax.axis_index("band") * bands
    for row in range(2 * tiles, BLOCK):
        stage_ref[pl.ds(row, devices, stride=BLOCK), :] = jnp.zeros((devices, LANES), F32)
    line = lax.broadcasted_iota(jnp.int32, (8, bands), 0)
    lane = lax.broadcasted_iota(jnp.int32, (8, bands), 1) + base
    copies[0].wait()
    picks = []
    for group in range(devices // senders):
        wanted = jnp.full((8, bands), -1, jnp.int32)
        if group < each:
            for sender in range(senders):
                orbital = sender * each + group
                wanted = jnp.where(line == sender, occ_ref[orbital // per_spin, orbital % per_spin], wanted)
        picks.append(jnp.where(lane == wanted, 1.0, 0.0))
    pick = jnp.concatenate(picks, axis=0).astype(BF16)
    for part in range(2):
        copies[1 + part].wait()
        taken = lax.dot_general(
            pick, coef_ref[part], (((1,), (1,)), ((), ())), preferred_element_type=F32
        )
        for tile in range(tiles):
            stage_ref[pl.ds(part * tiles + tile, devices, stride=BLOCK), :] = taken[:, tile * LANES : (tile + 1) * LANES]
    out_ref[...] = stage_ref[...].astype(BF16)


def order_kernel(pos_ref, label_ref, out_ref, slot_ref, up_ref):
    chunks = label_ref.shape[0]
    own = RUN // LANES
    runs = chunks // own
    up = label_ref[...] == 0
    ones = jnp.where(up, 1.0, 0.0)
    row = lax.broadcasted_iota(jnp.int32, (LANES, LANES), 0)
    column = lax.broadcasted_iota(jnp.int32, (LANES, LANES), 1)
    until = jnp.where(row <= column, 1.0, 0.0).astype(BF16)
    inside = jnp.dot(ones.astype(BF16), until, preferred_element_type=F32)
    whole = jnp.broadcast_to(inside[:, LANES - 1 : LANES], inside.shape).astype(BF16)
    row = lax.broadcasted_iota(jnp.int32, (chunks, chunks), 0)
    column = lax.broadcasted_iota(jnp.int32, (chunks, chunks), 1)
    same = jnp.where(row // own == column // own, 1.0, 0.0)
    before = jnp.where(column < row, same, 0.0).astype(BF16)
    rank = inside + jnp.dot(before, whole, preferred_element_type=F32)
    total = jnp.dot(same.astype(BF16), whole, preferred_element_type=F32)
    place = (
        lax.broadcasted_iota(jnp.int32, rank.shape, 0) % own * LANES + lax.broadcasted_iota(jnp.int32, rank.shape, 1)
    ).astype(F32)
    slot = jnp.where(up, rank - 1.0, total + place - rank)
    first = jnp.where(place < total, 1.0, 0.0)
    up_ref[...] = jnp.concatenate([first[chunk : chunk + 1, :] for chunk in range(chunks)], axis=1)
    parts = jnp.concatenate([part.astype(F32) for part in split3(pos_ref[...])], axis=0).astype(BF16)
    here = lax.broadcasted_iota(jnp.int32, (RUN, RUN), 0).astype(F32)
    for run in range(runs):
        line = jnp.concatenate([slot[run * own + k : run * own + k + 1, :] for k in range(own)], axis=1)
        slot_ref[run : run + 1, :] = line
        move = jnp.where(here == line, 1.0, 0.0).astype(BF16)
        moved = lax.dot_general(
            parts[:, run * RUN : (run + 1) * RUN], move, (((1,), (1,)), ((), ())), preferred_element_type=F32
        )
        moved = moved[0:2] + moved[2:4] + moved[4:6]
        for axis in range(2):
            for k in range(own):
                at = axis * chunks + run * own + k
                out_ref[at : at + 1, :] = moved[axis : axis + 1, k * LANES : (k + 1) * LANES]
        out_ref[2 * chunks + run : 2 * chunks + run + 1, :] = total[run * own : run * own + 1, :]
    out_ref[2 * chunks + runs :, :] = jnp.zeros((out_ref.shape[0] - 2 * chunks - runs, LANES), F32)


def sort_kernel(slot_ref, feature_ref, out_ref):
    here = lax.broadcasted_iota(jnp.int32, (RUN, RUN), 0).astype(F32)
    for run in range(slot_ref.shape[0]):
        move = jnp.where(here == slot_ref[run : run + 1, :], 1.0, 0.0).astype(BF16)
        moved = jnp.dot(move, feature_ref[run * RUN : (run + 1) * RUN, :], preferred_element_type=F32)
        out_ref[run * RUN : (run + 1) * RUN, :] = moved.astype(BF16)


def base_wave(turns):
    quarter = (turns - 0.5) * (0.5 * PI)
    square = quarter * quarter
    sine = quarter * (
        1.0 + square * (-1 / 6 + square * (1 / 120 + square * (-1 / 5040 + square * (1 / 362880))))
    )
    cosine = 1.0 + square * (
        -1 / 2 + square * (1 / 24 + square * (-1 / 720 + square * (1 / 40320 - square * (1 / 3628800))))
    )
    sine, cosine = 2.0 * sine * cosine, 1.0 - 2.0 * sine * sine
    sine, cosine = 2.0 * sine * cosine, 1.0 - 2.0 * sine * sine
    return -cosine, -sine


def times(left, right):
    return left[0] * right[0] - left[1] * right[1], left[1] * right[0] + left[0] * right[1]


def fold_kernel(recv_ref, lat_ref, table_ref, sum_ref):
    groups = lat_ref.shape[1]
    senders = recv_ref.shape[0] // groups
    rows = lat_ref.shape[2]
    tiles = rows // LANES

    sum_ref[...] = jnp.zeros_like(sum_ref)
    frequency = lax.broadcasted_iota(jnp.int32, (HALF, rows), 0)

    def fold(group, carry):
        both = recv_ref[group * senders].astype(F32)
        for sender in range(1, senders):
            both = both + recv_ref[group * senders + sender].astype(F32)
        c_real, c_imag = (jnp.concatenate([both[k + t : k + t + 1] for t in range(tiles)], axis=1) for k in (0, tiles))
        lat_a = lat_ref[0, pl.ds(group, 1), :]
        lat_b = lat_ref[1, pl.ds(group, 1), :]
        sign_a = jnp.where(lat_a < 0, -1.0, 1.0)
        sign_b = jnp.where(lat_b < 0, -1.0, 1.0)
        at_a = frequency == jnp.abs(lat_a)
        at_b = frequency == jnp.abs(lat_b)
        zero = jnp.zeros((), F32)
        left = jnp.concatenate(
            [
                jnp.where(at_a, value, zero).astype(BF16)
                for value in (c_real, c_real * sign_a, c_imag, c_imag * sign_a)
            ],
            axis=0,
        )
        right = jnp.concatenate(
            [jnp.where(at_b, value, zero).astype(BF16) for value in (jnp.ones_like(sign_b), sign_b)], axis=0
        )
        sum_ref[...] += lax.dot_general(left, right, (((1,), (1,)), ((), ())), preferred_element_type=F32)
        return carry

    lax.fori_loop(0, groups, fold, 0, unroll=4)
    real_even = sum_ref[0:HALF, :]
    real_odd = sum_ref[HALF : 2 * HALF, :]
    imag_even = sum_ref[2 * HALF : 3 * HALF, :]
    imag_odd = sum_ref[3 * HALF : 4 * HALF, :]
    even = lax.broadcasted_iota(jnp.int32, real_even.shape, 1) < HALF
    table = jnp.concatenate(
        [
            jnp.where(even, real_even, -imag_even),
            jnp.where(even, -imag_odd, -real_odd),
            jnp.where(even, imag_even, real_even),
            jnp.where(even, real_odd, -imag_odd),
        ],
        axis=0,
    )
    high = table.astype(BF16).astype(F32)
    low = table - high
    pad = jnp.zeros((4 * HALF, table_ref.shape[1] - 6 * HALF), F32)
    table_ref[...] = jnp.concatenate([high, high, low, pad], axis=1).astype(BF16)


def orbital_kernel(table_ref, pos_ref, out_ref, wave_ref, eight_ref, list_ref, *, unroll, each):
    groups = out_ref.shape[0]
    chunks = out_ref.shape[1] // 2
    own = RUN // LANES
    runs = chunks // own
    upper = lax.axis_index("band") < lax.axis_size("band") // 2
    walk = lax.axis_index("walk")
    active = walk < each
    out_ref[...] = jnp.zeros_like(out_ref)

    def waves(group, length):
        away = group ^ walk
        for line in range(0, 2 * chunks, 8):
            first = base_wave(pos_ref[away, line : line + 8, :])
            power = (jnp.ones((8, LANES), F32), jnp.zeros((8, LANES), F32))
            for k in range(8):
                for half in range(2):
                    wave_ref[half, group, pl.ds(line * 8 + k, 8, stride=8), :] = power[half]
                power = first if k == 0 else times(power, first)
            for half in range(2):
                eight_ref[half, group, line : line + 8, :] = power[half]
        numbers = pos_ref[away, 2 * chunks : 2 * chunks + runs, :].astype(jnp.int32)
        for run in range(runs):
            number = numbers[run, 0]
            low = jnp.where(upper, 0, number // LANES)
            high = jnp.where(upper, (number + LANES - 1) // LANES, own)
            high = jnp.where(active, high, low)

            def note(chunk, at):
                list_ref[at] = group * chunks + run * own + chunk
                return at + 1

            length = lax.fori_loop(low, high, note, length)
        return length

    length = lax.fori_loop(0, groups, waves, 0)

    def basis(entry, axis):
        group = entry // chunks
        line = axis * chunks + entry % chunks
        start = pl.multiple_of(line * 8, 8)
        now = tuple(wave_ref[half, group, pl.ds(start, 8), :] for half in range(2))
        step = tuple(jnp.broadcast_to(eight_ref[half, group, pl.ds(line, 1), :], (8, LANES)) for half in range(2))
        twice = 2.0 * step[0]
        last, now = now, times(now, step)
        cosines, sines = [last[0], now[0]], [last[1], now[1]]
        for _ in range(2, HALF // 8):
            last, now = now, tuple(twice * now[half] - last[half] for half in range(2))
            cosines.append(now[0])
            sines.append(now[1])
        return jnp.concatenate(cosines + sines, axis=0)

    zeros = jnp.zeros((table_ref.shape[1] - 6 * HALF, 2 * LANES), BF16)

    def evaluate(index, carry):
        for inner in range(unroll):
            entries = [
                list_ref[jnp.minimum((index * unroll + inner) * 2 + side, length - 1)] for side in range(2)
            ]
            wave_y = jnp.concatenate([basis(entry, 1) for entry in entries], axis=1)
            high_y = wave_y.astype(BF16)
            low_y = (wave_y - high_y.astype(F32)).astype(BF16)
            weights = jnp.concatenate([high_y, low_y, high_y, zeros], axis=0)
            inside = jnp.dot(table_ref[...], weights, preferred_element_type=F32)
            wave_x = jnp.concatenate([basis(entry, 0) for entry in entries], axis=1)
            for half in range(2):
                value = jnp.sum(inside[half * 2 * HALF : (half + 1) * 2 * HALF, :] * wave_x, axis=0, keepdims=True)
                for side, entry in enumerate(entries):
                    out_ref[entry // chunks, pl.ds(half * chunks + entry % chunks, 1), :] = value[:, side * LANES : (side + 1) * LANES]
        return carry

    lax.fori_loop(0, (length + 2 * unroll - 1) // (2 * unroll), evaluate, 0)


def gradient_kernel(target_ref, feature_ref, head_ref, up_ref, out_ref, *, scale):
    count = feature_ref.shape[0]
    chunks = count // LANES
    slots = head_ref.shape[0] // 2
    features = feature_ref[...]
    net = lax.dot_general(head_ref[...], features, (((1,), (1,)), ((), ())), preferred_element_type=F32)
    upper = lax.axis_index("band") < lax.axis_size("band") // 2
    mine = up_ref[...] == jnp.where(upper, 1.0, 0.0)
    parts = []
    for half in range(2):
        target = jnp.concatenate(
            [target_ref[pl.ds(half * chunks + chunk, slots, stride=2 * chunks), :] for chunk in range(chunks)], axis=1
        )
        scaled = (net[half * slots : (half + 1) * slots, :] - target) * scale
        parts.append(jnp.where(mine, scaled, 0.0))
    spread = jnp.concatenate(parts, axis=0)
    total = jnp.zeros(out_ref.shape, F32)
    for piece in split3(spread):
        total = total + jnp.dot(piece, features, preferred_element_type=F32)
    out_ref[...] = total


def call(kernel, out, scratch=(), **more):
    return pl.pallas_call(
        kernel,
        out_shape=out,
        **more,
        scratch_shapes=list(scratch),
        interpret=INTERPRET,
        compiler_params=pltpu.CompilerParams(vmem_limit_bytes=48 * 1024 * 1024),
    )


def local(positions, coefficients, lattice, spin_labels, occupied, features, orbital_head):
    walk_count = lax.axis_size("walk")
    band_count = lax.axis_size("band")
    band_index = lax.axis_index("band")
    devices = walk_count * band_count
    rows = coefficients.shape[1]
    count = positions.shape[1]
    orbitals = occupied.shape[0] * occupied.shape[1]
    each = orbitals // band_count

    chunks = count // LANES
    anywhere = pl.BlockSpec(memory_space=pl.ANY)
    picked = call(
        pick_kernel,
        jax.ShapeDtypeStruct((devices * BLOCK, LANES), BF16),
        [
            pltpu.VMEM(coefficients.shape, BF16),
            pltpu.SMEM(occupied.shape, jnp.int32),
            pltpu.VMEM((devices * BLOCK, LANES), F32),
            pltpu.SemaphoreType.DMA((3,)),
        ],
        in_specs=[anywhere, anywhere],
    )(coefficients, occupied)
    picked, positions = lax.optimization_barrier((picked, positions))
    received = lax.all_to_all(picked.reshape(devices, BLOCK, LANES), ("walk", "band"), 0, 0, tiled=True)
    ordered, slot, up = call(
        order_kernel,
        (
            jax.ShapeDtypeStruct((2 * chunks + 8, LANES), F32),
            jax.ShapeDtypeStruct((count // RUN, RUN), F32),
            jax.ShapeDtypeStruct((1, count), F32),
        ),
    )(positions, spin_labels.reshape(chunks, LANES))
    everyone = ordered[None]
    for flips in ((1,), (2, 4, 6), (8,)):
        moved = [lax.ppermute(everyone, "walk", [(k, k ^ flip) for k in range(walk_count)]) for flip in flips]
        everyone = jnp.concatenate([everyone, *moved], axis=0)
    sorted_features = call(sort_kernel, jax.ShapeDtypeStruct(features.shape, BF16))(slot, features)
    table = call(
        fold_kernel, jax.ShapeDtypeStruct((4 * HALF, 512), BF16), [pltpu.VMEM((4 * HALF, 2 * HALF), F32)]
    )(received, lattice.reshape(2, walk_count, rows))
    values = call(
        functools.partial(orbital_kernel, unroll=8, each=each),
        jax.ShapeDtypeStruct((walk_count, 2 * chunks, LANES), F32),
        [
            pltpu.VMEM((2, walk_count, 16 * chunks, LANES), F32),
            pltpu.VMEM((2, walk_count, 2 * chunks, LANES), F32),
            pltpu.SMEM((walk_count * chunks,), jnp.int32),
        ],
    )(table, everyone)
    target = lax.all_to_all(values, "walk", 0, 0, tiled=True).reshape(-1, LANES)

    spins = occupied.shape[0]
    per_spin = band_count // spins
    spin = band_index // per_spin
    columns = orbital_head.reshape(orbital_head.shape[0], spins, 2, per_spin, each)
    columns = lax.dynamic_index_in_dim(columns, spin, 1, keepdims=False)
    columns = lax.dynamic_index_in_dim(columns, band_index % per_spin, 2, keepdims=False)
    columns = jnp.transpose(columns, (1, 2, 0))
    columns = jnp.pad(columns, ((0, 0), (0, walk_count - each), (0, 0))).reshape(2 * walk_count, -1)
    walkers = walk_count * count // orbitals
    hidden = features.shape[1]
    own = call(
        functools.partial(gradient_kernel, scale=1.0 / walkers), jax.ShapeDtypeStruct((2 * walk_count, hidden), F32)
    )(target, sorted_features, columns, up)
    own = own.reshape(2, walk_count, hidden)[:, :each].reshape(-1, LANES)
    own = own + lax.ppermute(own, "walk", [(k, k ^ 1) for k in range(walk_count)])
    chips = walk_count // 2
    shares = lax.all_to_all(
        jnp.broadcast_to(own, (chips, *own.shape)),
        "walk",
        0,
        0,
        axis_index_groups=[[2 * chip + core for chip in range(chips)] for core in range(2)],
        tiled=True,
    )
    summed = jnp.sum(shares, axis=0)
    whole = lax.all_to_all(jnp.broadcast_to(summed, (band_count, *own.shape)), "band", 0, 0, tiled=True)
    whole = whole.reshape(spins, per_spin, 2, each, hidden)
    return jnp.transpose(whole, (4, 0, 2, 1, 3)).reshape(hidden, 2 * orbitals)


def solution(mesh):
    return jax.shard_map(
        local,
        mesh=mesh,
        in_specs=(
            P(None, "walk"),
            P(None, "walk", "band"),
            P(),
            P("walk"),
            P(),
            P("walk", None),
            P(),
        ),
        out_specs=P(),
        check_vma=False,
    )
```

```python
import functools

import jax
import jax.numpy as jnp
from jax import lax
from jax.experimental import pallas as pl
from jax.experimental.pallas import tpu as pltpu
from jax.sharding import PartitionSpec as P


INTERPRET = False
F32 = jnp.float32
BF16 = jnp.bfloat16
PI = 3.141592653589793
BLOCK = 24
RUN = 1024
HALF = 80
LANES = 128


def split3(value):
    high = value.astype(BF16)
    rest = value - high.astype(F32)
    middle = rest.astype(BF16)
    low = (rest - middle.astype(F32)).astype(BF16)
    return high, middle, low


def start_kernel(
    coef_hbm, occ_hbm, pos_hbm, label_hbm, sent_ref, ordered_ref, slot_ref, up_ref,
    coef_ref, occ_ref, pos_ref, label_ref, stage_ref, sems,
):
    copies = [
        pltpu.make_async_copy(label_hbm, label_ref, sems.at[0]),
        pltpu.make_async_copy(pos_hbm, pos_ref, sems.at[1]),
        pltpu.make_async_copy(occ_hbm, occ_ref, sems.at[2]),
    ]
    copies += [pltpu.make_async_copy(coef_hbm.at[part], coef_ref.at[part], sems.at[3 + part]) for part in range(2)]
    for copy in copies:
        copy.start()
    copies[0].wait()
    copies[1].wait()
    order(pos_ref, label_ref, ordered_ref, slot_ref, up_ref)
    copies[2].wait()
    pick(coef_ref, occ_ref, sent_ref, stage_ref, copies[3:])


def pick(coef_ref, occ_ref, out_ref, stage_ref, copies):
    _, rows, bands = coef_ref.shape
    spins, per_spin = occ_ref.shape
    devices = stage_ref.shape[0] // BLOCK
    senders = lax.axis_size("band")
    each = spins * per_spin // senders
    tiles = rows // LANES
    base = lax.axis_index("band") * bands
    for row in range(2 * tiles, BLOCK):
        stage_ref[pl.ds(row, devices, stride=BLOCK), :] = jnp.zeros((devices, LANES), F32)
    line = lax.broadcasted_iota(jnp.int32, (8, bands), 0)
    lane = lax.broadcasted_iota(jnp.int32, (8, bands), 1) + base
    picks = []
    for group in range(devices // senders):
        wanted = jnp.full((8, bands), -1, jnp.int32)
        if group < each:
            for sender in range(senders):
                orbital = sender * each + group
                wanted = jnp.where(line == sender, occ_ref[orbital // per_spin, orbital % per_spin], wanted)
        picks.append(jnp.where(lane == wanted, 1.0, 0.0))
    pick = jnp.concatenate(picks, axis=0).astype(BF16)
    for part in range(2):
        copies[part].wait()
        taken = lax.dot_general(
            pick, coef_ref[part], (((1,), (1,)), ((), ())), preferred_element_type=F32
        )
        for tile in range(tiles):
            stage_ref[pl.ds(part * tiles + tile, devices, stride=BLOCK), :] = taken[:, tile * LANES : (tile + 1) * LANES]
    out_ref[...] = stage_ref[...].astype(BF16)


def order(pos_ref, label_ref, out_ref, slot_ref, up_ref):
    chunks = label_ref.shape[0]
    own = RUN // LANES
    runs = chunks // own
    up = label_ref[...] == 0
    ones = jnp.where(up, 1.0, 0.0)
    row = lax.broadcasted_iota(jnp.int32, (LANES, LANES), 0)
    column = lax.broadcasted_iota(jnp.int32, (LANES, LANES), 1)
    until = jnp.where(row <= column, 1.0, 0.0).astype(BF16)
    inside = jnp.dot(ones.astype(BF16), until, preferred_element_type=F32)
    whole = jnp.broadcast_to(inside[:, LANES - 1 : LANES], inside.shape).astype(BF16)
    row = lax.broadcasted_iota(jnp.int32, (chunks, chunks), 0)
    column = lax.broadcasted_iota(jnp.int32, (chunks, chunks), 1)
    same = jnp.where(row // own == column // own, 1.0, 0.0)
    before = jnp.where(column < row, same, 0.0).astype(BF16)
    rank = inside + jnp.dot(before, whole, preferred_element_type=F32)
    total = jnp.dot(same.astype(BF16), whole, preferred_element_type=F32)
    place = (
        lax.broadcasted_iota(jnp.int32, rank.shape, 0) % own * LANES + lax.broadcasted_iota(jnp.int32, rank.shape, 1)
    ).astype(F32)
    slot = jnp.where(up, rank - 1.0, total + place - rank)
    first = jnp.where(place < total, 1.0, 0.0)
    up_ref[...] = jnp.concatenate([first[chunk : chunk + 1, :] for chunk in range(chunks)], axis=1)
    parts = jnp.concatenate([part.astype(F32) for part in split3(pos_ref[...])], axis=0).astype(BF16)
    here = lax.broadcasted_iota(jnp.int32, (RUN, RUN), 0).astype(F32)
    for run in range(runs):
        line = jnp.concatenate([slot[run * own + k : run * own + k + 1, :] for k in range(own)], axis=1)
        slot_ref[run : run + 1, :] = line
        move = jnp.where(here == line, 1.0, 0.0).astype(BF16)
        moved = lax.dot_general(
            parts[:, run * RUN : (run + 1) * RUN], move, (((1,), (1,)), ((), ())), preferred_element_type=F32
        )
        moved = moved[0:2] + moved[2:4] + moved[4:6]
        for axis in range(2):
            for k in range(own):
                at = axis * chunks + run * own + k
                out_ref[at : at + 1, :] = moved[axis : axis + 1, k * LANES : (k + 1) * LANES]
        out_ref[2 * chunks + run : 2 * chunks + run + 1, :] = total[run * own : run * own + 1, :]
    out_ref[2 * chunks + runs :, :] = jnp.zeros((out_ref.shape[0] - 2 * chunks - runs, LANES), F32)


def sort_kernel(slot_ref, feature_ref, head_ref, up_ref, out_ref, net_ref):
    here = lax.broadcasted_iota(jnp.int32, (RUN, RUN), 0).astype(F32)
    for run in range(slot_ref.shape[0]):
        move = jnp.where(here == slot_ref[run : run + 1, :], 1.0, 0.0).astype(BF16)
        moved = jnp.dot(move, feature_ref[run * RUN : (run + 1) * RUN, :], preferred_element_type=F32).astype(BF16)
        out_ref[run * RUN : (run + 1) * RUN, :] = moved
        net_ref[: head_ref.shape[0], run * RUN : (run + 1) * RUN] = lax.dot_general(
            head_ref[...], moved, (((1,), (1,)), ((), ())), preferred_element_type=F32
        )
    tail = net_ref.shape[0] - head_ref.shape[0]
    net_ref[head_ref.shape[0] :, :] = jnp.broadcast_to(up_ref[...], (tail, up_ref.shape[1]))


def base_wave(turns):
    quarter = (turns - 0.5) * (0.5 * PI)
    square = quarter * quarter
    sine = quarter * (
        1.0 + square * (-1 / 6 + square * (1 / 120 + square * (-1 / 5040 + square * (1 / 362880))))
    )
    cosine = 1.0 + square * (
        -1 / 2 + square * (1 / 24 + square * (-1 / 720 + square * (1 / 40320 - square * (1 / 3628800))))
    )
    sine, cosine = 2.0 * sine * cosine, 1.0 - 2.0 * sine * sine
    sine, cosine = 2.0 * sine * cosine, 1.0 - 2.0 * sine * sine
    return -cosine, -sine


def times(left, right):
    return left[0] * right[0] - left[1] * right[1], left[1] * right[0] + left[0] * right[1]


def fold_kernel(recv_ref, lat_ref, table_ref, sum_ref):
    groups = lat_ref.shape[1]
    senders = recv_ref.shape[0] // groups
    rows = lat_ref.shape[2]
    tiles = rows // LANES

    sum_ref[...] = jnp.zeros_like(sum_ref)
    frequency = lax.broadcasted_iota(jnp.int32, (HALF, rows), 0)

    def fold(group, carry):
        both = recv_ref[group * senders].astype(F32)
        for sender in range(1, senders):
            both = both + recv_ref[group * senders + sender].astype(F32)
        c_real, c_imag = (jnp.concatenate([both[k + t : k + t + 1] for t in range(tiles)], axis=1) for k in (0, tiles))
        lat_a = lat_ref[0, pl.ds(group, 1), :]
        lat_b = lat_ref[1, pl.ds(group, 1), :]
        sign_a = jnp.where(lat_a < 0, -1.0, 1.0)
        sign_b = jnp.where(lat_b < 0, -1.0, 1.0)
        at_a = frequency == jnp.abs(lat_a)
        at_b = frequency == jnp.abs(lat_b)
        zero = jnp.zeros((), F32)
        left = jnp.concatenate(
            [
                jnp.where(at_a, value, zero).astype(BF16)
                for value in (c_real, c_real * sign_a, c_imag, c_imag * sign_a)
            ],
            axis=0,
        )
        right = jnp.concatenate(
            [jnp.where(at_b, value, zero).astype(BF16) for value in (jnp.ones_like(sign_b), sign_b)], axis=0
        )
        sum_ref[...] += lax.dot_general(left, right, (((1,), (1,)), ((), ())), preferred_element_type=F32)
        return carry

    lax.fori_loop(0, groups, fold, 0, unroll=4)
    real_even = sum_ref[0:HALF, :]
    real_odd = sum_ref[HALF : 2 * HALF, :]
    imag_even = sum_ref[2 * HALF : 3 * HALF, :]
    imag_odd = sum_ref[3 * HALF : 4 * HALF, :]
    even = lax.broadcasted_iota(jnp.int32, real_even.shape, 1) < HALF
    table = jnp.concatenate(
        [
            jnp.where(even, real_even, -imag_even),
            jnp.where(even, -imag_odd, -real_odd),
            jnp.where(even, imag_even, real_even),
            jnp.where(even, real_odd, -imag_odd),
        ],
        axis=0,
    )
    high = table.astype(BF16).astype(F32)
    low = table - high
    pad = jnp.zeros((4 * HALF, table_ref.shape[1] - 6 * HALF), F32)
    table_ref[...] = jnp.concatenate([high, high, low, pad], axis=1).astype(BF16)


def place_of(flip):
    return ((flip >> 1) & 3) * 4 + ((flip >> 3) & 1) * 2 + (flip & 1)


def orbital_kernel(table_ref, pos_ref, out_ref, wave_ref, eight_ref, group_ref, chunk_ref, *, unroll, each):
    groups = out_ref.shape[0]
    chunks = out_ref.shape[1] // 2
    own = RUN // LANES
    runs = chunks // own
    upper = lax.axis_index("band") < lax.axis_size("band") // 2
    walk = lax.axis_index("walk")
    active = walk < each
    out_ref[...] = jnp.zeros_like(out_ref)

    def waves(group, length):
        away = place_of(group ^ walk)
        for line in range(0, 2 * chunks, 8):
            first = base_wave(pos_ref[away, line : line + 8, :])
            power = (jnp.ones((8, LANES), F32), jnp.zeros((8, LANES), F32))
            for k in range(8):
                for half in range(2):
                    wave_ref[half, group, pl.ds(line * 8 + k, 8, stride=8), :] = power[half]
                power = first if k == 0 else times(power, first)
            for half in range(2):
                eight_ref[half, group, line : line + 8, :] = power[half]
        numbers = pos_ref[away, 2 * chunks : 2 * chunks + runs, :].astype(jnp.int32)
        for run in range(runs):
            number = numbers[run, 0]
            low = jnp.where(upper, 0, number // LANES)
            high = jnp.where(upper, (number + LANES - 1) // LANES, own)
            high = jnp.where(active, high, low)

            def note(chunk, at):
                group_ref[at] = group
                chunk_ref[at] = run * own + chunk
                return at + 1

            length = lax.fori_loop(low, high, note, length)
        return length

    length = lax.fori_loop(0, groups, waves, 0)

    def basis(entry, axis):
        group, chunk = entry
        line = axis * chunks + chunk
        start = pl.multiple_of(line * 8, 8)
        now = tuple(wave_ref[half, group, pl.ds(start, 8), :] for half in range(2))
        step = tuple(jnp.broadcast_to(eight_ref[half, group, pl.ds(line, 1), :], (8, LANES)) for half in range(2))
        twice = 2.0 * step[0]
        last, now = now, times(now, step)
        cosines, sines = [last[0], now[0]], [last[1], now[1]]
        for _ in range(2, HALF // 8):
            last, now = now, tuple(twice * now[half] - last[half] for half in range(2))
            cosines.append(now[0])
            sines.append(now[1])
        return jnp.concatenate(cosines + sines, axis=0)

    zeros = jnp.zeros((table_ref.shape[1] - 6 * HALF, 2 * LANES), BF16)

    def evaluate(index, carry):
        for inner in range(unroll):
            places = [jnp.minimum((index * unroll + inner) * 2 + side, length - 1) for side in range(2)]
            entries = [(group_ref[place], chunk_ref[place]) for place in places]
            wave_y = jnp.concatenate([basis(entry, 1) for entry in entries], axis=1)
            high_y = wave_y.astype(BF16)
            low_y = (wave_y - high_y.astype(F32)).astype(BF16)
            weights = jnp.concatenate([high_y, low_y, high_y, zeros], axis=0)
            inside = jnp.dot(table_ref[...], weights, preferred_element_type=F32)
            wave_x = jnp.concatenate([basis(entry, 0) for entry in entries], axis=1)
            for half in range(2):
                value = jnp.sum(inside[half * 2 * HALF : (half + 1) * 2 * HALF, :] * wave_x, axis=0, keepdims=True)
                for side, (group, chunk) in enumerate(entries):
                    out_ref[group, pl.ds(half * chunks + chunk, 1), :] = value[:, side * LANES : (side + 1) * LANES]
        return carry

    lax.fori_loop(0, (length + 2 * unroll - 1) // (2 * unroll), evaluate, 0)


def gradient_kernel(target_ref, feature_ref, net_hbm, out_ref, net_ref, sem, *, scale):
    copy = pltpu.make_async_copy(net_hbm, net_ref, sem)
    copy.start()
    chunks = feature_ref.shape[0] // LANES
    slots = out_ref.shape[0] // 2
    upper = lax.axis_index("band") < lax.axis_size("band") // 2
    targets = [
        jnp.concatenate(
            [target_ref[pl.ds(half * chunks + chunk, slots, stride=2 * chunks), :] for chunk in range(chunks)], axis=1
        )
        for half in range(2)
    ]
    copy.wait()
    mine = net_ref[2 * slots : 2 * slots + 1, :] == jnp.where(upper, 1.0, 0.0)
    parts = []
    for half in range(2):
        scaled = (net_ref[half * slots : (half + 1) * slots, :] - targets[half]) * scale
        parts.append(jnp.where(mine, scaled, 0.0))
    spread = jnp.concatenate(parts, axis=0)
    total = jnp.zeros(out_ref.shape, F32)
    for piece in split3(spread):
        total = total + jnp.dot(piece, feature_ref[...], preferred_element_type=F32)
    out_ref[...] = total


def call(kernel, out, scratch=(), mebibytes=16, **more):
    return pl.pallas_call(
        kernel,
        out_shape=out,
        **more,
        scratch_shapes=list(scratch),
        interpret=INTERPRET,
        compiler_params=pltpu.CompilerParams(vmem_limit_bytes=mebibytes * 1024 * 1024),
    )


def local(positions, coefficients, lattice, spin_labels, occupied, features, orbital_head):
    walk_count = lax.axis_size("walk")
    band_count = lax.axis_size("band")
    band_index = lax.axis_index("band")
    devices = walk_count * band_count
    rows = coefficients.shape[1]
    count = positions.shape[1]
    orbitals = occupied.shape[0] * occupied.shape[1]
    each = orbitals // band_count

    chunks = count // LANES
    anywhere = pl.BlockSpec(memory_space=pltpu.HBM)
    labels = spin_labels.reshape(chunks, LANES)
    arrays = tuple(
        pltpu.with_memory_space_constraint(array, pltpu.HBM) for array in (coefficients, occupied, positions, labels)
    )
    picked, ordered, slot, up = call(
        start_kernel,
        (
            jax.ShapeDtypeStruct((devices * BLOCK, LANES), BF16),
            jax.ShapeDtypeStruct((2 * chunks + 8, LANES), F32),
            jax.ShapeDtypeStruct((count // RUN, RUN), F32),
            jax.ShapeDtypeStruct((1, count), F32),
        ),
        [
            pltpu.VMEM(coefficients.shape, BF16),
            pltpu.SMEM(occupied.shape, jnp.int32),
            pltpu.VMEM(positions.shape, F32),
            pltpu.VMEM(labels.shape, jnp.int32),
            pltpu.VMEM((devices * BLOCK, LANES), F32),
            pltpu.SemaphoreType.DMA((5,)),
        ],
        in_specs=[anywhere] * 4,
    )(*arrays)
    received = lax.all_to_all(picked.reshape(devices, BLOCK, LANES), ("walk", "band"), 0, 0, tiled=True)
    everyone = ordered[None]
    for flips in ((1,), (8,), (2, 4, 6)):
        moved = [lax.ppermute(everyone, "walk", [(k, k ^ flip) for k in range(walk_count)]) for flip in flips]
        everyone = jnp.concatenate([everyone, *moved], axis=0)
    table = call(
        fold_kernel, jax.ShapeDtypeStruct((4 * HALF, 512), BF16), [pltpu.VMEM((4 * HALF, 2 * HALF), F32)]
    )(received, lattice.reshape(2, walk_count, rows))
    values = call(
        functools.partial(orbital_kernel, unroll=8, each=each),
        jax.ShapeDtypeStruct((walk_count, 2 * chunks, LANES), F32),
        [
            pltpu.VMEM((2, walk_count, 16 * chunks, LANES), F32),
            pltpu.VMEM((2, walk_count, 2 * chunks, LANES), F32),
            pltpu.SMEM((walk_count * chunks,), jnp.int32),
            pltpu.SMEM((walk_count * chunks,), jnp.int32),
        ],
        mebibytes=24,
    )(table, everyone)
    target = lax.all_to_all(values, "walk", 0, 0, tiled=True).reshape(-1, LANES)

    spins = occupied.shape[0]
    per_spin = band_count // spins
    spin = band_index // per_spin
    columns = orbital_head.reshape(orbital_head.shape[0], spins, 2, per_spin, each)
    columns = lax.dynamic_index_in_dim(columns, spin, 1, keepdims=False)
    columns = lax.dynamic_index_in_dim(columns, band_index % per_spin, 2, keepdims=False)
    columns = jnp.transpose(columns, (1, 2, 0))
    columns = jnp.pad(columns, ((0, 0), (0, walk_count - each), (0, 0))).reshape(2 * walk_count, -1)
    sorted_features, net = call(
        sort_kernel,
        (jax.ShapeDtypeStruct(features.shape, BF16), jax.ShapeDtypeStruct((2 * walk_count + 8, count), F32)),
    )(slot, features, columns, up)
    net = pltpu.with_memory_space_constraint(net, pltpu.HBM)
    walkers = walk_count * count // orbitals
    hidden = features.shape[1]
    in_vmem = pl.BlockSpec(memory_space=pltpu.VMEM)
    own = call(
        functools.partial(gradient_kernel, scale=1.0 / walkers),
        jax.ShapeDtypeStruct((2 * walk_count, hidden), F32),
        [pltpu.VMEM(net.shape, F32), pltpu.SemaphoreType.DMA],
        in_specs=[in_vmem, in_vmem, anywhere],
    )(target, sorted_features, net)
    own = own.reshape(2, walk_count, hidden)[:, :each].reshape(-1, LANES)
    own = own + lax.ppermute(own, "walk", [(k, k ^ 1) for k in range(walk_count)])
    chips = walk_count // 2
    shares = lax.all_to_all(
        jnp.broadcast_to(own, (chips, *own.shape)),
        "walk",
        0,
        0,
        axis_index_groups=[[2 * chip + core for chip in range(chips)] for core in range(2)],
        tiled=True,
    )
    summed = jnp.sum(shares, axis=0)
    whole = lax.all_to_all(jnp.broadcast_to(summed, (band_count, *own.shape)), "band", 0, 0, tiled=True)
    whole = whole.reshape(spins, per_spin, 2, each, hidden)
    return jnp.transpose(whole, (4, 0, 2, 1, 3)).reshape(hidden, 2 * orbitals)


def solution(mesh):
    return jax.shard_map(
        local,
        mesh=mesh,
        in_specs=(
            P(None, "walk"),
            P(None, "walk", "band"),
            P(),
            P("walk"),
            P(),
            P("walk", None),
            P(),
        ),
        out_specs=P(),
        check_vma=False,
    )
```

```python
import functools

import jax
import jax.numpy as jnp
from jax import lax
from jax.experimental import pallas as pl
from jax.experimental.pallas import tpu as pltpu
from jax.sharding import PartitionSpec as P


INTERPRET = False
F32 = jnp.float32
BF16 = jnp.bfloat16
PI = 3.141592653589793
BLOCK = 24
RUN = 1024
HALF = 80
LANES = 128


def split3(value):
    high = value.astype(BF16)
    rest = value - high.astype(F32)
    middle = rest.astype(BF16)
    low = (rest - middle.astype(F32)).astype(BF16)
    return high, middle, low


def pick_kernel(coef_hbm, occ_hbm, out_ref, coef_ref, occ_ref, stage_ref, sems):
    copies = [pltpu.make_async_copy(occ_hbm, occ_ref, sems.at[2])]
    copies += [pltpu.make_async_copy(coef_hbm.at[part], coef_ref.at[part], sems.at[part]) for part in range(2)]
    for copy in copies:
        copy.start()
    _, rows, bands = coef_ref.shape
    spins, per_spin = occ_ref.shape
    devices = stage_ref.shape[0] // BLOCK
    senders = lax.axis_size("band")
    each = spins * per_spin // senders
    tiles = rows // LANES
    base = lax.axis_index("band") * bands
    for row in range(2 * tiles, BLOCK):
        stage_ref[pl.ds(row, devices, stride=BLOCK), :] = jnp.zeros((devices, LANES), F32)
    line = lax.broadcasted_iota(jnp.int32, (8, bands), 0)
    lane = lax.broadcasted_iota(jnp.int32, (8, bands), 1) + base
    copies[0].wait()
    picks = []
    core = lax.axis_index("walk") % 2
    for first in range(0, devices, 8):
        wanted = jnp.full((8, bands), -1, jnp.int32)
        for block in range(first, first + 8):
            chip, other = block // 2, block % 2
            pair, sender = chip // senders, chip % senders
            if 2 * pair < each:
                orbital = sender * each + 2 * pair + (core ^ other)
                spin = sender * each // per_spin
                wanted = jnp.where(line == block - first, occ_ref[spin, orbital - spin * per_spin], wanted)
        picks.append(jnp.where(lane == wanted, 1.0, 0.0))
    pick = jnp.concatenate(picks, axis=0).astype(BF16)
    for part in range(2):
        copies[1 + part].wait()
        taken = lax.dot_general(
            pick, coef_ref[part], (((1,), (1,)), ((), ())), preferred_element_type=F32
        )
        for tile in range(tiles):
            stage_ref[pl.ds(part * tiles + tile, devices, stride=BLOCK), :] = taken[:, tile * LANES : (tile + 1) * LANES]
    out_ref[...] = stage_ref[...].astype(BF16)


def order_kernel(pos_ref, label_ref, out_ref, slot_ref, up_ref):
    chunks = label_ref.shape[0]
    own = RUN // LANES
    runs = chunks // own
    up = label_ref[...] == 0
    ones = jnp.where(up, 1.0, 0.0)
    row = lax.broadcasted_iota(jnp.int32, (LANES, LANES), 0)
    column = lax.broadcasted_iota(jnp.int32, (LANES, LANES), 1)
    until = jnp.where(row <= column, 1.0, 0.0).astype(BF16)
    inside = jnp.dot(ones.astype(BF16), until, preferred_element_type=F32)
    whole = jnp.broadcast_to(inside[:, LANES - 1 : LANES], inside.shape).astype(BF16)
    row = lax.broadcasted_iota(jnp.int32, (chunks, chunks), 0)
    column = lax.broadcasted_iota(jnp.int32, (chunks, chunks), 1)
    same = jnp.where(row // own == column // own, 1.0, 0.0)
    before = jnp.where(column < row, same, 0.0).astype(BF16)
    rank = inside + jnp.dot(before, whole, preferred_element_type=F32)
    total = jnp.dot(same.astype(BF16), whole, preferred_element_type=F32)
    place = (
        lax.broadcasted_iota(jnp.int32, rank.shape, 0) % own * LANES + lax.broadcasted_iota(jnp.int32, rank.shape, 1)
    ).astype(F32)
    slot = jnp.where(up, rank - 1.0, total + place - rank)
    first = jnp.where(place < total, 1.0, 0.0)
    up_ref[...] = jnp.concatenate([first[chunk : chunk + 1, :] for chunk in range(chunks)], axis=1)
    parts = jnp.concatenate([part.astype(F32) for part in split3(pos_ref[...])], axis=0).astype(BF16)
    here = lax.broadcasted_iota(jnp.int32, (RUN, RUN), 0).astype(F32)
    for run in range(runs):
        line = jnp.concatenate([slot[run * own + k : run * own + k + 1, :] for k in range(own)], axis=1)
        slot_ref[run : run + 1, :] = line
        move = jnp.where(here == line, 1.0, 0.0).astype(BF16)
        moved = lax.dot_general(
            parts[:, run * RUN : (run + 1) * RUN], move, (((1,), (1,)), ((), ())), preferred_element_type=F32
        )
        moved = moved[0:2] + moved[2:4] + moved[4:6]
        for axis in range(2):
            for k in range(own):
                at = axis * chunks + run * own + k
                out_ref[at : at + 1, :] = moved[axis : axis + 1, k * LANES : (k + 1) * LANES]
        out_ref[2 * chunks + run : 2 * chunks + run + 1, :] = total[run * own : run * own + 1, :]
    out_ref[2 * chunks + runs :, :] = jnp.zeros((out_ref.shape[0] - 2 * chunks - runs, LANES), F32)


def sort_kernel(slot_ref, feature_ref, head_ref, up_ref, out_ref, net_ref):
    here = lax.broadcasted_iota(jnp.int32, (RUN, RUN), 0).astype(F32)
    for run in range(slot_ref.shape[0]):
        move = jnp.where(here == slot_ref[run : run + 1, :], 1.0, 0.0).astype(BF16)
        moved = jnp.dot(move, feature_ref[run * RUN : (run + 1) * RUN, :], preferred_element_type=F32).astype(BF16)
        out_ref[run * RUN : (run + 1) * RUN, :] = moved
        net_ref[: head_ref.shape[0], run * RUN : (run + 1) * RUN] = lax.dot_general(
            head_ref[...], moved, (((1,), (1,)), ((), ())), preferred_element_type=F32
        )
    tail = net_ref.shape[0] - head_ref.shape[0]
    net_ref[head_ref.shape[0] :, :] = jnp.broadcast_to(up_ref[...], (tail, up_ref.shape[1]))


def base_wave(turns):
    quarter = (turns - 0.5) * (0.5 * PI)
    square = quarter * quarter
    sine = quarter * (
        1.0 + square * (-1 / 6 + square * (1 / 120 + square * (-1 / 5040 + square * (1 / 362880))))
    )
    cosine = 1.0 + square * (
        -1 / 2 + square * (1 / 24 + square * (-1 / 720 + square * (1 / 40320 - square * (1 / 3628800))))
    )
    sine, cosine = 2.0 * sine * cosine, 1.0 - 2.0 * sine * sine
    sine, cosine = 2.0 * sine * cosine, 1.0 - 2.0 * sine * sine
    return -cosine, -sine


def times(left, right):
    return left[0] * right[0] - left[1] * right[1], left[1] * right[0] + left[0] * right[1]


def fold_kernel(recv_ref, lat_ref, past_ref, *refs, other):
    sum_ref = refs[-1]
    senders = lax.axis_size("band")
    halves = recv_ref.shape[0] // senders
    core = (lax.axis_index("walk") % 2) ^ other
    rows = lat_ref.shape[2]
    tiles = rows // LANES

    sum_ref[...] = past_ref[...] if other else jnp.zeros_like(sum_ref)
    frequency = lax.broadcasted_iota(jnp.int32, (HALF, rows), 0)

    def fold(half, carry):
        group = 2 * half + core
        both = recv_ref[half * senders, :BLOCK, :].astype(F32)
        for sender in range(1, senders):
            both = both + recv_ref[half * senders + sender, :BLOCK, :].astype(F32)
        c_real, c_imag = (jnp.concatenate([both[k + t : k + t + 1] for t in range(tiles)], axis=1) for k in (0, tiles))
        lat_a = lat_ref[0, pl.ds(group, 1), :]
        lat_b = lat_ref[1, pl.ds(group, 1), :]
        sign_a = jnp.where(lat_a < 0, -1.0, 1.0)
        sign_b = jnp.where(lat_b < 0, -1.0, 1.0)
        at_a = frequency == jnp.abs(lat_a)
        at_b = frequency == jnp.abs(lat_b)
        zero = jnp.zeros((), F32)
        left = jnp.concatenate(
            [
                jnp.where(at_a, value, zero).astype(BF16)
                for value in (c_real, c_real * sign_a, c_imag, c_imag * sign_a)
            ],
            axis=0,
        )
        right = jnp.concatenate(
            [jnp.where(at_b, value, zero).astype(BF16) for value in (jnp.ones_like(sign_b), sign_b)], axis=0
        )
        sum_ref[...] += lax.dot_general(left, right, (((1,), (1,)), ((), ())), preferred_element_type=F32)
        return carry

    lax.fori_loop(0, halves, fold, 0, unroll=4)
    if not other:
        return
    table_ref = refs[0]
    real_even = sum_ref[0:HALF, :]
    real_odd = sum_ref[HALF : 2 * HALF, :]
    imag_even = sum_ref[2 * HALF : 3 * HALF, :]
    imag_odd = sum_ref[3 * HALF : 4 * HALF, :]
    even = lax.broadcasted_iota(jnp.int32, real_even.shape, 1) < HALF
    table = jnp.concatenate(
        [
            jnp.where(even, real_even, -imag_even),
            jnp.where(even, -imag_odd, -real_odd),
            jnp.where(even, imag_even, real_even),
            jnp.where(even, real_odd, -imag_odd),
        ],
        axis=0,
    )
    high = table.astype(BF16).astype(F32)
    low = table - high
    pad = jnp.zeros((4 * HALF, table_ref.shape[1] - 6 * HALF), F32)
    table_ref[...] = jnp.concatenate([high, high, low, pad], axis=1).astype(BF16)


def orbital_kernel(table_ref, pos_ref, out_ref, wave_ref, eight_ref, group_ref, chunk_ref, *, unroll, each):
    groups = out_ref.shape[0]
    chunks = out_ref.shape[1] // 2
    own = RUN // LANES
    runs = chunks // own
    upper = lax.axis_index("band") < lax.axis_size("band") // 2
    walk = lax.axis_index("walk")
    active = walk < each
    out_ref[...] = jnp.zeros_like(out_ref)

    def waves(group, length):
        away = group ^ walk
        for line in range(0, 2 * chunks, 8):
            first = base_wave(pos_ref[away, line : line + 8, :])
            power = (jnp.ones((8, LANES), F32), jnp.zeros((8, LANES), F32))
            for k in range(8):
                for half in range(2):
                    wave_ref[half, group, pl.ds(line * 8 + k, 8, stride=8), :] = power[half]
                power = first if k == 0 else times(power, first)
            for half in range(2):
                eight_ref[half, group, line : line + 8, :] = power[half]
        numbers = pos_ref[away, 2 * chunks : 2 * chunks + runs, :].astype(jnp.int32)
        for run in range(runs):
            number = numbers[run, 0]
            low = jnp.where(upper, 0, number // LANES)
            high = jnp.where(upper, (number + LANES - 1) // LANES, own)
            high = jnp.where(active, high, low)

            def note(chunk, at):
                group_ref[at] = group
                chunk_ref[at] = run * own + chunk
                return at + 1

            length = lax.fori_loop(low, high, note, length)
        return length

    length = lax.fori_loop(0, groups, waves, 0)

    def basis(entry, axis):
        group, chunk = entry
        line = axis * chunks + chunk
        start = pl.multiple_of(line * 8, 8)
        now = tuple(wave_ref[half, group, pl.ds(start, 8), :] for half in range(2))
        step = tuple(jnp.broadcast_to(eight_ref[half, group, pl.ds(line, 1), :], (8, LANES)) for half in range(2))
        twice = 2.0 * step[0]
        last, now = now, times(now, step)
        cosines, sines = [last[0], now[0]], [last[1], now[1]]
        for _ in range(2, HALF // 8):
            last, now = now, tuple(twice * now[half] - last[half] for half in range(2))
            cosines.append(now[0])
            sines.append(now[1])
        return jnp.concatenate(cosines + sines, axis=0)

    zeros = jnp.zeros((table_ref.shape[1] - 6 * HALF, 2 * LANES), BF16)

    def evaluate(index, carry):
        for inner in range(unroll):
            places = [jnp.minimum((index * unroll + inner) * 2 + side, length - 1) for side in range(2)]
            entries = [(group_ref[place], chunk_ref[place]) for place in places]
            wave_y = jnp.concatenate([basis(entry, 1) for entry in entries], axis=1)
            high_y = wave_y.astype(BF16)
            low_y = (wave_y - high_y.astype(F32)).astype(BF16)
            weights = jnp.concatenate([high_y, low_y, high_y, zeros], axis=0)
            inside = jnp.dot(table_ref[...], weights, preferred_element_type=F32)
            wave_x = jnp.concatenate([basis(entry, 0) for entry in entries], axis=1)
            for half in range(2):
                value = jnp.sum(inside[half * 2 * HALF : (half + 1) * 2 * HALF, :] * wave_x, axis=0, keepdims=True)
                for side, (group, chunk) in enumerate(entries):
                    out_ref[group, pl.ds(half * chunks + chunk, 1), :] = value[:, side * LANES : (side + 1) * LANES]
        return carry

    lax.fori_loop(0, (length + 2 * unroll - 1) // (2 * unroll), evaluate, 0)


def gradient_kernel(target_ref, feature_ref, net_hbm, out_ref, net_ref, sem, *, scale):
    copy = pltpu.make_async_copy(net_hbm, net_ref, sem)
    copy.start()
    chunks = feature_ref.shape[0] // LANES
    slots = out_ref.shape[0] // 2
    upper = lax.axis_index("band") < lax.axis_size("band") // 2
    targets = [
        jnp.concatenate(
            [target_ref[pl.ds(half * chunks + chunk, slots, stride=2 * chunks), :] for chunk in range(chunks)], axis=1
        )
        for half in range(2)
    ]
    copy.wait()
    mine = net_ref[2 * slots : 2 * slots + 1, :] == jnp.where(upper, 1.0, 0.0)
    parts = []
    for half in range(2):
        scaled = (net_ref[half * slots : (half + 1) * slots, :] - targets[half]) * scale
        parts.append(jnp.where(mine, scaled, 0.0))
    spread = jnp.concatenate(parts, axis=0)
    total = jnp.zeros(out_ref.shape, F32)
    for piece in split3(spread):
        total = total + jnp.dot(piece, feature_ref[...], preferred_element_type=F32)
    out_ref[...] = total


def call(kernel, out, scratch=(), mebibytes=16, **more):
    return pl.pallas_call(
        kernel,
        out_shape=out,
        **more,
        scratch_shapes=list(scratch),
        interpret=INTERPRET,
        compiler_params=pltpu.CompilerParams(vmem_limit_bytes=mebibytes * 1024 * 1024),
    )


def local(positions, coefficients, lattice, spin_labels, occupied, features, orbital_head):
    walk_count = lax.axis_size("walk")
    band_count = lax.axis_size("band")
    band_index = lax.axis_index("band")
    devices = walk_count * band_count
    rows = coefficients.shape[1]
    count = positions.shape[1]
    orbitals = occupied.shape[0] * occupied.shape[1]
    each = orbitals // band_count

    chunks = count // LANES
    anywhere = pl.BlockSpec(memory_space=pltpu.HBM)
    picked = call(
        pick_kernel,
        jax.ShapeDtypeStruct((devices * BLOCK, LANES), BF16),
        [
            pltpu.VMEM(coefficients.shape, BF16),
            pltpu.SMEM(occupied.shape, jnp.int32),
            pltpu.VMEM((devices * BLOCK, LANES), F32),
            pltpu.SemaphoreType.DMA((3,)),
        ],
        in_specs=[anywhere, anywhere],
    )(pltpu.with_memory_space_constraint(coefficients, pltpu.HBM), pltpu.with_memory_space_constraint(occupied, pltpu.HBM))
    picked, positions = lax.optimization_barrier((picked, positions))
    chips = walk_count // 2
    same_core = [
        [(2 * pair + core) * band_count + band for pair in range(chips) for band in range(band_count)] for core in range(2)
    ]
    received = lax.all_to_all(
        picked.reshape(devices // 2, 2 * BLOCK, LANES), ("walk", "band"), 0, 0, axis_index_groups=same_core, tiled=True
    )
    swapped = lax.ppermute(received[:, BLOCK:, :], "walk", [(k, k ^ 1) for k in range(walk_count)])
    ordered, slot, up = call(
        order_kernel,
        (
            jax.ShapeDtypeStruct((2 * chunks + 8, LANES), F32),
            jax.ShapeDtypeStruct((count // RUN, RUN), F32),
            jax.ShapeDtypeStruct((1, count), F32),
        ),
    )(positions, spin_labels.reshape(chunks, LANES))
    everyone = ordered[None]
    for flips in ((1,), (2, 4, 6), (8,)):
        moved = [lax.ppermute(everyone, "walk", [(k, k ^ flip) for k in range(walk_count)]) for flip in flips]
        everyone = jnp.concatenate([everyone, *moved], axis=0)
    waves = lattice.reshape(2, walk_count, rows)
    sums = jax.ShapeDtypeStruct((4 * HALF, 2 * HALF), F32)
    past = call(functools.partial(fold_kernel, other=0), sums)(received, waves, jnp.zeros((8, LANES), F32))
    table = call(
        functools.partial(fold_kernel, other=1),
        jax.ShapeDtypeStruct((4 * HALF, 512), BF16),
        [pltpu.VMEM(sums.shape, F32)],
    )(swapped, waves, past)
    values = call(
        functools.partial(orbital_kernel, unroll=8, each=each),
        jax.ShapeDtypeStruct((walk_count, 2 * chunks, LANES), F32),
        [
            pltpu.VMEM((2, walk_count, 16 * chunks, LANES), F32),
            pltpu.VMEM((2, walk_count, 2 * chunks, LANES), F32),
            pltpu.SMEM((walk_count * chunks,), jnp.int32),
            pltpu.SMEM((walk_count * chunks,), jnp.int32),
        ],
        mebibytes=24,
    )(table, everyone)
    target = lax.all_to_all(values, "walk", 0, 0, tiled=True).reshape(-1, LANES)

    spins = occupied.shape[0]
    per_spin = band_count // spins
    spin = band_index // per_spin
    columns = orbital_head.reshape(orbital_head.shape[0], spins, 2, per_spin, each)
    columns = lax.dynamic_index_in_dim(columns, spin, 1, keepdims=False)
    columns = lax.dynamic_index_in_dim(columns, band_index % per_spin, 2, keepdims=False)
    columns = jnp.transpose(columns, (1, 2, 0))
    columns = jnp.pad(columns, ((0, 0), (0, walk_count - each), (0, 0))).reshape(2 * walk_count, -1)
    sorted_features, net = call(
        sort_kernel,
        (jax.ShapeDtypeStruct(features.shape, BF16), jax.ShapeDtypeStruct((2 * walk_count + 8, count), F32)),
    )(slot, features, columns, up)
    net = pltpu.with_memory_space_constraint(net, pltpu.HBM)
    walkers = walk_count * count // orbitals
    hidden = features.shape[1]
    in_vmem = pl.BlockSpec(memory_space=pltpu.VMEM)
    own = call(
        functools.partial(gradient_kernel, scale=1.0 / walkers),
        jax.ShapeDtypeStruct((2 * walk_count, hidden), F32),
        [pltpu.VMEM(net.shape, F32), pltpu.SemaphoreType.DMA],
        in_specs=[in_vmem, in_vmem, anywhere],
    )(target, sorted_features, net)
    own = own.reshape(2, walk_count, hidden)[:, :each].reshape(-1, LANES)
    own = own + lax.ppermute(own, "walk", [(k, k ^ 1) for k in range(walk_count)])
    shares = lax.all_to_all(
        jnp.broadcast_to(own, (chips, *own.shape)),
        "walk",
        0,
        0,
        axis_index_groups=[[2 * chip + core for chip in range(chips)] for core in range(2)],
        tiled=True,
    )
    summed = jnp.sum(shares, axis=0)
    whole = lax.all_to_all(jnp.broadcast_to(summed, (band_count, *own.shape)), "band", 0, 0, tiled=True)
    whole = whole.reshape(spins, per_spin, 2, each, hidden)
    return jnp.transpose(whole, (4, 0, 2, 1, 3)).reshape(hidden, 2 * orbitals)


def solution(mesh):
    return jax.shard_map(
        local,
        mesh=mesh,
        in_specs=(
            P(None, "walk"),
            P(None, "walk", "band"),
            P(),
            P("walk"),
            P(),
            P("walk", None),
            P(),
        ),
        out_specs=P(),
        check_vma=False,
    )
```

```python
import functools

import jax
import jax.numpy as jnp
from jax import lax
from jax.experimental import pallas as pl
from jax.experimental.pallas import tpu as pltpu
from jax.sharding import PartitionSpec as P


INTERPRET = False
F32 = jnp.float32
BF16 = jnp.bfloat16
PI = 3.141592653589793
BLOCK = 24
RUN = 1024
HALF = 80
LANES = 128


def split3(value):
    high = value.astype(BF16)
    rest = value - high.astype(F32)
    middle = rest.astype(BF16)
    low = (rest - middle.astype(F32)).astype(BF16)
    return high, middle, low


def pick_kernel(coef_hbm, occ_hbm, out_ref, coef_ref, occ_ref, stage_ref, sems):
    copies = [pltpu.make_async_copy(occ_hbm, occ_ref, sems.at[2])]
    copies += [pltpu.make_async_copy(coef_hbm.at[part], coef_ref.at[part], sems.at[part]) for part in range(2)]
    for copy in copies:
        copy.start()
    _, rows, bands = coef_ref.shape
    spins, per_spin = occ_ref.shape
    devices = stage_ref.shape[0] // BLOCK
    senders = lax.axis_size("band")
    each = spins * per_spin // senders
    tiles = rows // LANES
    base = lax.axis_index("band") * bands
    for row in range(2 * tiles, BLOCK):
        stage_ref[pl.ds(row, devices, stride=BLOCK), :] = jnp.zeros((devices, LANES), F32)
    line = lax.broadcasted_iota(jnp.int32, (8, bands), 0)
    lane = lax.broadcasted_iota(jnp.int32, (8, bands), 1) + base
    copies[0].wait()
    picks = []
    for group in range(devices // senders):
        wanted = jnp.full((8, bands), -1, jnp.int32)
        if group < each:
            for sender in range(senders):
                orbital = sender * each + group
                wanted = jnp.where(line == sender, occ_ref[orbital // per_spin, orbital % per_spin], wanted)
        picks.append(jnp.where(lane == wanted, 1.0, 0.0))
    pick = jnp.concatenate(picks, axis=0).astype(BF16)
    for part in range(2):
        copies[1 + part].wait()
        taken = lax.dot_general(
            pick, coef_ref[part], (((1,), (1,)), ((), ())), preferred_element_type=F32
        )
        for tile in range(tiles):
            stage_ref[pl.ds(part * tiles + tile, devices, stride=BLOCK), :] = taken[:, tile * LANES : (tile + 1) * LANES]
    out_ref[...] = stage_ref[...].astype(BF16)


def order_kernel(pos_ref, label_ref, out_ref, slot_ref, up_ref):
    chunks = label_ref.shape[0]
    own = RUN // LANES
    runs = chunks // own
    up = label_ref[...] == 0
    ones = jnp.where(up, 1.0, 0.0)
    row = lax.broadcasted_iota(jnp.int32, (LANES, LANES), 0)
    column = lax.broadcasted_iota(jnp.int32, (LANES, LANES), 1)
    until = jnp.where(row <= column, 1.0, 0.0).astype(BF16)
    inside = jnp.dot(ones.astype(BF16), until, preferred_element_type=F32)
    whole = jnp.broadcast_to(inside[:, LANES - 1 : LANES], inside.shape).astype(BF16)
    row = lax.broadcasted_iota(jnp.int32, (chunks, chunks), 0)
    column = lax.broadcasted_iota(jnp.int32, (chunks, chunks), 1)
    same = jnp.where(row // own == column // own, 1.0, 0.0)
    before = jnp.where(column < row, same, 0.0).astype(BF16)
    rank = inside + jnp.dot(before, whole, preferred_element_type=F32)
    total = jnp.dot(same.astype(BF16), whole, preferred_element_type=F32)
    place = (
        lax.broadcasted_iota(jnp.int32, rank.shape, 0) % own * LANES + lax.broadcasted_iota(jnp.int32, rank.shape, 1)
    ).astype(F32)
    slot = jnp.where(up, rank - 1.0, total + place - rank)
    first = jnp.where(place < total, 1.0, 0.0)
    up_ref[...] = jnp.concatenate([first[chunk : chunk + 1, :] for chunk in range(chunks)], axis=1)
    parts = jnp.concatenate([part.astype(F32) for part in split3(pos_ref[...])], axis=0).astype(BF16)
    here = lax.broadcasted_iota(jnp.int32, (RUN, RUN), 0).astype(F32)
    for run in range(runs):
        line = jnp.concatenate([slot[run * own + k : run * own + k + 1, :] for k in range(own)], axis=1)
        slot_ref[run : run + 1, :] = line
        move = jnp.where(here == line, 1.0, 0.0).astype(BF16)
        moved = lax.dot_general(
            parts[:, run * RUN : (run + 1) * RUN], move, (((1,), (1,)), ((), ())), preferred_element_type=F32
        )
        moved = moved[0:2] + moved[2:4] + moved[4:6]
        for axis in range(2):
            for k in range(own):
                at = axis * chunks + run * own + k
                out_ref[at : at + 1, :] = moved[axis : axis + 1, k * LANES : (k + 1) * LANES]
        out_ref[2 * chunks + run : 2 * chunks + run + 1, :] = total[run * own : run * own + 1, :]
    out_ref[2 * chunks + runs :, :] = jnp.zeros((out_ref.shape[0] - 2 * chunks - runs, LANES), F32)


def sort_kernel(slot_ref, feature_ref, head_ref, up_ref, out_ref, net_ref):
    here = lax.broadcasted_iota(jnp.int32, (RUN, RUN), 0).astype(F32)
    for run in range(slot_ref.shape[0]):
        move = jnp.where(here == slot_ref[run : run + 1, :], 1.0, 0.0).astype(BF16)
        moved = jnp.dot(move, feature_ref[run * RUN : (run + 1) * RUN, :], preferred_element_type=F32).astype(BF16)
        out_ref[run * RUN : (run + 1) * RUN, :] = moved
        net_ref[: head_ref.shape[0], run * RUN : (run + 1) * RUN] = lax.dot_general(
            head_ref[...], moved, (((1,), (1,)), ((), ())), preferred_element_type=F32
        )
    tail = net_ref.shape[0] - head_ref.shape[0]
    net_ref[head_ref.shape[0] :, :] = jnp.broadcast_to(up_ref[...], (tail, up_ref.shape[1]))


def base_wave(turns):
    quarter = (turns - 0.5) * (0.5 * PI)
    square = quarter * quarter
    sine = quarter * (
        1.0 + square * (-1 / 6 + square * (1 / 120 + square * (-1 / 5040 + square * (1 / 362880))))
    )
    cosine = 1.0 + square * (
        -1 / 2 + square * (1 / 24 + square * (-1 / 720 + square * (1 / 40320 - square * (1 / 3628800))))
    )
    sine, cosine = 2.0 * sine * cosine, 1.0 - 2.0 * sine * sine
    sine, cosine = 2.0 * sine * cosine, 1.0 - 2.0 * sine * sine
    return -cosine, -sine


def times(left, right):
    return left[0] * right[0] - left[1] * right[1], left[1] * right[0] + left[0] * right[1]


def fold_kernel(recv_ref, lat_ref, table_ref, sum_ref):
    groups = lat_ref.shape[1]
    senders = recv_ref.shape[0] // groups
    rows = lat_ref.shape[2]
    tiles = rows // LANES

    sum_ref[...] = jnp.zeros_like(sum_ref)
    frequency = lax.broadcasted_iota(jnp.int32, (HALF, rows), 0)

    def fold(group, carry):
        both = recv_ref[group * senders].astype(F32)
        for sender in range(1, senders):
            both = both + recv_ref[group * senders + sender].astype(F32)
        c_real, c_imag = (jnp.concatenate([both[k + t : k + t + 1] for t in range(tiles)], axis=1) for k in (0, tiles))
        lat_a = lat_ref[0, pl.ds(group, 1), :]
        lat_b = lat_ref[1, pl.ds(group, 1), :]
        sign_a = jnp.where(lat_a < 0, -1.0, 1.0)
        sign_b = jnp.where(lat_b < 0, -1.0, 1.0)
        at_a = frequency == jnp.abs(lat_a)
        at_b = frequency == jnp.abs(lat_b)
        zero = jnp.zeros((), F32)
        left = jnp.concatenate(
            [
                jnp.where(at_a, value, zero).astype(BF16)
                for value in (c_real, c_real * sign_a, c_imag, c_imag * sign_a)
            ],
            axis=0,
        )
        right = jnp.concatenate(
            [jnp.where(at_b, value, zero).astype(BF16) for value in (jnp.ones_like(sign_b), sign_b)], axis=0
        )
        sum_ref[...] += lax.dot_general(left, right, (((1,), (1,)), ((), ())), preferred_element_type=F32)
        return carry

    lax.fori_loop(0, groups, fold, 0, unroll=4)
    real_even = sum_ref[0:HALF, :]
    real_odd = sum_ref[HALF : 2 * HALF, :]
    imag_even = sum_ref[2 * HALF : 3 * HALF, :]
    imag_odd = sum_ref[3 * HALF : 4 * HALF, :]
    even = lax.broadcasted_iota(jnp.int32, real_even.shape, 1) < HALF
    table = jnp.concatenate(
        [
            jnp.where(even, real_even, -imag_even),
            jnp.where(even, -imag_odd, -real_odd),
            jnp.where(even, imag_even, real_even),
            jnp.where(even, real_odd, -imag_odd),
        ],
        axis=0,
    )
    high = table.astype(BF16).astype(F32)
    low = table - high
    pad = jnp.zeros((4 * HALF, table_ref.shape[1] - 6 * HALF), F32)
    table_ref[...] = jnp.concatenate([high, high, low, pad], axis=1).astype(BF16)


def orbital_kernel(table_ref, pos_ref, out_ref, wave_ref, eight_ref, group_ref, chunk_ref, *, unroll, each):
    groups = out_ref.shape[0]
    chunks = out_ref.shape[1] // 2
    own = RUN // LANES
    runs = chunks // own
    upper = lax.axis_index("band") < lax.axis_size("band") // 2
    walk = lax.axis_index("walk")
    active = walk < each
    out_ref[...] = jnp.zeros_like(out_ref)

    def waves(group, length):
        away = group ^ walk
        for line in range(0, 2 * chunks, 8):
            first = base_wave(pos_ref[away, line : line + 8, :])
            power = (jnp.ones((8, LANES), F32), jnp.zeros((8, LANES), F32))
            for k in range(8):
                for half in range(2):
                    wave_ref[half, group, pl.ds(line * 8 + k, 8, stride=8), :] = power[half]
                power = first if k == 0 else times(power, first)
            for half in range(2):
                eight_ref[half, group, line : line + 8, :] = power[half]
        numbers = pos_ref[away, 2 * chunks : 2 * chunks + runs, :].astype(jnp.int32)
        for run in range(runs):
            number = numbers[run, 0]
            low = jnp.where(upper, 0, number // LANES)
            high = jnp.where(upper, (number + LANES - 1) // LANES, own)
            high = jnp.where(active, high, low)

            def note(chunk, at):
                group_ref[at] = group
                chunk_ref[at] = run * own + chunk
                return at + 1

            length = lax.fori_loop(low, high, note, length)
        return length

    length = lax.fori_loop(0, groups, waves, 0)

    def basis(entry, axis):
        group, chunk = entry
        line = axis * chunks + chunk
        start = pl.multiple_of(line * 8, 8)
        now = tuple(wave_ref[half, group, pl.ds(start, 8), :] for half in range(2))
        step = tuple(jnp.broadcast_to(eight_ref[half, group, pl.ds(line, 1), :], (8, LANES)) for half in range(2))
        twice = 2.0 * step[0]
        last, now = now, times(now, step)
        cosines, sines = [last[0], now[0]], [last[1], now[1]]
        for _ in range(2, HALF // 8):
            last, now = now, tuple(twice * now[half] - last[half] for half in range(2))
            cosines.append(now[0])
            sines.append(now[1])
        return jnp.concatenate(cosines + sines, axis=0)

    zeros = jnp.zeros((table_ref.shape[1] - 6 * HALF, 2 * LANES), BF16)

    def evaluate(index, carry):
        for inner in range(unroll):
            places = [jnp.minimum((index * unroll + inner) * 2 + side, length - 1) for side in range(2)]
            entries = [(group_ref[place], chunk_ref[place]) for place in places]
            wave_y = jnp.concatenate([basis(entry, 1) for entry in entries], axis=1)
            high_y = wave_y.astype(BF16)
            low_y = (wave_y - high_y.astype(F32)).astype(BF16)
            weights = jnp.concatenate([high_y, low_y, high_y, zeros], axis=0)
            inside = jnp.dot(table_ref[...], weights, preferred_element_type=F32)
            wave_x = jnp.concatenate([basis(entry, 0) for entry in entries], axis=1)
            for half in range(2):
                value = jnp.sum(inside[half * 2 * HALF : (half + 1) * 2 * HALF, :] * wave_x, axis=0, keepdims=True)
                for side, (group, chunk) in enumerate(entries):
                    out_ref[group, pl.ds(half * chunks + chunk, 1), :] = value[:, side * LANES : (side + 1) * LANES]
        return carry

    lax.fori_loop(0, (length + 2 * unroll - 1) // (2 * unroll), evaluate, 0)


def gradient_kernel(target_ref, feature_ref, net_hbm, out_ref, net_ref, sem, *, scale):
    copy = pltpu.make_async_copy(net_hbm, net_ref, sem)
    copy.start()
    chunks = feature_ref.shape[0] // LANES
    slots = out_ref.shape[0] // 2
    upper = lax.axis_index("band") < lax.axis_size("band") // 2
    targets = [
        jnp.concatenate(
            [target_ref[pl.ds(half * chunks + chunk, slots, stride=2 * chunks), :] for chunk in range(chunks)], axis=1
        )
        for half in range(2)
    ]
    copy.wait()
    mine = net_ref[2 * slots : 2 * slots + 1, :] == jnp.where(upper, 1.0, 0.0)
    parts = []
    for half in range(2):
        scaled = (net_ref[half * slots : (half + 1) * slots, :] - targets[half]) * scale
        parts.append(jnp.where(mine, scaled, 0.0))
    spread = jnp.concatenate(parts, axis=0)
    total = jnp.zeros(out_ref.shape, F32)
    for piece in split3(spread):
        total = total + jnp.dot(piece, feature_ref[...], preferred_element_type=F32)
    out_ref[...] = total


def call(kernel, out, scratch=(), mebibytes=16, **more):
    return pl.pallas_call(
        kernel,
        out_shape=out,
        **more,
        scratch_shapes=list(scratch),
        interpret=INTERPRET,
        compiler_params=pltpu.CompilerParams(vmem_limit_bytes=mebibytes * 1024 * 1024),
    )


def local(positions, coefficients, lattice, spin_labels, occupied, features, orbital_head):
    walk_count = lax.axis_size("walk")
    band_count = lax.axis_size("band")
    band_index = lax.axis_index("band")
    devices = walk_count * band_count
    rows = coefficients.shape[1]
    count = positions.shape[1]
    orbitals = occupied.shape[0] * occupied.shape[1]
    each = orbitals // band_count

    chunks = count // LANES
    anywhere = pl.BlockSpec(memory_space=pltpu.HBM)
    picked = call(
        pick_kernel,
        jax.ShapeDtypeStruct((devices * BLOCK, LANES), BF16),
        [
            pltpu.VMEM(coefficients.shape, BF16),
            pltpu.SMEM(occupied.shape, jnp.int32),
            pltpu.VMEM((devices * BLOCK, LANES), F32),
            pltpu.SemaphoreType.DMA((3,)),
        ],
        in_specs=[anywhere, anywhere],
    )(pltpu.with_memory_space_constraint(coefficients, pltpu.HBM), pltpu.with_memory_space_constraint(occupied, pltpu.HBM))
    picked, positions = lax.optimization_barrier((picked, positions))
    received = lax.all_to_all(picked.reshape(devices, BLOCK, LANES), ("walk", "band"), 0, 0, tiled=True)
    ordered, slot, up = call(
        order_kernel,
        (
            jax.ShapeDtypeStruct((2 * chunks + 8, LANES), F32),
            jax.ShapeDtypeStruct((count // RUN, RUN), F32),
            jax.ShapeDtypeStruct((1, count), F32),
        ),
    )(positions, spin_labels.reshape(chunks, LANES))
    everyone = ordered[None]
    for flips in ((1,), tuple(range(2, walk_count, 2))):
        moved = [lax.ppermute(everyone, "walk", [(k, k ^ flip) for k in range(walk_count)]) for flip in flips]
        everyone = jnp.concatenate([everyone, *moved], axis=0)
    table = call(
        fold_kernel, jax.ShapeDtypeStruct((4 * HALF, 512), BF16), [pltpu.VMEM((4 * HALF, 2 * HALF), F32)]
    )(received, lattice.reshape(2, walk_count, rows))
    values = call(
        functools.partial(orbital_kernel, unroll=8, each=each),
        jax.ShapeDtypeStruct((walk_count, 2 * chunks, LANES), F32),
        [
            pltpu.VMEM((2, walk_count, 16 * chunks, LANES), F32),
            pltpu.VMEM((2, walk_count, 2 * chunks, LANES), F32),
            pltpu.SMEM((walk_count * chunks,), jnp.int32),
            pltpu.SMEM((walk_count * chunks,), jnp.int32),
        ],
        mebibytes=24,
    )(table, everyone)
    target = lax.all_to_all(values, "walk", 0, 0, tiled=True).reshape(-1, LANES)

    spins = occupied.shape[0]
    per_spin = band_count // spins
    spin = band_index // per_spin
    columns = orbital_head.reshape(orbital_head.shape[0], spins, 2, per_spin, each)
    columns = lax.dynamic_index_in_dim(columns, spin, 1, keepdims=False)
    columns = lax.dynamic_index_in_dim(columns, band_index % per_spin, 2, keepdims=False)
    columns = jnp.transpose(columns, (1, 2, 0))
    columns = jnp.pad(columns, ((0, 0), (0, walk_count - each), (0, 0))).reshape(2 * walk_count, -1)
    sorted_features, net = call(
        sort_kernel,
        (jax.ShapeDtypeStruct(features.shape, BF16), jax.ShapeDtypeStruct((2 * walk_count + 8, count), F32)),
    )(slot, features, columns, up)
    net = pltpu.with_memory_space_constraint(net, pltpu.HBM)
    walkers = walk_count * count // orbitals
    hidden = features.shape[1]
    in_vmem = pl.BlockSpec(memory_space=pltpu.VMEM)
    own = call(
        functools.partial(gradient_kernel, scale=1.0 / walkers),
        jax.ShapeDtypeStruct((2 * walk_count, hidden), F32),
        [pltpu.VMEM(net.shape, F32), pltpu.SemaphoreType.DMA],
        in_specs=[in_vmem, in_vmem, anywhere],
    )(target, sorted_features, net)
    own = own.reshape(2, walk_count, hidden)[:, :each].reshape(-1, LANES)
    own = own + lax.ppermute(own, "walk", [(k, k ^ 1) for k in range(walk_count)])
    chips = walk_count // 2
    shares = lax.all_to_all(
        jnp.broadcast_to(own, (chips, *own.shape)),
        "walk",
        0,
        0,
        axis_index_groups=[[2 * chip + core for chip in range(chips)] for core in range(2)],
        tiled=True,
    )
    summed = jnp.sum(shares, axis=0)
    whole = lax.all_to_all(jnp.broadcast_to(summed, (band_count, *own.shape)), "band", 0, 0, tiled=True)
    whole = whole.reshape(spins, per_spin, 2, each, hidden)
    return jnp.transpose(whole, (4, 0, 2, 1, 3)).reshape(hidden, 2 * orbitals)


def solution(mesh):
    return jax.shard_map(
        local,
        mesh=mesh,
        in_specs=(
            P(None, "walk"),
            P(None, "walk", "band"),
            P(),
            P("walk"),
            P(),
            P("walk", None),
            P(),
        ),
        out_specs=P(),
        check_vma=False,
    )
```

```python
import functools

import jax
import jax.numpy as jnp
from jax import lax
from jax.experimental import pallas as pl
from jax.experimental.pallas import tpu as pltpu
from jax.sharding import PartitionSpec as P


INTERPRET = False
F32 = jnp.float32
BF16 = jnp.bfloat16
PI = 3.141592653589793
BLOCK = 24
RUN = 1024
HALF = 80
LANES = 128


def split3(value):
    high = value.astype(BF16)
    rest = value - high.astype(F32)
    middle = rest.astype(BF16)
    low = (rest - middle.astype(F32)).astype(BF16)
    return high, middle, low


def pick_kernel(coef_hbm, occ_hbm, out_ref, coef_ref, occ_ref, stage_ref, sems):
    copies = [pltpu.make_async_copy(occ_hbm, occ_ref, sems.at[2])]
    copies += [pltpu.make_async_copy(coef_hbm.at[part], coef_ref.at[part], sems.at[part]) for part in range(2)]
    for copy in copies:
        copy.start()
    _, rows, bands = coef_ref.shape
    spins, per_spin = occ_ref.shape
    devices = stage_ref.shape[0] // BLOCK
    senders = lax.axis_size("band")
    each = spins * per_spin // senders
    tiles = rows // LANES
    base = lax.axis_index("band") * bands
    for row in range(2 * tiles, BLOCK):
        stage_ref[pl.ds(row, devices, stride=BLOCK), :] = jnp.zeros((devices, LANES), F32)
    line = lax.broadcasted_iota(jnp.int32, (8, bands), 0)
    lane = lax.broadcasted_iota(jnp.int32, (8, bands), 1) + base
    copies[0].wait()
    picks = []
    for group in range(devices // senders):
        wanted = jnp.full((8, bands), -1, jnp.int32)
        if group < each:
            for sender in range(senders):
                orbital = sender * each + group
                wanted = jnp.where(line == sender, occ_ref[orbital // per_spin, orbital % per_spin], wanted)
        picks.append(jnp.where(lane == wanted, 1.0, 0.0))
    pick = jnp.concatenate(picks, axis=0).astype(BF16)
    for part in range(2):
        copies[1 + part].wait()
        taken = lax.dot_general(
            pick, coef_ref[part], (((1,), (1,)), ((), ())), preferred_element_type=F32
        )
        for tile in range(tiles):
            stage_ref[pl.ds(part * tiles + tile, devices, stride=BLOCK), :] = taken[:, tile * LANES : (tile + 1) * LANES]
    out_ref[...] = stage_ref[...].astype(BF16)


def order_kernel(pos_ref, label_ref, out_ref, slot_ref, up_ref):
    chunks = label_ref.shape[0]
    own = RUN // LANES
    runs = chunks // own
    up = label_ref[...] == 0
    ones = jnp.where(up, 1.0, 0.0)
    row = lax.broadcasted_iota(jnp.int32, (LANES, LANES), 0)
    column = lax.broadcasted_iota(jnp.int32, (LANES, LANES), 1)
    until = jnp.where(row <= column, 1.0, 0.0).astype(BF16)
    inside = jnp.dot(ones.astype(BF16), until, preferred_element_type=F32)
    whole = jnp.broadcast_to(inside[:, LANES - 1 : LANES], inside.shape).astype(BF16)
    row = lax.broadcasted_iota(jnp.int32, (chunks, chunks), 0)
    column = lax.broadcasted_iota(jnp.int32, (chunks, chunks), 1)
    same = jnp.where(row // own == column // own, 1.0, 0.0)
    before = jnp.where(column < row, same, 0.0).astype(BF16)
    rank = inside + jnp.dot(before, whole, preferred_element_type=F32)
    total = jnp.dot(same.astype(BF16), whole, preferred_element_type=F32)
    place = (
        lax.broadcasted_iota(jnp.int32, rank.shape, 0) % own * LANES + lax.broadcasted_iota(jnp.int32, rank.shape, 1)
    ).astype(F32)
    slot = jnp.where(up, rank - 1.0, total + place - rank)
    first = jnp.where(place < total, 1.0, 0.0)
    up_ref[...] = jnp.concatenate([first[chunk : chunk + 1, :] for chunk in range(chunks)], axis=1)
    parts = jnp.concatenate([part.astype(F32) for part in split3(pos_ref[...])], axis=0).astype(BF16)
    here = lax.broadcasted_iota(jnp.int16, (RUN, RUN), 0)
    for run in range(runs):
        line = jnp.concatenate([slot[run * own + k : run * own + k + 1, :] for k in range(own)], axis=1)
        slot_ref[run : run + 1, :] = line
        move = jnp.where(here == line.astype(jnp.int32).astype(jnp.int16), jnp.ones((), BF16), jnp.zeros((), BF16))
        moved = lax.dot_general(
            parts[:, run * RUN : (run + 1) * RUN], move, (((1,), (1,)), ((), ())), preferred_element_type=F32
        )
        moved = moved[0:2] + moved[2:4] + moved[4:6]
        for axis in range(2):
            for k in range(own):
                at = axis * chunks + run * own + k
                out_ref[at : at + 1, :] = moved[axis : axis + 1, k * LANES : (k + 1) * LANES]
        out_ref[2 * chunks + run : 2 * chunks + run + 1, :] = total[run * own : run * own + 1, :]
    out_ref[2 * chunks + runs :, :] = jnp.zeros((out_ref.shape[0] - 2 * chunks - runs, LANES), F32)


def sort_kernel(slot_ref, feature_ref, head_ref, up_ref, out_ref, net_ref):
    here = lax.broadcasted_iota(jnp.int32, (RUN, RUN), 0).astype(F32)
    for run in range(slot_ref.shape[0]):
        move = jnp.where(here == slot_ref[run : run + 1, :], 1.0, 0.0).astype(BF16)
        moved = jnp.dot(move, feature_ref[run * RUN : (run + 1) * RUN, :], preferred_element_type=F32).astype(BF16)
        out_ref[run * RUN : (run + 1) * RUN, :] = moved
        net_ref[: head_ref.shape[0], run * RUN : (run + 1) * RUN] = lax.dot_general(
            head_ref[...], moved, (((1,), (1,)), ((), ())), preferred_element_type=F32
        )
    tail = net_ref.shape[0] - head_ref.shape[0]
    net_ref[head_ref.shape[0] :, :] = jnp.broadcast_to(up_ref[...], (tail, up_ref.shape[1]))


def base_wave(turns):
    quarter = (turns - 0.5) * (0.5 * PI)
    square = quarter * quarter
    sine = quarter * (
        1.0 + square * (-1 / 6 + square * (1 / 120 + square * (-1 / 5040 + square * (1 / 362880))))
    )
    cosine = 1.0 + square * (
        -1 / 2 + square * (1 / 24 + square * (-1 / 720 + square * (1 / 40320 - square * (1 / 3628800))))
    )
    sine, cosine = 2.0 * sine * cosine, 1.0 - 2.0 * sine * sine
    sine, cosine = 2.0 * sine * cosine, 1.0 - 2.0 * sine * sine
    return -cosine, -sine


def times(left, right):
    return left[0] * right[0] - left[1] * right[1], left[1] * right[0] + left[0] * right[1]


def fold_kernel(recv_ref, lat_ref, table_ref, sum_ref):
    groups = lat_ref.shape[1]
    senders = recv_ref.shape[0] // groups
    rows = lat_ref.shape[2]
    tiles = rows // LANES

    sum_ref[...] = jnp.zeros_like(sum_ref)
    frequency = lax.broadcasted_iota(jnp.int16, (HALF, rows), 0)

    def fold(group, carry):
        both = recv_ref[group * senders].astype(F32)
        for sender in range(1, senders):
            both = both + recv_ref[group * senders + sender].astype(F32)
        c_real, c_imag = (jnp.concatenate([both[k + t : k + t + 1] for t in range(tiles)], axis=1) for k in (0, tiles))
        lat_a = lat_ref[0, pl.ds(group, 1), :]
        lat_b = lat_ref[1, pl.ds(group, 1), :]
        sign_a = jnp.where(lat_a < 0, -1.0, 1.0)
        sign_b = jnp.where(lat_b < 0, -1.0, 1.0)
        at_a = frequency == jnp.abs(lat_a).astype(jnp.int16)
        at_b = frequency == jnp.abs(lat_b).astype(jnp.int16)
        zero = jnp.zeros((), BF16)
        left = jnp.concatenate(
            [
                jnp.where(at_a, value.astype(BF16), zero)
                for value in (c_real, c_real * sign_a, c_imag, c_imag * sign_a)
            ],
            axis=0,
        )
        right = jnp.concatenate(
            [jnp.where(at_b, value.astype(BF16), zero) for value in (jnp.ones_like(sign_b), sign_b)], axis=0
        )
        sum_ref[...] += lax.dot_general(left, right, (((1,), (1,)), ((), ())), preferred_element_type=F32)
        return carry

    lax.fori_loop(0, groups, fold, 0, unroll=8)
    real_even = sum_ref[0:HALF, :]
    real_odd = sum_ref[HALF : 2 * HALF, :]
    imag_even = sum_ref[2 * HALF : 3 * HALF, :]
    imag_odd = sum_ref[3 * HALF : 4 * HALF, :]
    even = lax.broadcasted_iota(jnp.int32, real_even.shape, 1) < HALF
    table = jnp.concatenate(
        [
            jnp.where(even, real_even, -imag_even),
            jnp.where(even, -imag_odd, -real_odd),
            jnp.where(even, imag_even, real_even),
            jnp.where(even, real_odd, -imag_odd),
        ],
        axis=0,
    )
    high = table.astype(BF16).astype(F32)
    low = table - high
    pad = jnp.zeros((4 * HALF, table_ref.shape[1] - 6 * HALF), F32)
    table_ref[...] = jnp.concatenate([high, high, low, pad], axis=1).astype(BF16)


def orbital_kernel(table_ref, pos_ref, out_ref, wave_ref, eight_ref, group_ref, chunk_ref, *, unroll, each):
    groups = out_ref.shape[0]
    chunks = out_ref.shape[1] // 2
    own = RUN // LANES
    runs = chunks // own
    upper = lax.axis_index("band") < lax.axis_size("band") // 2
    walk = lax.axis_index("walk")
    active = walk < each
    out_ref[...] = jnp.zeros_like(out_ref)

    def waves(group, length):
        away = group ^ walk
        for line in range(0, 2 * chunks, 8):
            first = base_wave(pos_ref[away, line : line + 8, :])
            power = (jnp.ones((8, LANES), F32), jnp.zeros((8, LANES), F32))
            for k in range(8):
                for half in range(2):
                    wave_ref[half, group, pl.ds(line * 8 + k, 8, stride=8), :] = power[half]
                power = first if k == 0 else times(power, first)
            for half in range(2):
                eight_ref[half, group, line : line + 8, :] = power[half]
        numbers = pos_ref[away, 2 * chunks : 2 * chunks + runs, :].astype(jnp.int32)
        for run in range(runs):
            number = numbers[run, 0]
            low = jnp.where(upper, 0, number // LANES)
            high = jnp.where(upper, (number + LANES - 1) // LANES, own)
            high = jnp.where(active, high, low)

            def note(chunk, at):
                group_ref[at] = group
                chunk_ref[at] = run * own + chunk
                return at + 1

            length = lax.fori_loop(low, high, note, length)
        return length

    length = lax.fori_loop(0, groups, waves, 0)

    def basis(entry, axis):
        group, chunk = entry
        line = axis * chunks + chunk
        start = pl.multiple_of(line * 8, 8)
        now = tuple(wave_ref[half, group, pl.ds(start, 8), :] for half in range(2))
        step = tuple(jnp.broadcast_to(eight_ref[half, group, pl.ds(line, 1), :], (8, LANES)) for half in range(2))
        twice = 2.0 * step[0]
        last, now = now, times(now, step)
        cosines, sines = [last[0], now[0]], [last[1], now[1]]
        for _ in range(2, HALF // 8):
            last, now = now, tuple(twice * now[half] - last[half] for half in range(2))
            cosines.append(now[0])
            sines.append(now[1])
        return jnp.concatenate(cosines + sines, axis=0)

    zeros = jnp.zeros((table_ref.shape[1] - 6 * HALF, 2 * LANES), BF16)

    def evaluate(index, carry):
        for inner in range(unroll):
            places = [jnp.minimum((index * unroll + inner) * 2 + side, length - 1) for side in range(2)]
            entries = [(group_ref[place], chunk_ref[place]) for place in places]
            wave_y = jnp.concatenate([basis(entry, 1) for entry in entries], axis=1)
            high_y = wave_y.astype(BF16)
            low_y = (wave_y - high_y.astype(F32)).astype(BF16)
            weights = jnp.concatenate([high_y, low_y, high_y, zeros], axis=0)
            inside = jnp.dot(table_ref[...], weights, preferred_element_type=F32)
            wave_x = jnp.concatenate([basis(entry, 0) for entry in entries], axis=1)
            for half in range(2):
                value = jnp.sum(inside[half * 2 * HALF : (half + 1) * 2 * HALF, :] * wave_x, axis=0, keepdims=True)
                for side, (group, chunk) in enumerate(entries):
                    out_ref[group, pl.ds(half * chunks + chunk, 1), :] = value[:, side * LANES : (side + 1) * LANES]
        return carry

    lax.fori_loop(0, (length + 2 * unroll - 1) // (2 * unroll), evaluate, 0)


def gradient_kernel(target_ref, feature_ref, net_hbm, out_ref, net_ref, sem, *, scale):
    copy = pltpu.make_async_copy(net_hbm, net_ref, sem)
    copy.start()
    chunks = feature_ref.shape[0] // LANES
    slots = out_ref.shape[0] // 2
    upper = lax.axis_index("band") < lax.axis_size("band") // 2
    targets = [
        jnp.concatenate(
            [target_ref[pl.ds(half * chunks + chunk, slots, stride=2 * chunks), :] for chunk in range(chunks)], axis=1
        )
        for half in range(2)
    ]
    copy.wait()
    mine = net_ref[2 * slots : 2 * slots + 1, :] == jnp.where(upper, 1.0, 0.0)
    parts = []
    for half in range(2):
        scaled = (net_ref[half * slots : (half + 1) * slots, :] - targets[half]) * scale
        parts.append(jnp.where(mine, scaled, 0.0))
    spread = jnp.concatenate(parts, axis=0)
    pieces = jnp.concatenate([piece.astype(F32) for piece in split3(spread)], axis=0).astype(BF16)
    total = jnp.dot(pieces, feature_ref[...], preferred_element_type=F32)
    height = out_ref.shape[0]
    out_ref[...] = total[:height] + total[height : 2 * height] + total[2 * height :]


def call(kernel, out, scratch=(), mebibytes=16, **more):
    return pl.pallas_call(
        kernel,
        out_shape=out,
        **more,
        scratch_shapes=list(scratch),
        interpret=INTERPRET,
        compiler_params=pltpu.CompilerParams(vmem_limit_bytes=mebibytes * 1024 * 1024),
    )


def local(positions, coefficients, lattice, spin_labels, occupied, features, orbital_head):
    walk_count = lax.axis_size("walk")
    band_count = lax.axis_size("band")
    band_index = lax.axis_index("band")
    devices = walk_count * band_count
    rows = coefficients.shape[1]
    count = positions.shape[1]
    orbitals = occupied.shape[0] * occupied.shape[1]
    each = orbitals // band_count

    chunks = count // LANES
    anywhere = pl.BlockSpec(memory_space=pltpu.HBM)
    picked = call(
        pick_kernel,
        jax.ShapeDtypeStruct((devices * BLOCK, LANES), BF16),
        [
            pltpu.VMEM(coefficients.shape, BF16),
            pltpu.SMEM(occupied.shape, jnp.int32),
            pltpu.VMEM((devices * BLOCK, LANES), F32),
            pltpu.SemaphoreType.DMA((3,)),
        ],
        in_specs=[anywhere, anywhere],
    )(pltpu.with_memory_space_constraint(coefficients, pltpu.HBM), pltpu.with_memory_space_constraint(occupied, pltpu.HBM))
    picked, positions = lax.optimization_barrier((picked, positions))
    received = lax.all_to_all(picked.reshape(devices, BLOCK, LANES), ("walk", "band"), 0, 0, tiled=True)
    ordered, slot, up = call(
        order_kernel,
        (
            jax.ShapeDtypeStruct((2 * chunks + 8, LANES), F32),
            jax.ShapeDtypeStruct((count // RUN, RUN), F32),
            jax.ShapeDtypeStruct((1, count), F32),
        ),
    )(positions, spin_labels.reshape(chunks, LANES))
    everyone = ordered[None]
    for flips in ((1,), tuple(range(2, walk_count, 2))):
        moved = [lax.ppermute(everyone, "walk", [(k, k ^ flip) for k in range(walk_count)]) for flip in flips]
        everyone = jnp.concatenate([everyone, *moved], axis=0)
    table = call(
        fold_kernel, jax.ShapeDtypeStruct((4 * HALF, 512), BF16), [pltpu.VMEM((4 * HALF, 2 * HALF), F32)]
    )(received, lattice.reshape(2, walk_count, rows))
    values = call(
        functools.partial(orbital_kernel, unroll=12, each=each),
        jax.ShapeDtypeStruct((walk_count, 2 * chunks, LANES), F32),
        [
            pltpu.VMEM((2, walk_count, 16 * chunks, LANES), F32),
            pltpu.VMEM((2, walk_count, 2 * chunks, LANES), F32),
            pltpu.SMEM((walk_count * chunks,), jnp.int32),
            pltpu.SMEM((walk_count * chunks,), jnp.int32),
        ],
        mebibytes=24,
    )(table, everyone)
    target = lax.all_to_all(values, "walk", 0, 0, tiled=True).reshape(-1, LANES)

    spins = occupied.shape[0]
    per_spin = band_count // spins
    spin = band_index // per_spin
    columns = orbital_head.reshape(orbital_head.shape[0], spins, 2, per_spin, each)
    columns = lax.dynamic_index_in_dim(columns, spin, 1, keepdims=False)
    columns = lax.dynamic_index_in_dim(columns, band_index % per_spin, 2, keepdims=False)
    columns = jnp.transpose(columns, (1, 2, 0))
    columns = jnp.pad(columns, ((0, 0), (0, walk_count - each), (0, 0))).reshape(2 * walk_count, -1)
    sorted_features, net = call(
        sort_kernel,
        (jax.ShapeDtypeStruct(features.shape, BF16), jax.ShapeDtypeStruct((2 * walk_count + 8, count), F32)),
    )(slot, features, columns, up)
    net = pltpu.with_memory_space_constraint(net, pltpu.HBM)
    walkers = walk_count * count // orbitals
    hidden = features.shape[1]
    in_vmem = pl.BlockSpec(memory_space=pltpu.VMEM)
    own = call(
        functools.partial(gradient_kernel, scale=1.0 / walkers),
        jax.ShapeDtypeStruct((2 * walk_count, hidden), F32),
        [pltpu.VMEM(net.shape, F32), pltpu.SemaphoreType.DMA],
        in_specs=[in_vmem, in_vmem, anywhere],
    )(target, sorted_features, net)
    own = own.reshape(2, walk_count, hidden)[:, :each].reshape(-1, LANES)
    own = own + lax.ppermute(own, "walk", [(k, k ^ 1) for k in range(walk_count)])
    chips = walk_count // 2
    shares = lax.all_to_all(
        jnp.broadcast_to(own, (chips, *own.shape)),
        "walk",
        0,
        0,
        axis_index_groups=[[2 * chip + core for chip in range(chips)] for core in range(2)],
        tiled=True,
    )
    summed = jnp.sum(shares, axis=0)
    whole = lax.all_to_all(jnp.broadcast_to(summed, (band_count, *own.shape)), "band", 0, 0, tiled=True)
    whole = whole.reshape(spins, per_spin, 2, each, hidden)
    return jnp.transpose(whole, (4, 0, 2, 1, 3)).reshape(hidden, 2 * orbitals)


def solution(mesh):
    return jax.shard_map(
        local,
        mesh=mesh,
        in_specs=(
            P(None, "walk"),
            P(None, "walk", "band"),
            P(),
            P("walk"),
            P(),
            P("walk", None),
            P(),
        ),
        out_specs=P(),
        check_vma=False,
    )
```

```python
import functools

import jax
import jax.numpy as jnp
from jax import lax
from jax.experimental import pallas as pl
from jax.experimental.pallas import tpu as pltpu
from jax.sharding import PartitionSpec as P


INTERPRET = False
F32 = jnp.float32
BF16 = jnp.bfloat16
PI = 3.141592653589793
BLOCK = 24
RUN = 1024
HALF = 80
LANES = 128


def split3(value):
    high = value.astype(BF16)
    rest = value - high.astype(F32)
    middle = rest.astype(BF16)
    low = (rest - middle.astype(F32)).astype(BF16)
    return high, middle, low


def pick_kernel(coef_hbm, occ_hbm, out_ref, coef_ref, occ_ref, stage_ref, sems):
    copies = [pltpu.make_async_copy(occ_hbm, occ_ref, sems.at[2])]
    copies += [pltpu.make_async_copy(coef_hbm.at[part], coef_ref.at[part], sems.at[part]) for part in range(2)]
    for copy in copies:
        copy.start()
    _, rows, bands = coef_ref.shape
    spins, per_spin = occ_ref.shape
    devices = stage_ref.shape[0] // BLOCK
    senders = lax.axis_size("band")
    each = spins * per_spin // senders
    tiles = rows // LANES
    base = lax.axis_index("band") * bands
    for row in range(2 * tiles, BLOCK):
        stage_ref[pl.ds(row, devices, stride=BLOCK), :] = jnp.zeros((devices, LANES), F32)
    line = lax.broadcasted_iota(jnp.int32, (8, bands), 0)
    lane = lax.broadcasted_iota(jnp.int32, (8, bands), 1) + base
    copies[0].wait()
    picks = []
    for group in range(devices // senders):
        wanted = jnp.full((8, bands), -1, jnp.int32)
        if group < each:
            for sender in range(senders):
                orbital = sender * each + group
                wanted = jnp.where(line == sender, occ_ref[orbital // per_spin, orbital % per_spin], wanted)
        picks.append(jnp.where(lane == wanted, 1.0, 0.0))
    pick = jnp.concatenate(picks, axis=0).astype(BF16)
    for part in range(2):
        copies[1 + part].wait()
        taken = lax.dot_general(
            pick, coef_ref[part], (((1,), (1,)), ((), ())), preferred_element_type=F32
        )
        for tile in range(tiles):
            stage_ref[pl.ds(part * tiles + tile, devices, stride=BLOCK), :] = taken[:, tile * LANES : (tile + 1) * LANES]
    out_ref[...] = stage_ref[...].astype(BF16)


def order_kernel(pos_ref, label_ref, out_ref, slot_ref, up_ref):
    chunks = label_ref.shape[0]
    own = RUN // LANES
    runs = chunks // own
    up = label_ref[...] == 0
    ones = jnp.where(up, 1.0, 0.0)
    row = lax.broadcasted_iota(jnp.int32, (LANES, LANES), 0)
    column = lax.broadcasted_iota(jnp.int32, (LANES, LANES), 1)
    until = jnp.where(row <= column, 1.0, 0.0).astype(BF16)
    inside = jnp.dot(ones.astype(BF16), until, preferred_element_type=F32)
    whole = jnp.broadcast_to(inside[:, LANES - 1 : LANES], inside.shape).astype(BF16)
    row = lax.broadcasted_iota(jnp.int32, (chunks, chunks), 0)
    column = lax.broadcasted_iota(jnp.int32, (chunks, chunks), 1)
    same = jnp.where(row // own == column // own, 1.0, 0.0)
    before = jnp.where(column < row, same, 0.0).astype(BF16)
    rank = inside + jnp.dot(before, whole, preferred_element_type=F32)
    total = jnp.dot(same.astype(BF16), whole, preferred_element_type=F32)
    place = (
        lax.broadcasted_iota(jnp.int32, rank.shape, 0) % own * LANES + lax.broadcasted_iota(jnp.int32, rank.shape, 1)
    ).astype(F32)
    slot = jnp.where(up, rank - 1.0, total + place - rank)
    first = jnp.where(place < total, 1.0, 0.0)
    up_ref[...] = jnp.concatenate([first[chunk : chunk + 1, :] for chunk in range(chunks)], axis=1)
    parts = jnp.concatenate([part.astype(F32) for part in split3(pos_ref[...])], axis=0).astype(BF16)
    here = lax.broadcasted_iota(jnp.int16, (RUN, RUN), 0)
    for run in range(runs):
        line = jnp.concatenate([slot[run * own + k : run * own + k + 1, :] for k in range(own)], axis=1)
        slot_ref[run : run + 1, :] = line
        move = jnp.where(here == line.astype(jnp.int32).astype(jnp.int16), jnp.ones((), BF16), jnp.zeros((), BF16))
        moved = lax.dot_general(
            parts[:, run * RUN : (run + 1) * RUN], move, (((1,), (1,)), ((), ())), preferred_element_type=F32
        )
        moved = moved[0:2] + moved[2:4] + moved[4:6]
        for axis in range(2):
            for k in range(own):
                at = axis * chunks + run * own + k
                out_ref[at : at + 1, :] = moved[axis : axis + 1, k * LANES : (k + 1) * LANES]
        out_ref[2 * chunks + run : 2 * chunks + run + 1, :] = total[run * own : run * own + 1, :]
    out_ref[2 * chunks + runs :, :] = jnp.zeros((out_ref.shape[0] - 2 * chunks - runs, LANES), F32)


def sort_kernel(slot_ref, feature_ref, head_ref, up_ref, out_ref, net_ref):
    here = lax.broadcasted_iota(jnp.int32, (RUN, RUN), 0).astype(F32)
    for run in range(slot_ref.shape[0]):
        move = jnp.where(here == slot_ref[run : run + 1, :], 1.0, 0.0).astype(BF16)
        moved = jnp.dot(move, feature_ref[run * RUN : (run + 1) * RUN, :], preferred_element_type=F32).astype(BF16)
        out_ref[run * RUN : (run + 1) * RUN, :] = moved
        net_ref[: head_ref.shape[0], run * RUN : (run + 1) * RUN] = lax.dot_general(
            head_ref[...], moved, (((1,), (1,)), ((), ())), preferred_element_type=F32
        )
    tail = net_ref.shape[0] - head_ref.shape[0]
    net_ref[head_ref.shape[0] :, :] = jnp.broadcast_to(up_ref[...], (tail, up_ref.shape[1]))


def base_wave(turns):
    quarter = (turns - 0.5) * (0.5 * PI)
    square = quarter * quarter
    sine = quarter * (
        1.0 + square * (-1 / 6 + square * (1 / 120 + square * (-1 / 5040 + square * (1 / 362880))))
    )
    cosine = 1.0 + square * (
        -1 / 2 + square * (1 / 24 + square * (-1 / 720 + square * (1 / 40320 - square * (1 / 3628800))))
    )
    sine, cosine = 2.0 * sine * cosine, 1.0 - 2.0 * sine * sine
    sine, cosine = 2.0 * sine * cosine, 1.0 - 2.0 * sine * sine
    return -cosine, -sine


def times(left, right):
    return left[0] * right[0] - left[1] * right[1], left[1] * right[0] + left[0] * right[1]


def fold_kernel(recv_ref, lat_ref, table_ref, sum_ref):
    groups = lat_ref.shape[1]
    senders = recv_ref.shape[0] // groups
    rows = lat_ref.shape[2]
    tiles = rows // LANES

    sum_ref[...] = jnp.zeros_like(sum_ref)
    frequency = lax.broadcasted_iota(jnp.int16, (HALF, rows), 0)

    def fold(group, carry):
        both = recv_ref[group * senders].astype(F32)
        for sender in range(1, senders):
            both = both + recv_ref[group * senders + sender].astype(F32)
        c_real, c_imag = (jnp.concatenate([both[k + t : k + t + 1] for t in range(tiles)], axis=1) for k in (0, tiles))
        lat_a = lat_ref[0, pl.ds(group, 1), :]
        lat_b = lat_ref[1, pl.ds(group, 1), :]
        sign_a = jnp.where(lat_a < 0, -1.0, 1.0)
        sign_b = jnp.where(lat_b < 0, -1.0, 1.0)
        at_a = frequency == jnp.abs(lat_a).astype(jnp.int16)
        at_b = frequency == jnp.abs(lat_b).astype(jnp.int16)
        zero = jnp.zeros((), BF16)
        left = jnp.concatenate(
            [
                jnp.where(at_a, value.astype(BF16), zero)
                for value in (c_real, c_real * sign_a, c_imag, c_imag * sign_a)
            ],
            axis=0,
        )
        right = jnp.concatenate(
            [jnp.where(at_b, value.astype(BF16), zero) for value in (jnp.ones_like(sign_b), sign_b)], axis=0
        )
        sum_ref[...] += lax.dot_general(left, right, (((1,), (1,)), ((), ())), preferred_element_type=F32)
        return carry

    lax.fori_loop(0, groups, fold, 0, unroll=8)
    real_even = sum_ref[0:HALF, :]
    real_odd = sum_ref[HALF : 2 * HALF, :]
    imag_even = sum_ref[2 * HALF : 3 * HALF, :]
    imag_odd = sum_ref[3 * HALF : 4 * HALF, :]
    even = lax.broadcasted_iota(jnp.int32, real_even.shape, 1) < HALF
    table = jnp.concatenate(
        [
            jnp.where(even, real_even, -imag_even),
            jnp.where(even, -imag_odd, -real_odd),
            jnp.where(even, imag_even, real_even),
            jnp.where(even, real_odd, -imag_odd),
        ],
        axis=0,
    )
    high = table.astype(BF16).astype(F32)
    low = table - high
    pad = jnp.zeros((4 * HALF, table_ref.shape[1] - 6 * HALF), F32)
    table_ref[...] = jnp.concatenate([high, high, low, pad], axis=1).astype(BF16)


def orbital_kernel(table_ref, pos_ref, out_ref, wave_ref, eight_ref, group_ref, chunk_ref, *, unroll, each):
    groups = out_ref.shape[0]
    chunks = out_ref.shape[1] // 2
    own = RUN // LANES
    runs = chunks // own
    upper = lax.axis_index("band") < lax.axis_size("band") // 2
    walk = lax.axis_index("walk")
    active = walk < each
    out_ref[...] = jnp.zeros_like(out_ref)

    def waves(group, length):
        away = group ^ walk
        for line in range(0, 2 * chunks, 8):
            first = base_wave(pos_ref[away, line : line + 8, :])
            power = (jnp.ones((8, LANES), F32), jnp.zeros((8, LANES), F32))
            for k in range(8):
                for half in range(2):
                    wave_ref[half, group, pl.ds(line * 8 + k, 8, stride=8), :] = power[half]
                power = first if k == 0 else times(power, first)
            for half in range(2):
                eight_ref[half, group, line : line + 8, :] = power[half]
        numbers = pos_ref[away, 2 * chunks : 2 * chunks + runs, :].astype(jnp.int32)
        for run in range(runs):
            number = numbers[run, 0]
            low = jnp.where(upper, 0, number // LANES)
            high = jnp.where(upper, (number + LANES - 1) // LANES, own)
            high = jnp.where(active, high, low)

            def note(chunk, at):
                group_ref[at] = group
                chunk_ref[at] = run * own + chunk
                return at + 1

            length = lax.fori_loop(low, high, note, length)
        return length

    length = lax.fori_loop(0, groups, waves, 0)

    def basis(entry, axis):
        group, chunk = entry
        line = axis * chunks + chunk
        start = pl.multiple_of(line * 8, 8)
        now = tuple(wave_ref[half, group, pl.ds(start, 8), :] for half in range(2))
        step = tuple(jnp.broadcast_to(eight_ref[half, group, pl.ds(line, 1), :], (8, LANES)) for half in range(2))
        twice = 2.0 * step[0]
        last, now = now, times(now, step)
        cosines, sines = [last[0], now[0]], [last[1], now[1]]
        for _ in range(2, HALF // 8):
            last, now = now, tuple(twice * now[half] - last[half] for half in range(2))
            cosines.append(now[0])
            sines.append(now[1])
        return jnp.concatenate(cosines + sines, axis=0)

    zeros = jnp.zeros((table_ref.shape[1] - 6 * HALF, 2 * LANES), BF16)

    def evaluate(first, size):
        for inner in range(size):
            places = [jnp.minimum(first + inner * 2 + side, length - 1) for side in range(2)]
            entries = [(group_ref[place], chunk_ref[place]) for place in places]
            wave_y = jnp.concatenate([basis(entry, 1) for entry in entries], axis=1)
            high_y = wave_y.astype(BF16)
            low_y = (wave_y - high_y.astype(F32)).astype(BF16)
            weights = jnp.concatenate([high_y, low_y, high_y, zeros], axis=0)
            inside = jnp.dot(table_ref[...], weights, preferred_element_type=F32)
            wave_x = jnp.concatenate([basis(entry, 0) for entry in entries], axis=1)
            for half in range(2):
                value = jnp.sum(inside[half * 2 * HALF : (half + 1) * 2 * HALF, :] * wave_x, axis=0, keepdims=True)
                for side, (group, chunk) in enumerate(entries):
                    out_ref[group, pl.ds(half * chunks + chunk, 1), :] = value[:, side * LANES : (side + 1) * LANES]

    def many(index, carry):
        evaluate(index * 2 * unroll, unroll)
        return carry

    def few(index, carry):
        evaluate(length // (2 * unroll) * 2 * unroll + index * 2 * rest, rest)
        return carry

    rest = 4
    lax.fori_loop(0, length // (2 * unroll), many, 0)
    lax.fori_loop(0, (length % (2 * unroll) + 2 * rest - 1) // (2 * rest), few, 0)


def gradient_kernel(target_ref, feature_ref, net_hbm, out_ref, net_ref, sem, *, scale):
    copy = pltpu.make_async_copy(net_hbm, net_ref, sem)
    copy.start()
    chunks = feature_ref.shape[0] // LANES
    slots = out_ref.shape[0] // 2
    upper = lax.axis_index("band") < lax.axis_size("band") // 2
    targets = [
        jnp.concatenate(
            [target_ref[pl.ds(half * chunks + chunk, slots, stride=2 * chunks), :] for chunk in range(chunks)], axis=1
        )
        for half in range(2)
    ]
    copy.wait()
    mine = net_ref[2 * slots : 2 * slots + 1, :] == jnp.where(upper, 1.0, 0.0)
    parts = []
    for half in range(2):
        scaled = (net_ref[half * slots : (half + 1) * slots, :] - targets[half]) * scale
        parts.append(jnp.where(mine, scaled, 0.0))
    spread = jnp.concatenate(parts, axis=0)
    pieces = jnp.concatenate([piece.astype(F32) for piece in split3(spread)], axis=0).astype(BF16)
    total = jnp.dot(pieces, feature_ref[...], preferred_element_type=F32)
    height = out_ref.shape[0]
    out_ref[...] = total[:height] + total[height : 2 * height] + total[2 * height :]


def call(kernel, out, scratch=(), mebibytes=16, **more):
    return pl.pallas_call(
        kernel,
        out_shape=out,
        **more,
        scratch_shapes=list(scratch),
        interpret=INTERPRET,
        compiler_params=pltpu.CompilerParams(vmem_limit_bytes=mebibytes * 1024 * 1024),
    )


def local(positions, coefficients, lattice, spin_labels, occupied, features, orbital_head):
    walk_count = lax.axis_size("walk")
    band_count = lax.axis_size("band")
    band_index = lax.axis_index("band")
    devices = walk_count * band_count
    rows = coefficients.shape[1]
    count = positions.shape[1]
    orbitals = occupied.shape[0] * occupied.shape[1]
    each = orbitals // band_count

    chunks = count // LANES
    anywhere = pl.BlockSpec(memory_space=pltpu.HBM)
    picked = call(
        pick_kernel,
        jax.ShapeDtypeStruct((devices * BLOCK, LANES), BF16),
        [
            pltpu.VMEM(coefficients.shape, BF16),
            pltpu.SMEM(occupied.shape, jnp.int32),
            pltpu.VMEM((devices * BLOCK, LANES), F32),
            pltpu.SemaphoreType.DMA((3,)),
        ],
        in_specs=[anywhere, anywhere],
    )(pltpu.with_memory_space_constraint(coefficients, pltpu.HBM), pltpu.with_memory_space_constraint(occupied, pltpu.HBM))
    picked, positions = lax.optimization_barrier((picked, positions))
    received = lax.all_to_all(picked.reshape(devices, BLOCK, LANES), ("walk", "band"), 0, 0, tiled=True)
    ordered, slot, up = call(
        order_kernel,
        (
            jax.ShapeDtypeStruct((2 * chunks + 8, LANES), F32),
            jax.ShapeDtypeStruct((count // RUN, RUN), F32),
            jax.ShapeDtypeStruct((1, count), F32),
        ),
    )(positions, spin_labels.reshape(chunks, LANES))
    everyone = ordered[None]
    for flips in ((1,), tuple(range(2, walk_count, 2))):
        moved = [lax.ppermute(everyone, "walk", [(k, k ^ flip) for k in range(walk_count)]) for flip in flips]
        everyone = jnp.concatenate([everyone, *moved], axis=0)
    table = call(
        fold_kernel, jax.ShapeDtypeStruct((4 * HALF, 512), BF16), [pltpu.VMEM((4 * HALF, 2 * HALF), F32)]
    )(received, lattice.reshape(2, walk_count, rows))
    values = call(
        functools.partial(orbital_kernel, unroll=12, each=each),
        jax.ShapeDtypeStruct((walk_count, 2 * chunks, LANES), F32),
        [
            pltpu.VMEM((2, walk_count, 16 * chunks, LANES), F32),
            pltpu.VMEM((2, walk_count, 2 * chunks, LANES), F32),
            pltpu.SMEM((walk_count * chunks,), jnp.int32),
            pltpu.SMEM((walk_count * chunks,), jnp.int32),
        ],
        mebibytes=24,
    )(table, everyone)
    target = lax.all_to_all(values, "walk", 0, 0, tiled=True).reshape(-1, LANES)

    spins = occupied.shape[0]
    per_spin = band_count // spins
    spin = band_index // per_spin
    columns = orbital_head.reshape(orbital_head.shape[0], spins, 2, per_spin, each)
    columns = lax.dynamic_index_in_dim(columns, spin, 1, keepdims=False)
    columns = lax.dynamic_index_in_dim(columns, band_index % per_spin, 2, keepdims=False)
    columns = jnp.transpose(columns, (1, 2, 0))
    columns = jnp.pad(columns, ((0, 0), (0, walk_count - each), (0, 0))).reshape(2 * walk_count, -1)
    sorted_features, net = call(
        sort_kernel,
        (jax.ShapeDtypeStruct(features.shape, BF16), jax.ShapeDtypeStruct((2 * walk_count + 8, count), F32)),
    )(slot, features, columns, up)
    net = pltpu.with_memory_space_constraint(net, pltpu.HBM)
    walkers = walk_count * count // orbitals
    hidden = features.shape[1]
    in_vmem = pl.BlockSpec(memory_space=pltpu.VMEM)
    own = call(
        functools.partial(gradient_kernel, scale=1.0 / walkers),
        jax.ShapeDtypeStruct((2 * walk_count, hidden), F32),
        [pltpu.VMEM(net.shape, F32), pltpu.SemaphoreType.DMA],
        in_specs=[in_vmem, in_vmem, anywhere],
    )(target, sorted_features, net)
    own = own.reshape(2, walk_count, hidden)[:, :each].reshape(-1, LANES)
    own = own + lax.ppermute(own, "walk", [(k, k ^ 1) for k in range(walk_count)])
    chips = walk_count // 2
    shares = lax.all_to_all(
        jnp.broadcast_to(own, (chips, *own.shape)),
        "walk",
        0,
        0,
        axis_index_groups=[[2 * chip + core for chip in range(chips)] for core in range(2)],
        tiled=True,
    )
    summed = jnp.sum(shares, axis=0)
    whole = lax.all_to_all(jnp.broadcast_to(summed, (band_count, *own.shape)), "band", 0, 0, tiled=True)
    whole = whole.reshape(spins, per_spin, 2, each, hidden)
    return jnp.transpose(whole, (4, 0, 2, 1, 3)).reshape(hidden, 2 * orbitals)


def solution(mesh):
    return jax.shard_map(
        local,
        mesh=mesh,
        in_specs=(
            P(None, "walk"),
            P(None, "walk", "band"),
            P(),
            P("walk"),
            P(),
            P("walk", None),
            P(),
        ),
        out_specs=P(),
        check_vma=False,
    )
```

```python
import functools

import jax
import jax.numpy as jnp
from jax import lax
from jax.experimental import pallas as pl
from jax.experimental.pallas import tpu as pltpu
from jax.sharding import PartitionSpec as P


INTERPRET = False
F32 = jnp.float32
BF16 = jnp.bfloat16
PI = 3.141592653589793
BLOCK = 24
RUN = 1024
HALF = 80
LANES = 128


def split3(value):
    high = value.astype(BF16)
    rest = value - high.astype(F32)
    middle = rest.astype(BF16)
    low = (rest - middle.astype(F32)).astype(BF16)
    return high, middle, low


def pick_kernel(coef_hbm, occ_hbm, out_ref, coef_ref, occ_ref, stage_ref, sems):
    copies = [pltpu.make_async_copy(occ_hbm, occ_ref, sems.at[2])]
    copies += [pltpu.make_async_copy(coef_hbm.at[part], coef_ref.at[part], sems.at[part]) for part in range(2)]
    for copy in copies:
        copy.start()
    _, rows, bands = coef_ref.shape
    spins, per_spin = occ_ref.shape
    devices = stage_ref.shape[0] // BLOCK
    senders = lax.axis_size("band")
    each = spins * per_spin // senders
    tiles = rows // LANES
    base = lax.axis_index("band") * bands
    for row in range(2 * tiles, BLOCK):
        stage_ref[pl.ds(row, devices, stride=BLOCK), :] = jnp.zeros((devices, LANES), F32)
    line = lax.broadcasted_iota(jnp.int32, (8, bands), 0)
    lane = lax.broadcasted_iota(jnp.int32, (8, bands), 1) + base
    copies[0].wait()
    picks = []
    for group in range(devices // senders):
        wanted = jnp.full((8, bands), -1, jnp.int32)
        if group < each:
            for sender in range(senders):
                orbital = sender * each + group
                wanted = jnp.where(line == sender, occ_ref[orbital // per_spin, orbital % per_spin], wanted)
        picks.append(jnp.where(lane == wanted, 1.0, 0.0))
    pick = jnp.concatenate(picks, axis=0).astype(BF16)
    for part in range(2):
        copies[1 + part].wait()
        taken = lax.dot_general(
            pick, coef_ref[part], (((1,), (1,)), ((), ())), preferred_element_type=F32
        )
        for tile in range(tiles):
            stage_ref[pl.ds(part * tiles + tile, devices, stride=BLOCK), :] = taken[:, tile * LANES : (tile + 1) * LANES]
    out_ref[...] = stage_ref[...].astype(BF16)


def order_kernel(pos_ref, label_ref, out_ref, slot_ref, up_ref):
    chunks = label_ref.shape[0]
    own = RUN // LANES
    runs = chunks // own
    up = label_ref[...] == 0
    ones = jnp.where(up, 1.0, 0.0)
    row = lax.broadcasted_iota(jnp.int32, (LANES, LANES), 0)
    column = lax.broadcasted_iota(jnp.int32, (LANES, LANES), 1)
    until = jnp.where(row <= column, 1.0, 0.0).astype(BF16)
    inside = jnp.dot(ones.astype(BF16), until, preferred_element_type=F32)
    whole = jnp.broadcast_to(inside[:, LANES - 1 : LANES], inside.shape).astype(BF16)
    row = lax.broadcasted_iota(jnp.int32, (chunks, chunks), 0)
    column = lax.broadcasted_iota(jnp.int32, (chunks, chunks), 1)
    same = jnp.where(row // own == column // own, 1.0, 0.0)
    before = jnp.where(column < row, same, 0.0).astype(BF16)
    rank = inside + jnp.dot(before, whole, preferred_element_type=F32)
    total = jnp.dot(same.astype(BF16), whole, preferred_element_type=F32)
    place = (
        lax.broadcasted_iota(jnp.int32, rank.shape, 0) % own * LANES + lax.broadcasted_iota(jnp.int32, rank.shape, 1)
    ).astype(F32)
    slot = jnp.where(up, rank - 1.0, total + place - rank)
    first = jnp.where(place < total, 1.0, 0.0)
    up_ref[...] = jnp.concatenate([first[chunk : chunk + 1, :] for chunk in range(chunks)], axis=1)
    parts = jnp.concatenate([part.astype(F32) for part in split3(pos_ref[...])], axis=0).astype(BF16)
    here = lax.broadcasted_iota(jnp.int16, (RUN, RUN), 0)
    for run in range(runs):
        line = jnp.concatenate([slot[run * own + k : run * own + k + 1, :] for k in range(own)], axis=1)
        slot_ref[run : run + 1, :] = line
        move = jnp.where(here == line.astype(jnp.int32).astype(jnp.int16), jnp.ones((), BF16), jnp.zeros((), BF16))
        moved = lax.dot_general(
            parts[:, run * RUN : (run + 1) * RUN], move, (((1,), (1,)), ((), ())), preferred_element_type=F32
        )
        moved = moved[0:2] + moved[2:4] + moved[4:6]
        for axis in range(2):
            for k in range(own):
                at = axis * chunks + run * own + k
                out_ref[at : at + 1, :] = moved[axis : axis + 1, k * LANES : (k + 1) * LANES]
        out_ref[2 * chunks + run : 2 * chunks + run + 1, :] = total[run * own : run * own + 1, :]
    out_ref[2 * chunks + runs :, :] = jnp.zeros((out_ref.shape[0] - 2 * chunks - runs, LANES), F32)


def sort_kernel(slot_ref, feature_ref, head_ref, up_ref, out_ref, net_ref):
    here = lax.broadcasted_iota(jnp.int32, (RUN, RUN), 0).astype(F32)
    for run in range(slot_ref.shape[0]):
        move = jnp.where(here == slot_ref[run : run + 1, :], 1.0, 0.0).astype(BF16)
        moved = jnp.dot(move, feature_ref[run * RUN : (run + 1) * RUN, :], preferred_element_type=F32).astype(BF16)
        out_ref[run * RUN : (run + 1) * RUN, :] = moved
        net_ref[: head_ref.shape[0], run * RUN : (run + 1) * RUN] = lax.dot_general(
            head_ref[...], moved, (((1,), (1,)), ((), ())), preferred_element_type=F32
        )
    tail = net_ref.shape[0] - head_ref.shape[0]
    net_ref[head_ref.shape[0] :, :] = jnp.broadcast_to(up_ref[...], (tail, up_ref.shape[1]))


def base_wave(turns):
    quarter = (turns - 0.5) * (0.5 * PI)
    square = quarter * quarter
    sine = quarter * (
        1.0 + square * (-1 / 6 + square * (1 / 120 + square * (-1 / 5040 + square * (1 / 362880))))
    )
    cosine = 1.0 + square * (
        -1 / 2 + square * (1 / 24 + square * (-1 / 720 + square * (1 / 40320 - square * (1 / 3628800))))
    )
    sine, cosine = 2.0 * sine * cosine, 1.0 - 2.0 * sine * sine
    sine, cosine = 2.0 * sine * cosine, 1.0 - 2.0 * sine * sine
    return -cosine, -sine


def times(left, right):
    return left[0] * right[0] - left[1] * right[1], left[1] * right[0] + left[0] * right[1]


def fold_kernel(recv_ref, lat_ref, table_ref, sum_ref):
    groups = lat_ref.shape[1]
    senders = recv_ref.shape[0] // groups
    rows = lat_ref.shape[2]
    tiles = rows // LANES

    sum_ref[...] = jnp.zeros_like(sum_ref)
    frequency = lax.broadcasted_iota(jnp.int16, (HALF, rows), 0)

    def fold(group, carry):
        both = recv_ref[group * senders].astype(F32)
        for sender in range(1, senders):
            both = both + recv_ref[group * senders + sender].astype(F32)
        c_real, c_imag = (jnp.concatenate([both[k + t : k + t + 1] for t in range(tiles)], axis=1) for k in (0, tiles))
        lat_a = lat_ref[0, pl.ds(group, 1), :]
        lat_b = lat_ref[1, pl.ds(group, 1), :]
        sign_a = jnp.where(lat_a < 0, -1.0, 1.0)
        sign_b = jnp.where(lat_b < 0, -1.0, 1.0)
        at_a = frequency == jnp.abs(lat_a).astype(jnp.int16)
        at_b = frequency == jnp.abs(lat_b).astype(jnp.int16)
        zero = jnp.zeros((), BF16)
        left = jnp.concatenate(
            [
                jnp.where(at_a, value.astype(BF16), zero)
                for value in (c_real, c_real * sign_a, c_imag, c_imag * sign_a)
            ],
            axis=0,
        )
        right = jnp.concatenate(
            [jnp.where(at_b, value.astype(BF16), zero) for value in (jnp.ones_like(sign_b), sign_b)], axis=0
        )
        sum_ref[...] += lax.dot_general(left, right, (((1,), (1,)), ((), ())), preferred_element_type=F32)
        return carry

    lax.fori_loop(0, groups, fold, 0, unroll=8)
    real_even = sum_ref[0:HALF, :]
    real_odd = sum_ref[HALF : 2 * HALF, :]
    imag_even = sum_ref[2 * HALF : 3 * HALF, :]
    imag_odd = sum_ref[3 * HALF : 4 * HALF, :]
    even = lax.broadcasted_iota(jnp.int32, real_even.shape, 1) < HALF
    table = jnp.concatenate(
        [
            jnp.where(even, real_even, -imag_even),
            jnp.where(even, -imag_odd, -real_odd),
            jnp.where(even, imag_even, real_even),
            jnp.where(even, real_odd, -imag_odd),
        ],
        axis=0,
    )
    high = table.astype(BF16).astype(F32)
    low = table - high
    pad = jnp.zeros((4 * HALF, table_ref.shape[1] - 6 * HALF), F32)
    table_ref[...] = jnp.concatenate([high, high, low, pad], axis=1).astype(BF16)


def orbital_kernel(table_ref, pos_ref, out_ref, wave_ref, eight_ref, group_ref, chunk_ref, *, unroll, each):
    groups = out_ref.shape[0]
    chunks = out_ref.shape[1] // 2
    own = RUN // LANES
    runs = chunks // own
    upper = lax.axis_index("band") < lax.axis_size("band") // 2
    walk = lax.axis_index("walk")
    active = walk < each
    out_ref[...] = jnp.zeros_like(out_ref)

    def waves(group, length):
        away = group ^ walk
        for line in range(0, 2 * chunks, 8):
            first = base_wave(pos_ref[away, line : line + 8, :])
            power = (jnp.ones((8, LANES), F32), jnp.zeros((8, LANES), F32))
            for k in range(8):
                for half in range(2):
                    wave_ref[half, group, pl.ds(line * 8 + k, 8, stride=8), :] = power[half]
                power = first if k == 0 else times(power, first)
            for half in range(2):
                eight_ref[half, group, line : line + 8, :] = power[half]
        numbers = pos_ref[away, 2 * chunks : 2 * chunks + runs, :].astype(jnp.int32)
        for run in range(runs):
            number = numbers[run, 0]
            low = jnp.where(upper, 0, number // LANES)
            high = jnp.where(upper, (number + LANES - 1) // LANES, own)
            high = jnp.where(active, high, low)

            for step in range(own):
                group_ref[length + step] = group
                chunk_ref[length + step] = run * own + low + step
            length = length + high - low
        return length

    length = lax.fori_loop(0, groups, waves, 0)

    def basis(entry, axis):
        group, chunk = entry
        line = axis * chunks + chunk
        start = pl.multiple_of(line * 8, 8)
        now = tuple(wave_ref[half, group, pl.ds(start, 8), :] for half in range(2))
        step = tuple(jnp.broadcast_to(eight_ref[half, group, pl.ds(line, 1), :], (8, LANES)) for half in range(2))
        twice = 2.0 * step[0]
        last, now = now, times(now, step)
        cosines, sines = [last[0], now[0]], [last[1], now[1]]
        for _ in range(2, HALF // 8):
            last, now = now, tuple(twice * now[half] - last[half] for half in range(2))
            cosines.append(now[0])
            sines.append(now[1])
        return jnp.concatenate(cosines + sines, axis=0)

    zeros = jnp.zeros((table_ref.shape[1] - 6 * HALF, 2 * LANES), BF16)

    def evaluate(first, size):
        for inner in range(size):
            places = [jnp.minimum(first + inner * 2 + side, length - 1) for side in range(2)]
            entries = [(group_ref[place], chunk_ref[place]) for place in places]
            wave_y = jnp.concatenate([basis(entry, 1) for entry in entries], axis=1)
            high_y = wave_y.astype(BF16)
            low_y = (wave_y - high_y.astype(F32)).astype(BF16)
            weights = jnp.concatenate([high_y, low_y, high_y, zeros], axis=0)
            inside = jnp.dot(table_ref[...], weights, preferred_element_type=F32)
            wave_x = jnp.concatenate([basis(entry, 0) for entry in entries], axis=1)
            for half in range(2):
                value = jnp.sum(inside[half * 2 * HALF : (half + 1) * 2 * HALF, :] * wave_x, axis=0, keepdims=True)
                for side, (group, chunk) in enumerate(entries):
                    out_ref[group, pl.ds(half * chunks + chunk, 1), :] = value[:, side * LANES : (side + 1) * LANES]

    def many(index, carry):
        evaluate(index * 2 * unroll, unroll)
        return carry

    def few(index, carry):
        evaluate(length // (2 * unroll) * 2 * unroll + index * 2 * rest, rest)
        return carry

    rest = 4
    lax.fori_loop(0, length // (2 * unroll), many, 0)
    lax.fori_loop(0, (length % (2 * unroll) + 2 * rest - 1) // (2 * rest), few, 0)


def gradient_kernel(target_ref, feature_ref, net_hbm, out_ref, net_ref, sem, *, scale):
    copy = pltpu.make_async_copy(net_hbm, net_ref, sem)
    copy.start()
    chunks = feature_ref.shape[0] // LANES
    slots = out_ref.shape[0] // 2
    upper = lax.axis_index("band") < lax.axis_size("band") // 2
    targets = [
        jnp.concatenate(
            [target_ref[pl.ds(half * chunks + chunk, slots, stride=2 * chunks), :] for chunk in range(chunks)], axis=1
        )
        for half in range(2)
    ]
    copy.wait()
    mine = net_ref[2 * slots : 2 * slots + 1, :] == jnp.where(upper, 1.0, 0.0)
    parts = []
    for half in range(2):
        scaled = (net_ref[half * slots : (half + 1) * slots, :] - targets[half]) * scale
        parts.append(jnp.where(mine, scaled, 0.0))
    spread = jnp.concatenate(parts, axis=0)
    pieces = jnp.concatenate([piece.astype(F32) for piece in split3(spread)], axis=0).astype(BF16)
    total = jnp.dot(pieces, feature_ref[...], preferred_element_type=F32)
    height = out_ref.shape[0]
    out_ref[...] = total[:height] + total[height : 2 * height] + total[2 * height :]


def call(kernel, out, scratch=(), mebibytes=16, **more):
    return pl.pallas_call(
        kernel,
        out_shape=out,
        **more,
        scratch_shapes=list(scratch),
        interpret=INTERPRET,
        compiler_params=pltpu.CompilerParams(vmem_limit_bytes=mebibytes * 1024 * 1024),
    )


def local(positions, coefficients, lattice, spin_labels, occupied, features, orbital_head):
    walk_count = lax.axis_size("walk")
    band_count = lax.axis_size("band")
    band_index = lax.axis_index("band")
    devices = walk_count * band_count
    rows = coefficients.shape[1]
    count = positions.shape[1]
    orbitals = occupied.shape[0] * occupied.shape[1]
    each = orbitals // band_count

    chunks = count // LANES
    anywhere = pl.BlockSpec(memory_space=pltpu.HBM)
    picked = call(
        pick_kernel,
        jax.ShapeDtypeStruct((devices * BLOCK, LANES), BF16),
        [
            pltpu.VMEM(coefficients.shape, BF16),
            pltpu.SMEM(occupied.shape, jnp.int32),
            pltpu.VMEM((devices * BLOCK, LANES), F32),
            pltpu.SemaphoreType.DMA((3,)),
        ],
        in_specs=[anywhere, anywhere],
    )(pltpu.with_memory_space_constraint(coefficients, pltpu.HBM), pltpu.with_memory_space_constraint(occupied, pltpu.HBM))
    picked, positions = lax.optimization_barrier((picked, positions))
    received = lax.all_to_all(picked.reshape(devices, BLOCK, LANES), ("walk", "band"), 0, 0, tiled=True)
    ordered, slot, up = call(
        order_kernel,
        (
            jax.ShapeDtypeStruct((2 * chunks + 8, LANES), F32),
            jax.ShapeDtypeStruct((count // RUN, RUN), F32),
            jax.ShapeDtypeStruct((1, count), F32),
        ),
    )(positions, spin_labels.reshape(chunks, LANES))
    everyone = ordered[None]
    for flips in ((1,), tuple(range(2, walk_count, 2))):
        moved = [lax.ppermute(everyone, "walk", [(k, k ^ flip) for k in range(walk_count)]) for flip in flips]
        everyone = jnp.concatenate([everyone, *moved], axis=0)
    table = call(
        fold_kernel, jax.ShapeDtypeStruct((4 * HALF, 512), BF16), [pltpu.VMEM((4 * HALF, 2 * HALF), F32)]
    )(received, lattice.reshape(2, walk_count, rows))
    values = call(
        functools.partial(orbital_kernel, unroll=12, each=each),
        jax.ShapeDtypeStruct((walk_count, 2 * chunks, LANES), F32),
        [
            pltpu.VMEM((2, walk_count, 16 * chunks, LANES), F32),
            pltpu.VMEM((2, walk_count, 2 * chunks, LANES), F32),
            pltpu.SMEM((walk_count * chunks + RUN // LANES,), jnp.int32),
            pltpu.SMEM((walk_count * chunks + RUN // LANES,), jnp.int32),
        ],
        mebibytes=24,
    )(table, everyone)
    target = lax.all_to_all(values, "walk", 0, 0, tiled=True).reshape(-1, LANES)

    spins = occupied.shape[0]
    per_spin = band_count // spins
    spin = band_index // per_spin
    columns = orbital_head.reshape(orbital_head.shape[0], spins, 2, per_spin, each)
    columns = lax.dynamic_index_in_dim(columns, spin, 1, keepdims=False)
    columns = lax.dynamic_index_in_dim(columns, band_index % per_spin, 2, keepdims=False)
    columns = jnp.transpose(columns, (1, 2, 0))
    columns = jnp.pad(columns, ((0, 0), (0, walk_count - each), (0, 0))).reshape(2 * walk_count, -1)
    sorted_features, net = call(
        sort_kernel,
        (jax.ShapeDtypeStruct(features.shape, BF16), jax.ShapeDtypeStruct((2 * walk_count + 8, count), F32)),
    )(slot, features, columns, up)
    net = pltpu.with_memory_space_constraint(net, pltpu.HBM)
    walkers = walk_count * count // orbitals
    hidden = features.shape[1]
    in_vmem = pl.BlockSpec(memory_space=pltpu.VMEM)
    own = call(
        functools.partial(gradient_kernel, scale=1.0 / walkers),
        jax.ShapeDtypeStruct((2 * walk_count, hidden), F32),
        [pltpu.VMEM(net.shape, F32), pltpu.SemaphoreType.DMA],
        in_specs=[in_vmem, in_vmem, anywhere],
    )(target, sorted_features, net)
    own = own.reshape(2, walk_count, hidden)[:, :each].reshape(-1, LANES)
    own = own + lax.ppermute(own, "walk", [(k, k ^ 1) for k in range(walk_count)])
    chips = walk_count // 2
    shares = lax.all_to_all(
        jnp.broadcast_to(own, (chips, *own.shape)),
        "walk",
        0,
        0,
        axis_index_groups=[[2 * chip + core for chip in range(chips)] for core in range(2)],
        tiled=True,
    )
    summed = jnp.sum(shares, axis=0)
    whole = lax.all_to_all(jnp.broadcast_to(summed, (band_count, *own.shape)), "band", 0, 0, tiled=True)
    whole = whole.reshape(spins, per_spin, 2, each, hidden)
    return jnp.transpose(whole, (4, 0, 2, 1, 3)).reshape(hidden, 2 * orbitals)


def solution(mesh):
    return jax.shard_map(
        local,
        mesh=mesh,
        in_specs=(
            P(None, "walk"),
            P(None, "walk", "band"),
            P(),
            P("walk"),
            P(),
            P("walk", None),
            P(),
        ),
        out_specs=P(),
        check_vma=False,
    )
```

```python
import functools

import jax
import jax.numpy as jnp
from jax import lax
from jax.experimental import pallas as pl
from jax.experimental.pallas import tpu as pltpu
from jax.sharding import PartitionSpec as P


INTERPRET = False
F32 = jnp.float32
BF16 = jnp.bfloat16
PI = 3.141592653589793
BLOCK = 24
RUN = 1024
HALF = 80
LANES = 128


def split3(value):
    high = value.astype(BF16)
    rest = value - high.astype(F32)
    middle = rest.astype(BF16)
    low = (rest - middle.astype(F32)).astype(BF16)
    return high, middle, low


def pick_kernel(coef_hbm, occ_hbm, out_ref, coef_ref, occ_ref, stage_ref, sems):
    copies = [pltpu.make_async_copy(occ_hbm, occ_ref, sems.at[2])]
    copies += [pltpu.make_async_copy(coef_hbm.at[part], coef_ref.at[part], sems.at[part]) for part in range(2)]
    for copy in copies:
        copy.start()
    _, rows, bands = coef_ref.shape
    spins, per_spin = occ_ref.shape
    devices = stage_ref.shape[0] // BLOCK
    senders = lax.axis_size("band")
    each = spins * per_spin // senders
    tiles = rows // LANES
    base = lax.axis_index("band") * bands
    for row in range(2 * tiles, BLOCK):
        stage_ref[pl.ds(row, devices, stride=BLOCK), :] = jnp.zeros((devices, LANES), F32)
    line = lax.broadcasted_iota(jnp.int32, (8, bands), 0)
    lane = lax.broadcasted_iota(jnp.int32, (8, bands), 1) + base
    copies[0].wait()
    picks = []
    for group in range(devices // senders):
        wanted = jnp.full((8, bands), -1, jnp.int32)
        if group < each:
            for sender in range(senders):
                orbital = sender * each + group
                wanted = jnp.where(line == sender, occ_ref[orbital // per_spin, orbital % per_spin], wanted)
        picks.append(jnp.where(lane == wanted, 1.0, 0.0))
    pick = jnp.concatenate(picks, axis=0).astype(BF16)
    for part in range(2):
        copies[1 + part].wait()
        taken = lax.dot_general(
            pick, coef_ref[part], (((1,), (1,)), ((), ())), preferred_element_type=F32
        )
        for tile in range(tiles):
            stage_ref[pl.ds(part * tiles + tile, devices, stride=BLOCK), :] = taken[:, tile * LANES : (tile + 1) * LANES]
    out_ref[...] = stage_ref[...].astype(BF16)


def order_kernel(pos_ref, label_ref, out_ref, slot_ref, up_ref):
    chunks = label_ref.shape[0]
    own = RUN // LANES
    runs = chunks // own
    up = label_ref[...] == 0
    ones = jnp.where(up, 1.0, 0.0)
    row = lax.broadcasted_iota(jnp.int32, (LANES, LANES), 0)
    column = lax.broadcasted_iota(jnp.int32, (LANES, LANES), 1)
    until = jnp.where(row <= column, 1.0, 0.0).astype(BF16)
    inside = jnp.dot(ones.astype(BF16), until, preferred_element_type=F32)
    whole = jnp.broadcast_to(inside[:, LANES - 1 : LANES], inside.shape).astype(BF16)
    row = lax.broadcasted_iota(jnp.int32, (chunks, chunks), 0)
    column = lax.broadcasted_iota(jnp.int32, (chunks, chunks), 1)
    same = jnp.where(row // own == column // own, 1.0, 0.0)
    before = jnp.where(column < row, same, 0.0).astype(BF16)
    rank = inside + jnp.dot(before, whole, preferred_element_type=F32)
    total = jnp.dot(same.astype(BF16), whole, preferred_element_type=F32)
    place = (
        lax.broadcasted_iota(jnp.int32, rank.shape, 0) % own * LANES + lax.broadcasted_iota(jnp.int32, rank.shape, 1)
    ).astype(F32)
    slot = jnp.where(up, rank - 1.0, total + place - rank)
    first = jnp.where(place < total, 1.0, 0.0)
    up_ref[...] = jnp.concatenate([first[chunk : chunk + 1, :] for chunk in range(chunks)], axis=1)
    parts = jnp.concatenate([part.astype(F32) for part in split3(pos_ref[...])], axis=0).astype(BF16)
    here = lax.broadcasted_iota(jnp.int16, (RUN, RUN), 0)
    for run in range(runs):
        line = jnp.concatenate([slot[run * own + k : run * own + k + 1, :] for k in range(own)], axis=1)
        slot_ref[run : run + 1, :] = line
        move = jnp.where(here == line.astype(jnp.int32).astype(jnp.int16), jnp.ones((), BF16), jnp.zeros((), BF16))
        moved = lax.dot_general(
            parts[:, run * RUN : (run + 1) * RUN], move, (((1,), (1,)), ((), ())), preferred_element_type=F32
        )
        moved = moved[0:2] + moved[2:4] + moved[4:6]
        for axis in range(2):
            for k in range(own):
                at = axis * chunks + run * own + k
                out_ref[at : at + 1, :] = moved[axis : axis + 1, k * LANES : (k + 1) * LANES]
        out_ref[2 * chunks + run : 2 * chunks + run + 1, :] = total[run * own : run * own + 1, :]
    out_ref[2 * chunks + runs :, :] = jnp.zeros((out_ref.shape[0] - 2 * chunks - runs, LANES), F32)


def sort_kernel(slot_ref, feature_ref, head_ref, up_ref, out_ref, net_ref):
    here = lax.broadcasted_iota(jnp.int32, (RUN, RUN), 0).astype(F32)
    for run in range(slot_ref.shape[0]):
        move = jnp.where(here == slot_ref[run : run + 1, :], 1.0, 0.0).astype(BF16)
        moved = jnp.dot(move, feature_ref[run * RUN : (run + 1) * RUN, :], preferred_element_type=F32).astype(BF16)
        out_ref[run * RUN : (run + 1) * RUN, :] = moved
        net_ref[: head_ref.shape[0], run * RUN : (run + 1) * RUN] = lax.dot_general(
            head_ref[...], moved, (((1,), (1,)), ((), ())), preferred_element_type=F32
        )
    tail = net_ref.shape[0] - head_ref.shape[0]
    net_ref[head_ref.shape[0] :, :] = jnp.broadcast_to(up_ref[...], (tail, up_ref.shape[1]))


def base_wave(turns):
    quarter = (turns - 0.5) * (0.5 * PI)
    square = quarter * quarter
    sine = quarter * (
        1.0 + square * (-1 / 6 + square * (1 / 120 + square * (-1 / 5040 + square * (1 / 362880))))
    )
    cosine = 1.0 + square * (
        -1 / 2 + square * (1 / 24 + square * (-1 / 720 + square * (1 / 40320 - square * (1 / 3628800))))
    )
    sine, cosine = 2.0 * sine * cosine, 1.0 - 2.0 * sine * sine
    sine, cosine = 2.0 * sine * cosine, 1.0 - 2.0 * sine * sine
    return -cosine, -sine


def times(left, right):
    return left[0] * right[0] - left[1] * right[1], left[1] * right[0] + left[0] * right[1]


def fold_kernel(recv_ref, lat_ref, table_ref, sum_ref):
    groups = lat_ref.shape[1]
    senders = recv_ref.shape[0] // groups
    rows = lat_ref.shape[2]
    tiles = rows // LANES

    sum_ref[...] = jnp.zeros_like(sum_ref)
    frequency = lax.broadcasted_iota(jnp.int16, (HALF, rows), 0)

    def fold(group, carry):
        both = recv_ref[group * senders].astype(F32)
        for sender in range(1, senders):
            both = both + recv_ref[group * senders + sender].astype(F32)
        c_real, c_imag = (jnp.concatenate([both[k + t : k + t + 1] for t in range(tiles)], axis=1) for k in (0, tiles))
        lat_a = lat_ref[0, pl.ds(group, 1), :]
        lat_b = lat_ref[1, pl.ds(group, 1), :]
        sign_a = jnp.where(lat_a < 0, -1.0, 1.0)
        sign_b = jnp.where(lat_b < 0, -1.0, 1.0)
        at_a = frequency == jnp.abs(lat_a).astype(jnp.int16)
        at_b = frequency == jnp.abs(lat_b).astype(jnp.int16)
        zero = jnp.zeros((), BF16)
        left = jnp.concatenate(
            [
                jnp.where(at_a, value.astype(BF16), zero)
                for value in (c_real, c_real * sign_a, c_imag, c_imag * sign_a)
            ],
            axis=0,
        )
        right = jnp.concatenate(
            [jnp.where(at_b, value.astype(BF16), zero) for value in (jnp.ones_like(sign_b), sign_b)], axis=0
        )
        sum_ref[...] += lax.dot_general(left, right, (((1,), (1,)), ((), ())), preferred_element_type=F32)
        return carry

    lax.fori_loop(0, groups, fold, 0, unroll=8)
    real_even = sum_ref[0:HALF, :]
    real_odd = sum_ref[HALF : 2 * HALF, :]
    imag_even = sum_ref[2 * HALF : 3 * HALF, :]
    imag_odd = sum_ref[3 * HALF : 4 * HALF, :]
    even = lax.broadcasted_iota(jnp.int32, real_even.shape, 1) < HALF
    table = jnp.concatenate(
        [
            jnp.where(even, real_even, -imag_even),
            jnp.where(even, -imag_odd, -real_odd),
            jnp.where(even, imag_even, real_even),
            jnp.where(even, real_odd, -imag_odd),
        ],
        axis=0,
    )
    high = table.astype(BF16).astype(F32)
    low = table - high
    pad = jnp.zeros((4 * HALF, table_ref.shape[1] - 6 * HALF), F32)
    table_ref[...] = jnp.concatenate([high, high, low, pad], axis=1).astype(BF16)


def orbital_kernel(table_ref, pos_ref, out_ref, wave_ref, eight_ref, list_ref, *, unroll, each):
    groups = out_ref.shape[0]
    chunks = out_ref.shape[1] // 2
    own = RUN // LANES
    runs = chunks // own
    upper = lax.axis_index("band") < lax.axis_size("band") // 2
    walk = lax.axis_index("walk")
    active = walk < each
    out_ref[...] = jnp.zeros_like(out_ref)

    def waves(group, length):
        away = group ^ walk
        for line in range(0, 2 * chunks, 8):
            first = base_wave(pos_ref[away, line : line + 8, :])
            power = (jnp.ones((8, LANES), F32), jnp.zeros((8, LANES), F32))
            for k in range(8):
                for half in range(2):
                    wave_ref[half, group, pl.ds(line * 8 + k, 8, stride=8), :] = power[half]
                power = first if k == 0 else times(power, first)
            for half in range(2):
                eight_ref[half, group, line : line + 8, :] = power[half]
        numbers = pos_ref[away, 2 * chunks : 2 * chunks + runs, :].astype(jnp.int32)
        for run in range(runs):
            number = numbers[run, 0]
            low = jnp.where(upper, 0, number // LANES)
            high = jnp.where(upper, (number + LANES - 1) // LANES, own)
            high = jnp.where(active, high, low)

            for step in range(own):
                list_ref[length + step] = group * LANES + run * own + low + step
            length = length + high - low
        return length

    length = lax.fori_loop(0, groups, waves, 0, unroll=2)

    def basis(entry, axis):
        group, chunk = entry
        line = axis * chunks + chunk
        start = pl.multiple_of(line * 8, 8)
        now = tuple(wave_ref[half, group, pl.ds(start, 8), :] for half in range(2))
        step = tuple(jnp.broadcast_to(eight_ref[half, group, pl.ds(line, 1), :], (8, LANES)) for half in range(2))
        twice = 2.0 * step[0]
        last, now = now, times(now, step)
        cosines, sines = [last[0], now[0]], [last[1], now[1]]
        for _ in range(2, HALF // 8):
            last, now = now, tuple(twice * now[half] - last[half] for half in range(2))
            cosines.append(now[0])
            sines.append(now[1])
        return jnp.concatenate(cosines + sines, axis=0)

    zeros = jnp.zeros((table_ref.shape[1] - 6 * HALF, 2 * LANES), BF16)

    def evaluate(first, size):
        for inner in range(size):
            places = [jnp.minimum(first + inner * 2 + side, length - 1) for side in range(2)]
            entries = [(list_ref[place] >> 7, list_ref[place] & (LANES - 1)) for place in places]
            wave_y = jnp.concatenate([basis(entry, 1) for entry in entries], axis=1)
            high_y = wave_y.astype(BF16)
            low_y = (wave_y - high_y.astype(F32)).astype(BF16)
            weights = jnp.concatenate([high_y, low_y, high_y, zeros], axis=0)
            inside = jnp.dot(table_ref[...], weights, preferred_element_type=F32)
            wave_x = jnp.concatenate([basis(entry, 0) for entry in entries], axis=1)
            for half in range(2):
                value = jnp.sum(inside[half * 2 * HALF : (half + 1) * 2 * HALF, :] * wave_x, axis=0, keepdims=True)
                for side, (group, chunk) in enumerate(entries):
                    out_ref[group, pl.ds(half * chunks + chunk, 1), :] = value[:, side * LANES : (side + 1) * LANES]

    def many(index, carry):
        evaluate(index * 2 * unroll, unroll)
        return carry

    def few(index, carry):
        evaluate(length // (2 * unroll) * 2 * unroll + index * 2 * rest, rest)
        return carry

    rest = 4
    lax.fori_loop(0, length // (2 * unroll), many, 0)
    lax.fori_loop(0, (length % (2 * unroll) + 2 * rest - 1) // (2 * rest), few, 0)


def gradient_kernel(target_ref, feature_ref, net_hbm, out_ref, net_ref, sem, *, scale):
    copy = pltpu.make_async_copy(net_hbm, net_ref, sem)
    copy.start()
    chunks = feature_ref.shape[0] // LANES
    slots = out_ref.shape[0] // 2
    upper = lax.axis_index("band") < lax.axis_size("band") // 2
    targets = [
        jnp.concatenate(
            [target_ref[pl.ds(half * chunks + chunk, slots, stride=2 * chunks), :] for chunk in range(chunks)], axis=1
        )
        for half in range(2)
    ]
    copy.wait()
    mine = net_ref[2 * slots : 2 * slots + 1, :] == jnp.where(upper, 1.0, 0.0)
    parts = []
    for half in range(2):
        scaled = (net_ref[half * slots : (half + 1) * slots, :] - targets[half]) * scale
        parts.append(jnp.where(mine, scaled, 0.0))
    spread = jnp.concatenate(parts, axis=0)
    pieces = jnp.concatenate([piece.astype(F32) for piece in split3(spread)], axis=0).astype(BF16)
    total = jnp.dot(pieces, feature_ref[...], preferred_element_type=F32)
    height = out_ref.shape[0]
    out_ref[...] = total[:height] + total[height : 2 * height] + total[2 * height :]


def call(kernel, out, scratch=(), mebibytes=16, **more):
    return pl.pallas_call(
        kernel,
        out_shape=out,
        **more,
        scratch_shapes=list(scratch),
        interpret=INTERPRET,
        compiler_params=pltpu.CompilerParams(vmem_limit_bytes=mebibytes * 1024 * 1024),
    )


def local(positions, coefficients, lattice, spin_labels, occupied, features, orbital_head):
    walk_count = lax.axis_size("walk")
    band_count = lax.axis_size("band")
    band_index = lax.axis_index("band")
    devices = walk_count * band_count
    rows = coefficients.shape[1]
    count = positions.shape[1]
    orbitals = occupied.shape[0] * occupied.shape[1]
    each = orbitals // band_count

    chunks = count // LANES
    anywhere = pl.BlockSpec(memory_space=pltpu.HBM)
    picked = call(
        pick_kernel,
        jax.ShapeDtypeStruct((devices * BLOCK, LANES), BF16),
        [
            pltpu.VMEM(coefficients.shape, BF16),
            pltpu.SMEM(occupied.shape, jnp.int32),
            pltpu.VMEM((devices * BLOCK, LANES), F32),
            pltpu.SemaphoreType.DMA((3,)),
        ],
        in_specs=[anywhere, anywhere],
    )(pltpu.with_memory_space_constraint(coefficients, pltpu.HBM), pltpu.with_memory_space_constraint(occupied, pltpu.HBM))
    picked, positions = lax.optimization_barrier((picked, positions))
    received = lax.all_to_all(picked.reshape(devices, BLOCK, LANES), ("walk", "band"), 0, 0, tiled=True)
    ordered, slot, up = call(
        order_kernel,
        (
            jax.ShapeDtypeStruct((2 * chunks + 8, LANES), F32),
            jax.ShapeDtypeStruct((count // RUN, RUN), F32),
            jax.ShapeDtypeStruct((1, count), F32),
        ),
    )(positions, spin_labels.reshape(chunks, LANES))
    everyone = ordered[None]
    for flips in ((1,), tuple(range(2, walk_count, 2))):
        moved = [lax.ppermute(everyone, "walk", [(k, k ^ flip) for k in range(walk_count)]) for flip in flips]
        everyone = jnp.concatenate([everyone, *moved], axis=0)
    table = call(
        fold_kernel, jax.ShapeDtypeStruct((4 * HALF, 512), BF16), [pltpu.VMEM((4 * HALF, 2 * HALF), F32)]
    )(received, lattice.reshape(2, walk_count, rows))
    values = call(
        functools.partial(orbital_kernel, unroll=12, each=each),
        jax.ShapeDtypeStruct((walk_count, 2 * chunks, LANES), F32),
        [
            pltpu.VMEM((2, walk_count, 16 * chunks, LANES), F32),
            pltpu.VMEM((2, walk_count, 2 * chunks, LANES), F32),
            pltpu.SMEM((walk_count * chunks + RUN // LANES,), jnp.int32),
        ],
        mebibytes=24,
    )(table, everyone)
    target = lax.all_to_all(values, "walk", 0, 0, tiled=True).reshape(-1, LANES)

    spins = occupied.shape[0]
    per_spin = band_count // spins
    spin = band_index // per_spin
    columns = orbital_head.reshape(orbital_head.shape[0], spins, 2, per_spin, each)
    columns = lax.dynamic_index_in_dim(columns, spin, 1, keepdims=False)
    columns = lax.dynamic_index_in_dim(columns, band_index % per_spin, 2, keepdims=False)
    columns = jnp.transpose(columns, (1, 2, 0))
    columns = jnp.pad(columns, ((0, 0), (0, walk_count - each), (0, 0))).reshape(2 * walk_count, -1)
    sorted_features, net = call(
        sort_kernel,
        (jax.ShapeDtypeStruct(features.shape, BF16), jax.ShapeDtypeStruct((2 * walk_count + 8, count), F32)),
    )(slot, features, columns, up)
    net = pltpu.with_memory_space_constraint(net, pltpu.HBM)
    walkers = walk_count * count // orbitals
    hidden = features.shape[1]
    in_vmem = pl.BlockSpec(memory_space=pltpu.VMEM)
    own = call(
        functools.partial(gradient_kernel, scale=1.0 / walkers),
        jax.ShapeDtypeStruct((2 * walk_count, hidden), F32),
        [pltpu.VMEM(net.shape, F32), pltpu.SemaphoreType.DMA],
        in_specs=[in_vmem, in_vmem, anywhere],
    )(target, sorted_features, net)
    own = own.reshape(2, walk_count, hidden)[:, :each].reshape(-1, LANES)
    own = own + lax.ppermute(own, "walk", [(k, k ^ 1) for k in range(walk_count)])
    chips = walk_count // 2
    shares = lax.all_to_all(
        jnp.broadcast_to(own, (chips, *own.shape)),
        "walk",
        0,
        0,
        axis_index_groups=[[2 * chip + core for chip in range(chips)] for core in range(2)],
        tiled=True,
    )
    summed = jnp.sum(shares, axis=0)
    whole = lax.all_to_all(jnp.broadcast_to(summed, (band_count, *own.shape)), "band", 0, 0, tiled=True)
    whole = whole.reshape(spins, per_spin, 2, each, hidden)
    return jnp.transpose(whole, (4, 0, 2, 1, 3)).reshape(hidden, 2 * orbitals)


def solution(mesh):
    return jax.shard_map(
        local,
        mesh=mesh,
        in_specs=(
            P(None, "walk"),
            P(None, "walk", "band"),
            P(),
            P("walk"),
            P(),
            P("walk", None),
            P(),
        ),
        out_specs=P(),
        check_vma=False,
    )
```

```python
import functools

import jax
import jax.numpy as jnp
from jax import lax
from jax.experimental import pallas as pl
from jax.experimental.pallas import tpu as pltpu
from jax.sharding import PartitionSpec as P


INTERPRET = False
F32 = jnp.float32
BF16 = jnp.bfloat16
PI = 3.141592653589793
BLOCK = 24
RUN = 1024
HALF = 80
LANES = 128


def split3(value):
    high = value.astype(BF16)
    rest = value - high.astype(F32)
    middle = rest.astype(BF16)
    low = (rest - middle.astype(F32)).astype(BF16)
    return high, middle, low


def pick_kernel(coef_hbm, occ_hbm, out_ref, coef_ref, occ_ref, stage_ref, sems):
    copies = [pltpu.make_async_copy(occ_hbm, occ_ref, sems.at[2])]
    copies += [pltpu.make_async_copy(coef_hbm.at[part], coef_ref.at[part], sems.at[part]) for part in range(2)]
    for copy in copies:
        copy.start()
    _, rows, bands = coef_ref.shape
    spins, per_spin = occ_ref.shape
    devices = stage_ref.shape[0] // BLOCK
    senders = lax.axis_size("band")
    each = spins * per_spin // senders
    tiles = rows // LANES
    base = lax.axis_index("band") * bands
    for row in range(2 * tiles, BLOCK):
        stage_ref[pl.ds(row, devices, stride=BLOCK), :] = jnp.zeros((devices, LANES), F32)
    line = lax.broadcasted_iota(jnp.int32, (8, bands), 0)
    lane = lax.broadcasted_iota(jnp.int32, (8, bands), 1) + base
    copies[0].wait()
    picks = []
    for group in range(devices // senders):
        wanted = jnp.full((8, bands), -1, jnp.int32)
        if group < each:
            for sender in range(senders):
                orbital = sender * each + group
                wanted = jnp.where(line == sender, occ_ref[orbital // per_spin, orbital % per_spin], wanted)
        picks.append(jnp.where(lane == wanted, 1.0, 0.0))
    pick = jnp.concatenate(picks, axis=0).astype(BF16)
    for part in range(2):
        copies[1 + part].wait()
        taken = lax.dot_general(
            pick, coef_ref[part], (((1,), (1,)), ((), ())), preferred_element_type=F32
        )
        for tile in range(tiles):
            stage_ref[pl.ds(part * tiles + tile, devices, stride=BLOCK), :] = taken[:, tile * LANES : (tile + 1) * LANES]
    out_ref[...] = stage_ref[...].astype(BF16)


def order_kernel(pos_ref, label_ref, out_ref, slot_ref, up_ref):
    chunks = label_ref.shape[0]
    own = RUN // LANES
    runs = chunks // own
    up = label_ref[...] == 0
    ones = jnp.where(up, 1.0, 0.0)
    row = lax.broadcasted_iota(jnp.int32, (LANES, LANES), 0)
    column = lax.broadcasted_iota(jnp.int32, (LANES, LANES), 1)
    until = jnp.where(row <= column, 1.0, 0.0).astype(BF16)
    inside = jnp.dot(ones.astype(BF16), until, preferred_element_type=F32)
    whole = jnp.broadcast_to(inside[:, LANES - 1 : LANES], inside.shape).astype(BF16)
    row = lax.broadcasted_iota(jnp.int32, (chunks, chunks), 0)
    column = lax.broadcasted_iota(jnp.int32, (chunks, chunks), 1)
    same = jnp.where(row // own == column // own, 1.0, 0.0)
    before = jnp.where(column < row, same, 0.0).astype(BF16)
    rank = inside + jnp.dot(before, whole, preferred_element_type=F32)
    total = jnp.dot(same.astype(BF16), whole, preferred_element_type=F32)
    place = (
        lax.broadcasted_iota(jnp.int32, rank.shape, 0) % own * LANES + lax.broadcasted_iota(jnp.int32, rank.shape, 1)
    ).astype(F32)
    slot = jnp.where(up, rank - 1.0, total + place - rank)
    first = jnp.where(place < total, 1.0, 0.0)
    up_ref[...] = jnp.concatenate([first[chunk : chunk + 1, :] for chunk in range(chunks)], axis=1)
    parts = jnp.concatenate([part.astype(F32) for part in split3(pos_ref[...])], axis=0).astype(BF16)
    here = lax.broadcasted_iota(jnp.int16, (RUN, RUN), 0)
    for run in range(runs):
        line = jnp.concatenate([slot[run * own + k : run * own + k + 1, :] for k in range(own)], axis=1)
        slot_ref[run : run + 1, :] = line
        move = jnp.where(here == line.astype(jnp.int32).astype(jnp.int16), jnp.ones((), BF16), jnp.zeros((), BF16))
        moved = lax.dot_general(
            parts[:, run * RUN : (run + 1) * RUN], move, (((1,), (1,)), ((), ())), preferred_element_type=F32
        )
        moved = moved[0:2] + moved[2:4] + moved[4:6]
        for axis in range(2):
            for k in range(own):
                at = axis * chunks + run * own + k
                out_ref[at : at + 1, :] = moved[axis : axis + 1, k * LANES : (k + 1) * LANES]
        out_ref[2 * chunks + run : 2 * chunks + run + 1, :] = total[run * own : run * own + 1, :]
    out_ref[2 * chunks + runs :, :] = jnp.zeros((out_ref.shape[0] - 2 * chunks - runs, LANES), F32)


def sort_kernel(slot_ref, feature_ref, head_ref, up_ref, out_ref, net_ref):
    here = lax.broadcasted_iota(jnp.int32, (RUN, RUN), 0).astype(F32)
    for run in range(slot_ref.shape[0]):
        move = jnp.where(here == slot_ref[run : run + 1, :], 1.0, 0.0).astype(BF16)
        moved = jnp.dot(move, feature_ref[run * RUN : (run + 1) * RUN, :], preferred_element_type=F32).astype(BF16)
        out_ref[run * RUN : (run + 1) * RUN, :] = moved
        net_ref[: head_ref.shape[0], run * RUN : (run + 1) * RUN] = lax.dot_general(
            head_ref[...], moved, (((1,), (1,)), ((), ())), preferred_element_type=F32
        )
    tail = net_ref.shape[0] - head_ref.shape[0]
    net_ref[head_ref.shape[0] :, :] = jnp.broadcast_to(up_ref[...], (tail, up_ref.shape[1]))


def base_wave(turns):
    quarter = (turns - 0.5) * (0.5 * PI)
    square = quarter * quarter
    sine = quarter * (
        1.0 + square * (-1 / 6 + square * (1 / 120 + square * (-1 / 5040 + square * (1 / 362880))))
    )
    cosine = 1.0 + square * (
        -1 / 2 + square * (1 / 24 + square * (-1 / 720 + square * (1 / 40320 - square * (1 / 3628800))))
    )
    sine, cosine = 2.0 * sine * cosine, 1.0 - 2.0 * sine * sine
    sine, cosine = 2.0 * sine * cosine, 1.0 - 2.0 * sine * sine
    return -cosine, -sine


def times(left, right):
    return left[0] * right[0] - left[1] * right[1], left[1] * right[0] + left[0] * right[1]


def fold_kernel(recv_ref, lat_ref, table_ref, sum_ref):
    groups = lat_ref.shape[1]
    senders = recv_ref.shape[0] // groups
    rows = lat_ref.shape[2]
    tiles = rows // LANES

    sum_ref[...] = jnp.zeros_like(sum_ref)
    frequency = lax.broadcasted_iota(jnp.int16, (HALF, rows), 0)

    def fold(group, carry):
        both = recv_ref[group * senders].astype(F32)
        for sender in range(1, senders):
            both = both + recv_ref[group * senders + sender].astype(F32)
        c_real, c_imag = (jnp.concatenate([both[k + t : k + t + 1] for t in range(tiles)], axis=1) for k in (0, tiles))
        lat_a = lat_ref[0, pl.ds(group, 1), :]
        lat_b = lat_ref[1, pl.ds(group, 1), :]
        sign_a = jnp.where(lat_a < 0, -1.0, 1.0)
        sign_b = jnp.where(lat_b < 0, -1.0, 1.0)
        at_a = frequency == jnp.abs(lat_a).astype(jnp.int16)
        at_b = frequency == jnp.abs(lat_b).astype(jnp.int16)
        zero = jnp.zeros((), BF16)
        left = jnp.concatenate(
            [
                jnp.where(at_a, value.astype(BF16), zero)
                for value in (c_real, c_real * sign_a, c_imag, c_imag * sign_a)
            ],
            axis=0,
        )
        right = jnp.concatenate(
            [jnp.where(at_b, value.astype(BF16), zero) for value in (jnp.ones_like(sign_b), sign_b)], axis=0
        )
        sum_ref[...] += lax.dot_general(left, right, (((1,), (1,)), ((), ())), preferred_element_type=F32)
        return carry

    lax.fori_loop(0, groups, fold, 0, unroll=8)
    real_even = sum_ref[0:HALF, :]
    real_odd = sum_ref[HALF : 2 * HALF, :]
    imag_even = sum_ref[2 * HALF : 3 * HALF, :]
    imag_odd = sum_ref[3 * HALF : 4 * HALF, :]
    even = lax.broadcasted_iota(jnp.int32, real_even.shape, 1) < HALF
    table = jnp.concatenate(
        [
            jnp.where(even, real_even, -imag_even),
            jnp.where(even, -imag_odd, -real_odd),
            jnp.where(even, imag_even, real_even),
            jnp.where(even, real_odd, -imag_odd),
        ],
        axis=0,
    )
    high = table.astype(BF16).astype(F32)
    low = table - high
    pad = jnp.zeros((4 * HALF, table_ref.shape[1] - 6 * HALF), F32)
    table_ref[...] = jnp.concatenate([high, high, low, pad], axis=1).astype(BF16)


def orbital_kernel(table_ref, pos_ref, out_ref, wave_ref, eight_ref, list_ref, *, unroll, each):
    groups = out_ref.shape[0]
    chunks = out_ref.shape[1] // 2
    own = RUN // LANES
    runs = chunks // own
    upper = lax.axis_index("band") < lax.axis_size("band") // 2
    walk = lax.axis_index("walk")
    active = walk < each
    out_ref[...] = jnp.zeros_like(out_ref)

    def waves(group, length):
        flip = group ^ walk
        away = ((groups - (flip & ~1)) & (groups - 1)) + (flip & 1)
        for line in range(0, 2 * chunks, 8):
            first = base_wave(pos_ref[away, line : line + 8, :])
            power = (jnp.ones((8, LANES), F32), jnp.zeros((8, LANES), F32))
            for k in range(8):
                for half in range(2):
                    wave_ref[half, group, pl.ds(line * 8 + k, 8, stride=8), :] = power[half]
                power = first if k == 0 else times(power, first)
            for half in range(2):
                eight_ref[half, group, line : line + 8, :] = power[half]
        numbers = pos_ref[away, 2 * chunks : 2 * chunks + runs, :].astype(jnp.int32)
        for run in range(runs):
            number = numbers[run, 0]
            low = jnp.where(upper, 0, number // LANES)
            high = jnp.where(upper, (number + LANES - 1) // LANES, own)
            high = jnp.where(active, high, low)

            for step in range(own):
                list_ref[length + step] = group * LANES + run * own + low + step
            length = length + high - low
        return length

    length = lax.fori_loop(0, groups, waves, 0, unroll=2)

    def basis(entry, axis):
        group, chunk = entry
        line = axis * chunks + chunk
        start = pl.multiple_of(line * 8, 8)
        now = tuple(wave_ref[half, group, pl.ds(start, 8), :] for half in range(2))
        step = tuple(jnp.broadcast_to(eight_ref[half, group, pl.ds(line, 1), :], (8, LANES)) for half in range(2))
        twice = 2.0 * step[0]
        last, now = now, times(now, step)
        cosines, sines = [last[0], now[0]], [last[1], now[1]]
        for _ in range(2, HALF // 8):
            last, now = now, tuple(twice * now[half] - last[half] for half in range(2))
            cosines.append(now[0])
            sines.append(now[1])
        return jnp.concatenate(cosines + sines, axis=0)

    zeros = jnp.zeros((table_ref.shape[1] - 6 * HALF, 2 * LANES), BF16)

    def evaluate(first, size):
        for inner in range(size):
            places = [jnp.minimum(first + inner * 2 + side, length - 1) for side in range(2)]
            entries = [(list_ref[place] >> 7, list_ref[place] & (LANES - 1)) for place in places]
            wave_y = jnp.concatenate([basis(entry, 1) for entry in entries], axis=1)
            high_y = wave_y.astype(BF16)
            low_y = (wave_y - high_y.astype(F32)).astype(BF16)
            weights = jnp.concatenate([high_y, low_y, high_y, zeros], axis=0)
            inside = jnp.dot(table_ref[...], weights, preferred_element_type=F32)
            wave_x = jnp.concatenate([basis(entry, 0) for entry in entries], axis=1)
            for half in range(2):
                value = jnp.sum(inside[half * 2 * HALF : (half + 1) * 2 * HALF, :] * wave_x, axis=0, keepdims=True)
                for side, (group, chunk) in enumerate(entries):
                    out_ref[group, pl.ds(half * chunks + chunk, 1), :] = value[:, side * LANES : (side + 1) * LANES]

    def many(index, carry):
        evaluate(index * 2 * unroll, unroll)
        return carry

    def few(index, carry):
        evaluate(length // (2 * unroll) * 2 * unroll + index * 2 * rest, rest)
        return carry

    rest = 4
    lax.fori_loop(0, length // (2 * unroll), many, 0)
    lax.fori_loop(0, (length % (2 * unroll) + 2 * rest - 1) // (2 * rest), few, 0)


def gradient_kernel(target_ref, feature_ref, net_hbm, out_ref, net_ref, sem, *, scale):
    copy = pltpu.make_async_copy(net_hbm, net_ref, sem)
    copy.start()
    chunks = feature_ref.shape[0] // LANES
    slots = out_ref.shape[0] // 2
    upper = lax.axis_index("band") < lax.axis_size("band") // 2
    targets = [
        jnp.concatenate(
            [target_ref[pl.ds(half * chunks + chunk, slots, stride=2 * chunks), :] for chunk in range(chunks)], axis=1
        )
        for half in range(2)
    ]
    copy.wait()
    mine = net_ref[2 * slots : 2 * slots + 1, :] == jnp.where(upper, 1.0, 0.0)
    parts = []
    for half in range(2):
        scaled = (net_ref[half * slots : (half + 1) * slots, :] - targets[half]) * scale
        parts.append(jnp.where(mine, scaled, 0.0))
    spread = jnp.concatenate(parts, axis=0)
    pieces = jnp.concatenate([piece.astype(F32) for piece in split3(spread)], axis=0).astype(BF16)
    total = jnp.dot(pieces, feature_ref[...], preferred_element_type=F32)
    height = out_ref.shape[0]
    out_ref[...] = total[:height] + total[height : 2 * height] + total[2 * height :]


def call(kernel, out, scratch=(), mebibytes=16, **more):
    return pl.pallas_call(
        kernel,
        out_shape=out,
        **more,
        scratch_shapes=list(scratch),
        interpret=INTERPRET,
        compiler_params=pltpu.CompilerParams(vmem_limit_bytes=mebibytes * 1024 * 1024),
    )


def local(positions, coefficients, lattice, spin_labels, occupied, features, orbital_head):
    walk_count = lax.axis_size("walk")
    band_count = lax.axis_size("band")
    band_index = lax.axis_index("band")
    devices = walk_count * band_count
    rows = coefficients.shape[1]
    count = positions.shape[1]
    orbitals = occupied.shape[0] * occupied.shape[1]
    each = orbitals // band_count

    chunks = count // LANES
    anywhere = pl.BlockSpec(memory_space=pltpu.HBM)
    picked = call(
        pick_kernel,
        jax.ShapeDtypeStruct((devices * BLOCK, LANES), BF16),
        [
            pltpu.VMEM(coefficients.shape, BF16),
            pltpu.SMEM(occupied.shape, jnp.int32),
            pltpu.VMEM((devices * BLOCK, LANES), F32),
            pltpu.SemaphoreType.DMA((3,)),
        ],
        in_specs=[anywhere, anywhere],
    )(pltpu.with_memory_space_constraint(coefficients, pltpu.HBM), pltpu.with_memory_space_constraint(occupied, pltpu.HBM))
    picked, positions = lax.optimization_barrier((picked, positions))
    received = lax.all_to_all(picked.reshape(devices, BLOCK, LANES), ("walk", "band"), 0, 0, tiled=True)
    ordered, slot, up = call(
        order_kernel,
        (
            jax.ShapeDtypeStruct((2 * chunks + 8, LANES), F32),
            jax.ShapeDtypeStruct((count // RUN, RUN), F32),
            jax.ShapeDtypeStruct((1, count), F32),
        ),
    )(positions, spin_labels.reshape(chunks, LANES))
    everyone = ordered[None]
    for flips in ((1,), tuple(range(walk_count - 2, 0, -2))):
        moved = [lax.ppermute(everyone, "walk", [(k, k ^ flip) for k in range(walk_count)]) for flip in flips]
        everyone = jnp.concatenate([everyone, *moved], axis=0)
    table = call(
        fold_kernel, jax.ShapeDtypeStruct((4 * HALF, 512), BF16), [pltpu.VMEM((4 * HALF, 2 * HALF), F32)]
    )(received, lattice.reshape(2, walk_count, rows))
    values = call(
        functools.partial(orbital_kernel, unroll=12, each=each),
        jax.ShapeDtypeStruct((walk_count, 2 * chunks, LANES), F32),
        [
            pltpu.VMEM((2, walk_count, 16 * chunks, LANES), F32),
            pltpu.VMEM((2, walk_count, 2 * chunks, LANES), F32),
            pltpu.SMEM((walk_count * chunks + RUN // LANES,), jnp.int32),
        ],
        mebibytes=24,
    )(table, everyone)
    target = lax.all_to_all(values, "walk", 0, 0, tiled=True).reshape(-1, LANES)

    spins = occupied.shape[0]
    per_spin = band_count // spins
    spin = band_index // per_spin
    columns = orbital_head.reshape(orbital_head.shape[0], spins, 2, per_spin, each)
    columns = lax.dynamic_index_in_dim(columns, spin, 1, keepdims=False)
    columns = lax.dynamic_index_in_dim(columns, band_index % per_spin, 2, keepdims=False)
    columns = jnp.transpose(columns, (1, 2, 0))
    columns = jnp.pad(columns, ((0, 0), (0, walk_count - each), (0, 0))).reshape(2 * walk_count, -1)
    sorted_features, net = call(
        sort_kernel,
        (jax.ShapeDtypeStruct(features.shape, BF16), jax.ShapeDtypeStruct((2 * walk_count + 8, count), F32)),
    )(slot, features, columns, up)
    net = pltpu.with_memory_space_constraint(net, pltpu.HBM)
    walkers = walk_count * count // orbitals
    hidden = features.shape[1]
    in_vmem = pl.BlockSpec(memory_space=pltpu.VMEM)
    own = call(
        functools.partial(gradient_kernel, scale=1.0 / walkers),
        jax.ShapeDtypeStruct((2 * walk_count, hidden), F32),
        [pltpu.VMEM(net.shape, F32), pltpu.SemaphoreType.DMA],
        in_specs=[in_vmem, in_vmem, anywhere],
    )(target, sorted_features, net)
    own = own.reshape(2, walk_count, hidden)[:, :each].reshape(-1, LANES)
    own = own + lax.ppermute(own, "walk", [(k, k ^ 1) for k in range(walk_count)])
    chips = walk_count // 2
    shares = lax.all_to_all(
        jnp.broadcast_to(own, (chips, *own.shape)),
        "walk",
        0,
        0,
        axis_index_groups=[[2 * chip + core for chip in range(chips)] for core in range(2)],
        tiled=True,
    )
    summed = jnp.sum(shares, axis=0)
    whole = lax.all_to_all(jnp.broadcast_to(summed, (band_count, *own.shape)), "band", 0, 0, tiled=True)
    whole = whole.reshape(spins, per_spin, 2, each, hidden)
    return jnp.transpose(whole, (4, 0, 2, 1, 3)).reshape(hidden, 2 * orbitals)


def solution(mesh):
    return jax.shard_map(
        local,
        mesh=mesh,
        in_specs=(
            P(None, "walk"),
            P(None, "walk", "band"),
            P(),
            P("walk"),
            P(),
            P("walk", None),
            P(),
        ),
        out_specs=P(),
        check_vma=False,
    )
```
